256 devices in a mesh: img: 8 (over z_lo, y), space: 32 (over x, z_hi, core).
Axes of the slice: x: 4, y: 4, z: 8 (z_hi: 4, z_lo: 2; z = z_hi * 2 + z_lo), core: 2. Of those that a mesh axis runs over, the one named last changes fastest.
Arguments:
- images: float32 [8, 768, 96, 128], P('img', 'space'), may hold values from -6 to 6
- pairings: int32 [3, 8], replicated, may hold values from 0 to 7, as said below
Outputs:
- advected: float32 [8, 768, 96, 128], P('img', 'space')
- velocity: float32 [8, 3, 768, 96, 128], P('img', None, 'space')
The draws below stay inside these ranges and needn't reach their ends.
Inputs may be any that keep to these rules, and one draw needn't show every extreme that they name: Each row of pairings is a permutation of the 8 images; an image may be its own partner.
All inputs are finite; a program needn't handle non-finite values.
Results may differ from the reference program's by a relative error of at most 0.00018.
Values sent between devices are 32-bit elements; how exact they have to be, the bound alone decides.
A program may use at most 64 MiB of HBM per device.

```python
import math
import jax
import jax.numpy as jnp
from jax import lax

Y = 96
Z = 128
RADIUS = 4
PAIRINGS = 3
IMAGES = 8
NX = 768


def draw_pairings(key, part):
    row_list = []
    for row_number in range(PAIRINGS):
        shuffled = jax.random.permutation(jax.random.fold_in(key, 17 + row_number), IMAGES).astype(jnp.int32)
        row_list.append(shuffled)
    return jnp.stack(row_list).astype(jnp.int32)


def levels(rng, dims, pieces, smallest, largest):
    loudness, own = 1.0, jax.random.fold_in(rng, 6)
    for axis_at, shards_of in pieces:
        heights = jnp.exp(jax.random.uniform(jax.random.fold_in(own, axis_at), (shards_of,), jnp.float32, smallest / len(pieces), largest / len(pieces)))
        loudness = loudness * jnp.repeat(heights, dims[axis_at] // shards_of).reshape([-1 if axis == axis_at else 1 for axis in range(len(dims))])
    return loudness


def bell_draw(rng, extent, scale, most, pieces=(), kind=jnp.bfloat16):
    values = jax.random.normal(rng, extent, jnp.float32) * scale
    if len(pieces) > 0:
        values = levels(rng, extent, pieces, -0.22, 0.18) * values
    return jnp.clip(values, min=-most, max=most).astype(kind)


def setup_inputs(seed: int = 0) -> dict:
    keys = jax.random.split(jax.random.key(seed), 3)
    return {
        "images": bell_draw(keys[0], (IMAGES, NX, Y, Z), 1.0, 6.0, ((0, 8), (1, 32)), jnp.float32),
        "pairings": draw_pairings(jax.random.fold_in(keys[2], 71), 0),
    }


gauss_sigma = 1.5
step_scale = 8.0
floor_product = 0.25
floor_variance = 0.5


def gauss_taps(radius):
    raw_taps = [math.exp(-(offset * offset) / (2.0 * gauss_sigma * gauss_sigma)) for offset in range(-radius, radius + 1)]
    total_weight = sum(raw_taps)
    return [raw_weight / total_weight for raw_weight in raw_taps]


def padded_along(volume, dimension, margin):
    widths = [(0, 0)] * volume.ndim
    widths[dimension] = (margin, margin)
    return jnp.pad(volume, widths)


def window(padded, dimension, offset, length):
    return lax.slice_in_dim(padded, offset, offset + length, axis=dimension)


def sum_three(volume, dimension):
    length = volume.shape[dimension]
    padded = padded_along(volume, dimension, 1)
    return window(padded, dimension, 0, length) + window(padded, dimension, 1, length) + window(padded, dimension, 2, length)


def box_mean(volume):
    return sum_three(sum_three(volume, 0), 1) / 9.0


def central(volume, dimension):
    length = volume.shape[dimension]
    padded = padded_along(volume, dimension, 1)
    return (window(padded, dimension, 2, length) - window(padded, dimension, 0, length)) * 0.5


def smooth_along(volume, dimension, weights):
    length = volume.shape[dimension]
    padded = padded_along(volume, dimension, len(weights) // 2)
    result = weights[0] * window(padded, dimension, 0, length)
    for tap_index in range(1, len(weights)):
        result = result + weights[tap_index] * window(padded, dimension, tap_index, length)
    return result


def advect(volume, velocity):
    change = None
    for dimension in range(3):
        length = volume.shape[dimension]
        padded = padded_along(volume, dimension, 1)
        backward = volume - window(padded, dimension, 0, length)
        forward = window(padded, dimension, 2, length) - volume
        speed_part = velocity[dimension]
        part_change = jnp.maximum(speed_part, 0.0) * backward + jnp.minimum(speed_part, 0.0) * forward
        change = part_change if change is None else change + part_change
    return volume - change


def correlation_drive(own_brick, partner):
    mean_own = box_mean(own_brick)
    mean_partner = box_mean(partner)
    cross_term = box_mean(own_brick * partner) - mean_own * mean_partner
    spread_own = box_mean(own_brick * own_brick) - mean_own * mean_own
    spread_partner = box_mean(partner * partner) - mean_partner * mean_partner
    factor = 2.0 * cross_term / jnp.maximum(spread_own * spread_partner, floor_product)
    ratio_term = cross_term / jnp.maximum(spread_own, floor_variance)
    return factor * ((partner - mean_partner) - ratio_term * (own_brick - mean_own))


def reference(images, pairings):
    weights = gauss_taps(RADIUS)

    def one_image(image_index):
        own_brick = lax.dynamic_index_in_dim(images, image_index, 0, keepdims=False)
        drive_sum = None
        for pairing_row in range(PAIRINGS):
            partner_index = lax.dynamic_index_in_dim(pairings[pairing_row], image_index, 0, keepdims=False)
            partner = lax.dynamic_index_in_dim(images, partner_index, 0, keepdims=False)
            pair_term = correlation_drive(own_brick, partner)
            drive_sum = pair_term if drive_sum is None else drive_sum + pair_term
        gradient = jnp.stack([central(own_brick, 0), central(own_brick, 1), central(own_brick, 2)])
        force = drive_sum[None] * gradient
        smoothed = smooth_along(force, 1, weights)
        smoothed = smooth_along(smoothed, 2, weights)
        smoothed = smooth_along(smoothed, 3, weights)
        velocity = step_scale * smoothed
        return advect(own_brick, velocity), velocity

    advected, velocity = lax.map(one_image, jnp.arange(IMAGES, dtype=jnp.int32))
    return advected, velocity
```

```python
import math

import jax
import jax.numpy as jnp
from jax import lax
from jax.sharding import PartitionSpec as P

RADIUS = 4
PAIRINGS = 3

gauss_sigma = 1.5
step_scale = 8.0
floor_product = 0.25
floor_variance = 0.5

Y_MARGIN = 2


def gauss_taps(radius):
    raw_taps = [
        math.exp(-(offset * offset) / (2.0 * gauss_sigma * gauss_sigma))
        for offset in range(-radius, radius + 1)
    ]
    total_weight = sum(raw_taps)
    return [raw_weight / total_weight for raw_weight in raw_taps]


def halo_rows(value, width):
    peers = lax.axis_size("space")
    up = [(i, i + 1) for i in range(peers - 1)]
    down = [(i + 1, i) for i in range(peers - 1)]
    before = lax.ppermute(value[-width:], "space", up)
    after = lax.ppermute(value[:width], "space", down)
    return jnp.concatenate([before, value, after], axis=0)


def padded_along(volume, dimension, margin):
    widths = [(0, 0)] * volume.ndim
    widths[dimension] = (margin, margin)
    return jnp.pad(volume, widths)


def window(padded, dimension, offset, length):
    return lax.slice_in_dim(padded, offset, offset + length, axis=dimension)


def central(volume, dimension):
    length = volume.shape[dimension]
    padded = padded_along(volume, dimension, 1)
    return (window(padded, dimension, 2, length) - window(padded, dimension, 0, length)) * 0.5


def smooth_along(volume, dimension, weights):
    length = volume.shape[dimension]
    padded = padded_along(volume, dimension, len(weights) // 2)
    result = weights[0] * window(padded, dimension, 0, length)
    for tap_index in range(1, len(weights)):
        result = result + weights[tap_index] * window(padded, dimension, tap_index, length)
    return result


def smooth_rows(extended, weights):
    length = extended.shape[1] - len(weights) + 1
    result = weights[0] * window(extended, 1, 0, length)
    for tap_index in range(1, len(weights)):
        result = result + weights[tap_index] * window(extended, 1, tap_index, length)
    return result


def box_valid(volume):
    sx = volume[..., :-2, :, :] + volume[..., 1:-1, :, :] + volume[..., 2:, :, :]
    sy = sx[..., :-2, :] + sx[..., 1:-1, :] + sx[..., 2:, :]
    return sy / 9.0


def slice_drive(stack, pairings, rows):
    keep = slice(Y_MARGIN - 1, Y_MARGIN - 1 + rows)
    center = stack[:, 1:-1, Y_MARGIN:Y_MARGIN + rows]
    mean = box_valid(stack)[:, :, keep]
    spread = box_valid(stack * stack)[:, :, keep] - mean * mean
    guarded_spread = jnp.maximum(spread, floor_variance)
    centered = center - mean
    drive_sum = None
    for pairing_row in range(PAIRINGS):
        index = pairings[pairing_row]
        partner = jnp.take(stack, index, axis=0)
        mean_partner = jnp.take(mean, index, axis=0)
        spread_partner = jnp.take(spread, index, axis=0)
        partner_center = jnp.take(center, index, axis=0)
        cross_term = box_valid(stack * partner)[:, :, keep] - mean * mean_partner
        factor = 2.0 * cross_term / jnp.maximum(spread * spread_partner, floor_product)
        ratio_term = cross_term / guarded_spread
        pair_term = factor * (partner_center - mean_partner - ratio_term * centered)
        drive_sum = pair_term if drive_sum is None else drive_sum + pair_term
    return drive_sum


def advect_rows(near_own, velocity):
    center = near_own[1:-1]
    backward = center - near_own[:-2]
    forward = near_own[2:] - center
    change = jnp.maximum(velocity[0], 0.0) * backward + jnp.minimum(velocity[0], 0.0) * forward
    for dimension in range(1, 3):
        length = center.shape[dimension]
        padded = padded_along(center, dimension, 1)
        backward = center - window(padded, dimension, 0, length)
        forward = window(padded, dimension, 2, length) - center
        speed_part = velocity[dimension]
        change = change + (
            jnp.maximum(speed_part, 0.0) * backward + jnp.minimum(speed_part, 0.0) * forward
        )
    return center - change


def shards(images, pairings):
    weights = gauss_taps(RADIUS)
    groups = lax.axis_size("img")
    own = images[0]
    x_rows, y_rows, _ = own.shape
    rows = y_rows // groups
    own_ext = halo_rows(own, RADIUS + 1)
    near = own_ext[RADIUS:-RADIUS]
    padded = jnp.pad(near, ((0, 0), (Y_MARGIN, Y_MARGIN), (0, 0)))
    width = rows + 2 * Y_MARGIN
    pieces = jnp.stack([padded[:, j * rows:j * rows + width] for j in range(groups)])
    stack = lax.all_to_all(pieces, "img", split_axis=0, concat_axis=0, tiled=True)
    drive_part = slice_drive(stack, pairings, rows)
    drive_sum = lax.all_to_all(drive_part, "img", split_axis=0, concat_axis=2, tiled=True)[0]
    drive_ext = halo_rows(drive_sum, RADIUS)
    center = own_ext[1:-1]
    gradient = jnp.stack(
        [(own_ext[2:] - own_ext[:-2]) * 0.5, central(center, 1), central(center, 2)]
    )
    force = drive_ext[None] * gradient
    smoothed = smooth_rows(force, weights)
    smoothed = smooth_along(smoothed, 2, weights)
    smoothed = smooth_along(smoothed, 3, weights)
    velocity = step_scale * smoothed
    advected = advect_rows(near, velocity)
    return (advected[None], velocity[None])


def solution(mesh):
    return jax.shard_map(
        shards,
        mesh=mesh,
        in_specs=(P("img", "space", None, None), P()),
        out_specs=(P("img", "space", None, None), P("img", None, "space", None, None)),
        check_vma=False,
    )
```

```python
import math

import jax
import jax.numpy as jnp
from jax import lax
from jax.experimental import pallas as pl
from jax.experimental.pallas import tpu as pltpu
from jax.sharding import PartitionSpec as P

RADIUS = 4
PAIRINGS = 3

gauss_sigma = 1.5
step_scale = 8.0
floor_product = 0.25
floor_variance = 0.5


def gauss_taps(radius):
    raw_taps = [
        math.exp(-(offset * offset) / (2.0 * gauss_sigma * gauss_sigma))
        for offset in range(-radius, radius + 1)
    ]
    total_weight = sum(raw_taps)
    return [raw_weight / total_weight for raw_weight in raw_taps]


def halo_rows(value, width):
    peers = lax.axis_size("space")
    up = [(i, i + 1) for i in range(peers - 1)]
    down = [(i + 1, i) for i in range(peers - 1)]
    before = lax.ppermute(value[-width:], "space", up)
    after = lax.ppermute(value[:width], "space", down)
    return jnp.concatenate([before, value, after], axis=0)


def padded_along(volume, dimension, margin):
    widths = [(0, 0)] * volume.ndim
    widths[dimension] = (margin, margin)
    return jnp.pad(volume, widths)


def window(padded, dimension, offset, length):
    return lax.slice_in_dim(padded, offset, offset + length, axis=dimension)


def central(volume, dimension):
    length = volume.shape[dimension]
    padded = padded_along(volume, dimension, 1)
    return (window(padded, dimension, 2, length) - window(padded, dimension, 0, length)) * 0.5


def smooth_along(volume, dimension, weights):
    length = volume.shape[dimension]
    padded = padded_along(volume, dimension, len(weights) // 2)
    result = weights[0] * window(padded, dimension, 0, length)
    for tap_index in range(1, len(weights)):
        result = result + weights[tap_index] * window(padded, dimension, tap_index, length)
    return result


def smooth_rows(extended, weights):
    length = extended.shape[1] - len(weights) + 1
    result = weights[0] * window(extended, 1, 0, length)
    for tap_index in range(1, len(weights)):
        result = result + weights[tap_index] * window(extended, 1, tap_index, length)
    return result


def box_rows(volume):
    sx = volume[:-2] + volume[1:-1] + volume[2:]
    last = sx.shape[1] - 1
    row = lax.broadcasted_iota(jnp.int32, sx.shape, 1)
    before = jnp.where(row >= 1, pltpu.roll(sx, 1, 1), 0.0)
    after = jnp.where(row < last, pltpu.roll(sx, last, 1), 0.0)
    return (before + sx + after) / 9.0


def drive_kernel(pair_ref, stack_ref, out_ref, mean_ref, spread_ref):
    groups = stack_ref.shape[0]

    def stats(g, carry):
        value = stack_ref[g]
        mean = box_rows(value)
        mean_ref[g] = mean
        spread_ref[g] = box_rows(value * value) - mean * mean
        return carry

    lax.fori_loop(0, groups, stats, 0)

    def pairs(g, carry):
        own = stack_ref[g]
        mean_own = mean_ref[g]
        spread_own = spread_ref[g]
        center_own = own[1:-1] - mean_own
        guarded_spread = jnp.maximum(spread_own, floor_variance)
        drive_sum = None
        for pairing_row in range(PAIRINGS):
            h = pair_ref[pairing_row, g]
            partner = stack_ref[h]
            mean_partner = mean_ref[h]
            spread_partner = spread_ref[h]
            cross_term = box_rows(own * partner) - mean_own * mean_partner
            factor = 2.0 * cross_term / jnp.maximum(spread_own * spread_partner, floor_product)
            ratio_term = cross_term / guarded_spread
            pair_term = factor * (partner[1:-1] - mean_partner - ratio_term * center_own)
            drive_sum = pair_term if drive_sum is None else drive_sum + pair_term
        out_ref[g] = drive_sum
        return carry

    lax.fori_loop(0, groups, pairs, 0)


def slice_drive(stack, pairings):
    groups, rows, y_rows, z_rows = stack.shape
    shape = (groups, rows - 2, y_rows, z_rows)
    return pl.pallas_call(
        drive_kernel,
        out_shape=jax.ShapeDtypeStruct(shape, jnp.float32),
        in_specs=[
            pl.BlockSpec(memory_space=pltpu.SMEM),
            pl.BlockSpec(memory_space=pltpu.VMEM),
        ],
        out_specs=pl.BlockSpec(memory_space=pltpu.VMEM),
        scratch_shapes=[pltpu.VMEM(shape, jnp.float32), pltpu.VMEM(shape, jnp.float32)],
    )(pairings, stack)


def advect_rows(near_own, velocity):
    center = near_own[1:-1]
    backward = center - near_own[:-2]
    forward = near_own[2:] - center
    change = jnp.maximum(velocity[0], 0.0) * backward + jnp.minimum(velocity[0], 0.0) * forward
    for dimension in range(1, 3):
        length = center.shape[dimension]
        padded = padded_along(center, dimension, 1)
        backward = center - window(padded, dimension, 0, length)
        forward = window(padded, dimension, 2, length) - center
        speed_part = velocity[dimension]
        change = change + (
            jnp.maximum(speed_part, 0.0) * backward + jnp.minimum(speed_part, 0.0) * forward
        )
    return center - change


def shards(images, pairings):
    weights = gauss_taps(RADIUS)
    groups = lax.axis_size("img")
    own = images[0]
    x_rows, y_rows, _ = own.shape
    rows = x_rows // groups
    own_ext = halo_rows(own, RADIUS + 1)
    near = own_ext[RADIUS:-RADIUS]
    pieces = jnp.stack([near[j * rows:j * rows + rows + 2] for j in range(groups)])
    stack = lax.all_to_all(pieces, "img", split_axis=0, concat_axis=0, tiled=True)
    drive_part = slice_drive(stack, pairings)
    returned = lax.all_to_all(drive_part, "img", split_axis=0, concat_axis=0, tiled=True)
    drive_sum = returned.reshape(own.shape)
    drive_ext = halo_rows(drive_sum, RADIUS)
    center = own_ext[1:-1]
    gradient = jnp.stack(
        [(own_ext[2:] - own_ext[:-2]) * 0.5, central(center, 1), central(center, 2)]
    )
    force = drive_ext[None] * gradient
    smoothed = smooth_rows(force, weights)
    smoothed = smooth_along(smoothed, 2, weights)
    smoothed = smooth_along(smoothed, 3, weights)
    velocity = step_scale * smoothed
    advected = advect_rows(near, velocity)
    return (advected[None], velocity[None])


def solution(mesh):
    return jax.shard_map(
        shards,
        mesh=mesh,
        in_specs=(P("img", "space", None, None), P()),
        out_specs=(P("img", "space", None, None), P("img", None, "space", None, None)),
        check_vma=False,
    )
```

```python
import math

import jax
import numpy as np
import jax.numpy as jnp
from jax import lax
from jax.experimental import pallas as pl
from jax.experimental.pallas import tpu as pltpu
from jax.sharding import PartitionSpec as P

RADIUS = 4
PAIRINGS = 3

gauss_sigma = 1.5
step_scale = 8.0
floor_product = 0.25
floor_variance = 0.5


def gauss_taps(radius):
    raw_taps = [
        math.exp(-(offset * offset) / (2.0 * gauss_sigma * gauss_sigma))
        for offset in range(-radius, radius + 1)
    ]
    total_weight = sum(raw_taps)
    return [raw_weight / total_weight for raw_weight in raw_taps]


def halo_rows(value, width):
    peers = lax.axis_size("space")
    up = [(i, i + 1) for i in range(peers - 1)]
    down = [(i + 1, i) for i in range(peers - 1)]
    before = lax.ppermute(value[-width:], "space", up)
    after = lax.ppermute(value[:width], "space", down)
    return jnp.concatenate([before, value, after], axis=0)


def padded_along(volume, dimension, margin):
    widths = [(0, 0)] * volume.ndim
    widths[dimension] = (margin, margin)
    return jnp.pad(volume, widths)


def window(padded, dimension, offset, length):
    return lax.slice_in_dim(padded, offset, offset + length, axis=dimension)


def central(volume, dimension):
    length = volume.shape[dimension]
    padded = padded_along(volume, dimension, 1)
    return (window(padded, dimension, 2, length) - window(padded, dimension, 0, length)) * 0.5


def smooth_along(volume, dimension, weights):
    length = volume.shape[dimension]
    padded = padded_along(volume, dimension, len(weights) // 2)
    result = weights[0] * window(padded, dimension, 0, length)
    for tap_index in range(1, len(weights)):
        result = result + weights[tap_index] * window(padded, dimension, tap_index, length)
    return result


def smooth_rows(extended, weights):
    length = extended.shape[1] - len(weights) + 1
    result = weights[0] * window(extended, 1, 0, length)
    for tap_index in range(1, len(weights)):
        result = result + weights[tap_index] * window(extended, 1, tap_index, length)
    return result


def box_rows(volume):
    sx = volume[:-2] + volume[1:-1] + volume[2:]
    last = sx.shape[1] - 1
    row = lax.broadcasted_iota(jnp.int32, sx.shape, 1)
    before = jnp.where(row >= 1, pltpu.roll(sx, 1, 1), 0.0)
    after = jnp.where(row < last, pltpu.roll(sx, last, 1), 0.0)
    return (before + sx + after) / 9.0


def drive_kernel(pair_ref, stack_ref, out_ref, mean_ref, spread_ref):
    groups = stack_ref.shape[0]

    def stats(g, carry):
        value = stack_ref[g]
        mean = box_rows(value)
        mean_ref[g] = mean
        spread_ref[g] = box_rows(value * value) - mean * mean
        return carry

    lax.fori_loop(0, groups, stats, 0)

    def pairs(g, carry):
        own = stack_ref[g]
        mean_own = mean_ref[g]
        spread_own = spread_ref[g]
        center_own = own[1:-1] - mean_own
        guarded_spread = jnp.maximum(spread_own, floor_variance)
        drive_sum = None
        for pairing_row in range(PAIRINGS):
            h = pair_ref[pairing_row, g]
            partner = stack_ref[h]
            mean_partner = mean_ref[h]
            spread_partner = spread_ref[h]
            cross_term = box_rows(own * partner) - mean_own * mean_partner
            factor = 2.0 * cross_term / jnp.maximum(spread_own * spread_partner, floor_product)
            ratio_term = cross_term / guarded_spread
            pair_term = factor * (partner[1:-1] - mean_partner - ratio_term * center_own)
            drive_sum = pair_term if drive_sum is None else drive_sum + pair_term
        out_ref[g] = drive_sum
        return carry

    lax.fori_loop(0, groups, pairs, 0)


def slice_drive(stack, pairings):
    groups, rows, y_rows, z_rows = stack.shape
    shape = (groups, rows - 2, y_rows, z_rows)
    return pl.pallas_call(
        drive_kernel,
        out_shape=jax.ShapeDtypeStruct(shape, jnp.float32),
        in_specs=[
            pl.BlockSpec(memory_space=pltpu.SMEM),
            pl.BlockSpec(memory_space=pltpu.VMEM),
        ],
        out_specs=pl.BlockSpec(memory_space=pltpu.VMEM),
        scratch_shapes=[pltpu.VMEM(shape, jnp.float32), pltpu.VMEM(shape, jnp.float32)],
    )(pairings, stack)


def advect_rows(near_own, velocity):
    center = near_own[1:-1]
    backward = center - near_own[:-2]
    forward = near_own[2:] - center
    change = jnp.maximum(velocity[0], 0.0) * backward + jnp.minimum(velocity[0], 0.0) * forward
    for dimension in range(1, 3):
        length = center.shape[dimension]
        padded = padded_along(center, dimension, 1)
        backward = center - window(padded, dimension, 0, length)
        forward = window(padded, dimension, 2, length) - center
        speed_part = velocity[dimension]
        change = change + (
            jnp.maximum(speed_part, 0.0) * backward + jnp.minimum(speed_part, 0.0) * forward
        )
    return center - change


def shifted(value, offset, axis):
    length = value.shape[axis]
    rolled = pltpu.roll(value, (-offset) % length, axis)
    index = lax.broadcasted_iota(jnp.int32, value.shape, axis) + offset
    return jnp.where((index >= 0) & (index < length), rolled, 0.0)


def post_kernel(drive_ref, own_ref, wy_ref, wz_ref, vel_ref, adv_ref, force_ref):
    extended = drive_ref.shape[0]
    x_rows = vel_ref.shape[1]
    taps = gauss_taps(RADIUS)
    highest = lax.Precision.HIGHEST

    def force_row(r, carry):
        value = own_ref[r + 1]
        drive = drive_ref[r]
        force_ref[0, r] = drive * ((own_ref[r + 2] - own_ref[r]) * 0.5)
        force_ref[1, r] = drive * ((shifted(value, 1, 0) - shifted(value, -1, 0)) * 0.5)
        force_ref[2, r] = drive * ((shifted(value, 1, 1) - shifted(value, -1, 1)) * 0.5)
        return carry

    lax.fori_loop(0, extended, force_row, 0)
    wy = wy_ref[...]
    wz = wz_ref[...]

    def out_row(x, carry):
        value = own_ref[x + RADIUS + 1]
        change = None
        for c in range(3):
            acc = taps[0] * force_ref[c, x]
            for t in range(1, len(taps)):
                acc = acc + taps[t] * force_ref[c, x + t]
            acc = jnp.dot(wy, acc, precision=highest, preferred_element_type=jnp.float32)
            acc = jnp.dot(acc, wz, precision=highest, preferred_element_type=jnp.float32)
            speed = step_scale * acc
            vel_ref[c, x] = speed
            if c == 0:
                backward = value - own_ref[x + RADIUS]
                forward = own_ref[x + RADIUS + 2] - value
            else:
                backward = value - shifted(value, -1, c - 1)
                forward = shifted(value, 1, c - 1) - value
            part = jnp.maximum(speed, 0.0) * backward + jnp.minimum(speed, 0.0) * forward
            change = part if change is None else change + part
        adv_ref[x] = value - change
        return carry

    lax.fori_loop(0, x_rows, out_row, 0)


def band(length, taps):
    radius = len(taps) // 2
    matrix = np.zeros((length, length), np.float32)
    for i in range(length):
        for t in range(-radius, radius + 1):
            if 0 <= i + t < length:
                matrix[i, i + t] = taps[t + radius]
    return matrix


def post_stage(drive_ext, own_ext):
    extended, y_rows, z_rows = drive_ext.shape
    x_rows = extended - 2 * RADIUS
    taps = gauss_taps(RADIUS)
    wy = jnp.asarray(band(y_rows, taps))
    wz = jnp.asarray(band(z_rows, taps).T)
    vmem = pl.BlockSpec(memory_space=pltpu.VMEM)
    return pl.pallas_call(
        post_kernel,
        out_shape=(
            jax.ShapeDtypeStruct((3, x_rows, y_rows, z_rows), jnp.float32),
            jax.ShapeDtypeStruct((x_rows, y_rows, z_rows), jnp.float32),
        ),
        in_specs=[vmem] * 4,
        out_specs=(vmem, vmem),
        scratch_shapes=[pltpu.VMEM((3, extended, y_rows, z_rows), jnp.float32)],
    )(drive_ext, own_ext, wy, wz)


def shards(images, pairings):
    weights = gauss_taps(RADIUS)
    groups = lax.axis_size("img")
    own = images[0]
    x_rows, y_rows, _ = own.shape
    rows = x_rows // groups
    own_ext = halo_rows(own, RADIUS + 1)
    near = own_ext[RADIUS:-RADIUS]
    pieces = jnp.stack([near[j * rows:j * rows + rows + 2] for j in range(groups)])
    stack = lax.all_to_all(pieces, "img", split_axis=0, concat_axis=0, tiled=True)
    drive_part = slice_drive(stack, pairings)
    returned = lax.all_to_all(drive_part, "img", split_axis=0, concat_axis=0, tiled=True)
    drive_sum = returned.reshape(own.shape)
    drive_ext = halo_rows(drive_sum, RADIUS)
    velocity, advected = post_stage(drive_ext, own_ext)
    return (advected[None], velocity[None])


def solution(mesh):
    return jax.shard_map(
        shards,
        mesh=mesh,
        in_specs=(P("img", "space", None, None), P()),
        out_specs=(P("img", "space", None, None), P("img", None, "space", None, None)),
        check_vma=False,
    )
```

```python
import math

import jax
import numpy as np
import jax.numpy as jnp
from jax import lax
from jax.experimental import pallas as pl
from jax.experimental.pallas import tpu as pltpu
from jax.sharding import PartitionSpec as P

RADIUS = 4
PAIRINGS = 3

gauss_sigma = 1.5
step_scale = 8.0
floor_product = 0.25
floor_variance = 0.5


def gauss_taps(radius):
    raw_taps = [
        math.exp(-(offset * offset) / (2.0 * gauss_sigma * gauss_sigma))
        for offset in range(-radius, radius + 1)
    ]
    total_weight = sum(raw_taps)
    return [raw_weight / total_weight for raw_weight in raw_taps]


def halo_rows(value, width):
    peers = lax.axis_size("space")
    up = [(i, i + 1) for i in range(peers - 1)]
    down = [(i + 1, i) for i in range(peers - 1)]
    before = lax.ppermute(value[-width:], "space", up)
    after = lax.ppermute(value[:width], "space", down)
    return jnp.concatenate([before, value, after], axis=0)


def padded_along(volume, dimension, margin):
    widths = [(0, 0)] * volume.ndim
    widths[dimension] = (margin, margin)
    return jnp.pad(volume, widths)


def window(padded, dimension, offset, length):
    return lax.slice_in_dim(padded, offset, offset + length, axis=dimension)


def central(volume, dimension):
    length = volume.shape[dimension]
    padded = padded_along(volume, dimension, 1)
    return (window(padded, dimension, 2, length) - window(padded, dimension, 0, length)) * 0.5


def smooth_along(volume, dimension, weights):
    length = volume.shape[dimension]
    padded = padded_along(volume, dimension, len(weights) // 2)
    result = weights[0] * window(padded, dimension, 0, length)
    for tap_index in range(1, len(weights)):
        result = result + weights[tap_index] * window(padded, dimension, tap_index, length)
    return result


def smooth_rows(extended, weights):
    length = extended.shape[1] - len(weights) + 1
    result = weights[0] * window(extended, 1, 0, length)
    for tap_index in range(1, len(weights)):
        result = result + weights[tap_index] * window(extended, 1, tap_index, length)
    return result


def box_rows(volume):
    sx = volume[:-2] + volume[1:-1] + volume[2:]
    last = sx.shape[1] - 1
    row = lax.broadcasted_iota(jnp.int32, sx.shape, 1)
    before = jnp.where(row >= 1, pltpu.roll(sx, 1, 1), 0.0)
    after = jnp.where(row < last, pltpu.roll(sx, last, 1), 0.0)
    return (before + sx + after) / 9.0


def drive_kernel(pair_ref, stack_ref, out_ref, mean_ref, spread_ref):
    groups = stack_ref.shape[0]

    def stats(g, carry):
        value = stack_ref[g]
        mean = box_rows(value)
        mean_ref[g] = mean
        spread_ref[g] = box_rows(value * value) - mean * mean
        return carry

    lax.fori_loop(0, groups, stats, 0)

    def pairs(g, carry):
        own = stack_ref[g]
        mean_own = mean_ref[g]
        spread_own = spread_ref[g]
        center_own = own[1:-1] - mean_own
        guarded_spread = jnp.maximum(spread_own, floor_variance)
        drive_sum = None
        for pairing_row in range(PAIRINGS):
            h = pair_ref[pairing_row, g]
            partner = stack_ref[h]
            mean_partner = mean_ref[h]
            spread_partner = spread_ref[h]
            cross_term = box_rows(own * partner) - mean_own * mean_partner
            factor = 2.0 * cross_term / jnp.maximum(spread_own * spread_partner, floor_product)
            ratio_term = cross_term / guarded_spread
            pair_term = factor * (partner[1:-1] - mean_partner - ratio_term * center_own)
            drive_sum = pair_term if drive_sum is None else drive_sum + pair_term
        out_ref[g] = drive_sum
        return carry

    lax.fori_loop(0, groups, pairs, 0)


def slice_drive(stack, pairings):
    groups, rows, y_rows, z_rows = stack.shape
    shape = (groups, rows - 2, y_rows, z_rows)
    return pl.pallas_call(
        drive_kernel,
        out_shape=jax.ShapeDtypeStruct(shape, jnp.float32),
        in_specs=[
            pl.BlockSpec(memory_space=pltpu.SMEM),
            pl.BlockSpec(memory_space=pltpu.VMEM),
        ],
        out_specs=pl.BlockSpec(memory_space=pltpu.VMEM),
        scratch_shapes=[pltpu.VMEM(shape, jnp.float32), pltpu.VMEM(shape, jnp.float32)],
    )(pairings, stack)


def advect_rows(near_own, velocity):
    center = near_own[1:-1]
    backward = center - near_own[:-2]
    forward = near_own[2:] - center
    change = jnp.maximum(velocity[0], 0.0) * backward + jnp.minimum(velocity[0], 0.0) * forward
    for dimension in range(1, 3):
        length = center.shape[dimension]
        padded = padded_along(center, dimension, 1)
        backward = center - window(padded, dimension, 0, length)
        forward = window(padded, dimension, 2, length) - center
        speed_part = velocity[dimension]
        change = change + (
            jnp.maximum(speed_part, 0.0) * backward + jnp.minimum(speed_part, 0.0) * forward
        )
    return center - change


def shifted(value, offset, axis):
    length = value.shape[axis]
    rolled = pltpu.roll(value, (-offset) % length, axis)
    index = lax.broadcasted_iota(jnp.int32, value.shape, axis) + offset
    return jnp.where((index >= 0) & (index < length), rolled, 0.0)


def post_kernel(drive_ref, own_ref, wz_ref, vel_ref, adv_ref, force_ref, pass_ref):
    extended, y_rows, _ = drive_ref.shape
    x_rows = vel_ref.shape[1]
    taps = gauss_taps(RADIUS)

    def plane(c, r, count):
        return pl.ds(pl.multiple_of((c * count + r) * y_rows, 8), y_rows)

    def force_row(r, carry):
        value = own_ref[r + 1]
        drive = drive_ref[r]
        force_ref[plane(0, r, extended)] = drive * ((own_ref[r + 2] - own_ref[r]) * 0.5)
        force_ref[plane(1, r, extended)] = drive * (
            (shifted(value, 1, 0) - shifted(value, -1, 0)) * 0.5
        )
        force_ref[plane(2, r, extended)] = drive * (
            (shifted(value, 1, 1) - shifted(value, -1, 1)) * 0.5
        )
        return carry

    lax.fori_loop(0, extended, force_row, 0)

    def x_pass(x, carry):
        for c in range(3):
            acc = taps[0] * force_ref[plane(c, x, extended)]
            for t in range(1, len(taps)):
                acc = acc + taps[t] * force_ref[plane(c, x + t, extended)]
            pass_ref[plane(c, x, x_rows)] = acc
        return carry

    lax.fori_loop(0, x_rows, x_pass, 0)
    wz = wz_ref[...]
    chunk = 8 * y_rows
    chunks = pass_ref.shape[0] // chunk

    def z_pass(i, carry):
        rows = pl.ds(pl.multiple_of(i * chunk, 8), chunk)
        pass_ref[rows] = jnp.dot(
            pass_ref[rows], wz, precision=lax.Precision.HIGHEST,
            preferred_element_type=jnp.float32,
        )
        return carry

    lax.fori_loop(0, chunks, z_pass, 0)

    def out_row(x, carry):
        value = own_ref[x + RADIUS + 1]
        change = None
        for c in range(3):
            smoothed_z = pass_ref[plane(c, x, x_rows)]
            acc = taps[0] * shifted(smoothed_z, -RADIUS, 0)
            for t in range(1, len(taps)):
                acc = acc + taps[t] * shifted(smoothed_z, t - RADIUS, 0)
            speed = step_scale * acc
            vel_ref[c, x] = speed
            if c == 0:
                backward = value - own_ref[x + RADIUS]
                forward = own_ref[x + RADIUS + 2] - value
            else:
                backward = value - shifted(value, -1, c - 1)
                forward = shifted(value, 1, c - 1) - value
            part = jnp.maximum(speed, 0.0) * backward + jnp.minimum(speed, 0.0) * forward
            change = part if change is None else change + part
        adv_ref[x] = value - change
        return carry

    lax.fori_loop(0, x_rows, out_row, 0)


def band(length, taps):
    radius = len(taps) // 2
    matrix = np.zeros((length, length), np.float32)
    for i in range(length):
        for t in range(-radius, radius + 1):
            if 0 <= i + t < length:
                matrix[i, i + t] = taps[t + radius]
    return matrix


def post_stage(drive_ext, own_ext):
    extended, y_rows, z_rows = drive_ext.shape
    x_rows = extended - 2 * RADIUS
    taps = gauss_taps(RADIUS)
    wz = jnp.asarray(band(z_rows, taps).T)
    vmem = pl.BlockSpec(memory_space=pltpu.VMEM)
    return pl.pallas_call(
        post_kernel,
        out_shape=(
            jax.ShapeDtypeStruct((3, x_rows, y_rows, z_rows), jnp.float32),
            jax.ShapeDtypeStruct((x_rows, y_rows, z_rows), jnp.float32),
        ),
        in_specs=[vmem] * 3,
        out_specs=(vmem, vmem),
        scratch_shapes=[
            pltpu.VMEM((3 * extended * y_rows, z_rows), jnp.float32),
            pltpu.VMEM((3 * x_rows * y_rows, z_rows), jnp.float32),
        ],
    )(drive_ext, own_ext, wz)


def shards(images, pairings):
    weights = gauss_taps(RADIUS)
    groups = lax.axis_size("img")
    own = images[0]
    x_rows, y_rows, _ = own.shape
    rows = x_rows // groups
    own_ext = halo_rows(own, RADIUS + 1)
    near = own_ext[RADIUS:-RADIUS]
    pieces = jnp.stack([near[j * rows:j * rows + rows + 2] for j in range(groups)])
    stack = lax.all_to_all(pieces, "img", split_axis=0, concat_axis=0, tiled=True)
    drive_part = slice_drive(stack, pairings)
    returned = lax.all_to_all(drive_part, "img", split_axis=0, concat_axis=0, tiled=True)
    drive_sum = returned.reshape(own.shape)
    drive_ext = halo_rows(drive_sum, RADIUS)
    velocity, advected = post_stage(drive_ext, own_ext)
    return (advected[None], velocity[None])


def solution(mesh):
    return jax.shard_map(
        shards,
        mesh=mesh,
        in_specs=(P("img", "space", None, None), P()),
        out_specs=(P("img", "space", None, None), P("img", None, "space", None, None)),
        check_vma=False,
    )
```

```python
import math

import jax
import numpy as np
import jax.numpy as jnp
from jax import lax
from jax.experimental import pallas as pl
from jax.experimental.pallas import tpu as pltpu
from jax.sharding import PartitionSpec as P

RADIUS = 4
PAIRINGS = 3

gauss_sigma = 1.5
step_scale = 8.0
floor_product = 0.25
floor_variance = 0.5


def gauss_taps(radius):
    raw_taps = [
        math.exp(-(offset * offset) / (2.0 * gauss_sigma * gauss_sigma))
        for offset in range(-radius, radius + 1)
    ]
    total_weight = sum(raw_taps)
    return [raw_weight / total_weight for raw_weight in raw_taps]


def halo_rows(value, width):
    peers = lax.axis_size("space")
    up = [(i, i + 1) for i in range(peers - 1)]
    down = [(i + 1, i) for i in range(peers - 1)]
    before = lax.ppermute(value[-width:], "space", up)
    after = lax.ppermute(value[:width], "space", down)
    return jnp.concatenate([before, value, after], axis=0)


def padded_along(volume, dimension, margin):
    widths = [(0, 0)] * volume.ndim
    widths[dimension] = (margin, margin)
    return jnp.pad(volume, widths)


def window(padded, dimension, offset, length):
    return lax.slice_in_dim(padded, offset, offset + length, axis=dimension)


def central(volume, dimension):
    length = volume.shape[dimension]
    padded = padded_along(volume, dimension, 1)
    return (window(padded, dimension, 2, length) - window(padded, dimension, 0, length)) * 0.5


def smooth_along(volume, dimension, weights):
    length = volume.shape[dimension]
    padded = padded_along(volume, dimension, len(weights) // 2)
    result = weights[0] * window(padded, dimension, 0, length)
    for tap_index in range(1, len(weights)):
        result = result + weights[tap_index] * window(padded, dimension, tap_index, length)
    return result


def smooth_rows(extended, weights):
    length = extended.shape[1] - len(weights) + 1
    result = weights[0] * window(extended, 1, 0, length)
    for tap_index in range(1, len(weights)):
        result = result + weights[tap_index] * window(extended, 1, tap_index, length)
    return result


def box_rows(volume):
    sx = volume[:-2] + volume[1:-1] + volume[2:]
    last = sx.shape[1] - 1
    row = lax.broadcasted_iota(jnp.int32, sx.shape, 1)
    before = jnp.where(row >= 1, pltpu.roll(sx, 1, 1), 0.0)
    after = jnp.where(row < last, pltpu.roll(sx, last, 1), 0.0)
    return (before + sx + after) / 9.0


def pair_terms(g, pair_ref, stack_ref, mean_ref, spread_ref):
    own = stack_ref[g]
    mean_own = mean_ref[g]
    spread_own = spread_ref[g]
    center_own = own[1:-1] - mean_own
    guarded_spread = jnp.maximum(spread_own, floor_variance)
    drive_sum = None
    for pairing_row in range(PAIRINGS):
        h = pair_ref[pairing_row, g]
        partner = stack_ref[h]
        mean_partner = mean_ref[h]
        spread_partner = spread_ref[h]
        cross_term = box_rows(own * partner) - mean_own * mean_partner
        factor = 2.0 * cross_term / jnp.maximum(spread_own * spread_partner, floor_product)
        ratio_term = cross_term / guarded_spread
        pair_term = factor * (partner[1:-1] - mean_partner - ratio_term * center_own)
        drive_sum = pair_term if drive_sum is None else drive_sum + pair_term
    return drive_sum


def row_groups(first, count, rows):
    groups = []
    for r in range(first, first + count):
        owner = r // rows
        if groups and groups[-1][0] == owner:
            groups[-1][2] += 1
        else:
            groups.append([owner, r - owner * rows, 1, r - first])
    return groups


def front_kernel(
    pair_ref, own_ref, drive_ref, stack_ref, mean_ref, spread_ref, out_ref, zero_ref,
    send_a, recv_a, send_h, recv_h, send_b, recv_b, send_c, recv_c, local_sem,
):
    mesh = pl.DeviceIdType.MESH
    groups, width, y_rows, z_rows = stack_ref.shape
    rows = width - 2
    x_rows = own_ref.shape[0]
    spaces = lax.axis_size("space")
    me = lax.axis_index("img")
    s = lax.axis_index("space")
    has_lo = (s + spaces - 1) // spaces
    has_hi = (2 * spaces - 2 - s) // spaces

    barrier = pltpu.get_barrier_semaphore()
    for offset in (-1, 0, 1):
        exists = {-1: s > 0, 0: s >= 0, 1: s < spaces - 1}[offset]
        for g in range(groups):
            @pl.when(exists & ((offset != 0) | (me != g)))
            def _():
                pl.semaphore_signal(barrier, inc=1, device_id=(g, (s + offset + spaces) % spaces), device_id_type=mesh)
    pl.semaphore_wait(barrier, groups * (1 + has_lo + has_hi) - 1)

    zero_ref[...] = jnp.zeros(zero_ref.shape, jnp.float32)

    def piece(t):
        lo = max(t * rows - 1, 0)
        hi = min(t * rows + rows + 1, x_rows)
        return own_ref.at[pl.ds(lo, hi - lo)], lo - (t * rows - 1), hi - lo

    def piece_copy(t, src_image):
        src, dst_lo, count = piece(t)
        dst = stack_ref.at[src_image, pl.ds(dst_lo, count)]
        return src, dst

    for t in range(groups):
        src, dst = piece_copy(t, me)

        @pl.when(me == t)
        def _():
            pltpu.make_async_copy(src, dst, local_sem.at[0]).start()

        @pl.when(me != t)
        def _():
            pltpu.make_async_remote_copy(
                src, dst, send_a.at[t], recv_a.at[me], device_id=(t, s), device_id_type=mesh
            ).start()

    @pl.when(s < spaces - 1)
    def _():
        pltpu.make_async_remote_copy(
            own_ref.at[pl.ds(x_rows - 1, 1)], stack_ref.at[me, pl.ds(0, 1)],
            send_h.at[0], recv_h.at[0, me], device_id=(0, (s + 1) % spaces), device_id_type=mesh,
        ).start()

    @pl.when(s > 0)
    def _():
        pltpu.make_async_remote_copy(
            own_ref.at[pl.ds(0, 1)], stack_ref.at[me, pl.ds(width - 1, 1)],
            send_h.at[1], recv_h.at[1, me], device_id=(groups - 1, (s + spaces - 1) % spaces), device_id_type=mesh,
        ).start()

    for t in range(groups):
        src, dst = piece_copy(t, 0)
        for g in range(groups):
            @pl.when((me == t) & (me != g))
            def _():
                pltpu.make_async_remote_copy(
                    src, stack_ref.at[g, pl.ds(piece(t)[1], piece(t)[2])],
                    send_a.at[0], recv_a.at[g], device_id=(g, s), device_id_type=mesh,
                ).wait_recv()

        @pl.when(me == t)
        def _():
            pltpu.make_async_copy(src, dst, local_sem.at[0]).wait()

    for g in range(groups):
        @pl.when((me == 0) & (s > 0))
        def _():
            pltpu.make_async_remote_copy(
                own_ref.at[pl.ds(0, 1)], stack_ref.at[g, pl.ds(0, 1)],
                send_h.at[0], recv_h.at[0, g], device_id=(0, s), device_id_type=mesh,
            ).wait_recv()

        @pl.when((me == groups - 1) & (s < spaces - 1))
        def _():
            pltpu.make_async_remote_copy(
                own_ref.at[pl.ds(0, 1)], stack_ref.at[g, pl.ds(width - 1, 1)],
                send_h.at[1], recv_h.at[1, g], device_id=(0, s), device_id_type=mesh,
            ).wait_recv()

    @pl.when((me == 0) & (s == 0))
    def _():
        stack_ref[:, 0] = jnp.zeros((groups, y_rows, z_rows), jnp.float32)

    @pl.when((me == groups - 1) & (s == spaces - 1))
    def _():
        stack_ref[:, width - 1] = jnp.zeros((groups, y_rows, z_rows), jnp.float32)

    def stats(g, carry):
        value = stack_ref[g]
        mean = box_rows(value)
        mean_ref[g] = mean
        spread_ref[g] = box_rows(value * value) - mean * mean
        return carry

    lax.fori_loop(0, groups, stats, 0)

    below = row_groups(x_rows - RADIUS, RADIUS, rows)
    above = row_groups(0, RADIUS, rows)

    def main_copy(g):
        src = out_ref.at[g]
        dst = drive_ref.at[pl.ds(RADIUS + me * rows, rows)]
        return src, dst

    def halo_copies(g):
        copies = []
        for index, (owner, src_lo, count, dst_lo) in enumerate(below):
            copies.append((owner, s < spaces - 1, 1, index, out_ref.at[g, pl.ds(src_lo, count)],
                           drive_ref.at[pl.ds(dst_lo, count)]))
        for index, (owner, src_lo, count, dst_lo) in enumerate(above):
            copies.append((owner, s > 0, -1, len(below) + index, out_ref.at[g, pl.ds(src_lo, count)],
                           drive_ref.at[pl.ds(x_rows + RADIUS + dst_lo, count)]))
        return copies

    def pairs(g, carry):
        out_ref[g] = pair_terms(g, pair_ref, stack_ref, mean_ref, spread_ref)
        src, dst = main_copy(g)

        @pl.when(me == g)
        def _():
            pltpu.make_async_copy(src, dst, local_sem.at[1]).start()

        @pl.when(me != g)
        def _():
            pltpu.make_async_remote_copy(
                src, dst, send_b.at[g], recv_b.at[me], device_id=(g, s), device_id_type=mesh
            ).start()

        for owner, exists, offset, index, hsrc, hdst in halo_copies(g):
            @pl.when((me == owner) & exists)
            def _():
                pltpu.make_async_remote_copy(
                    hsrc, hdst, send_c.at[index, g], recv_c.at[index],
                    device_id=(g, (s + offset + spaces) % spaces), device_id_type=mesh,
                ).start()
        return carry

    lax.fori_loop(0, groups, pairs, 0)

    @pl.when(s == 0)
    def _():
        pltpu.make_async_copy(zero_ref, drive_ref.at[pl.ds(0, RADIUS)], local_sem.at[2]).start()

    @pl.when(s == spaces - 1)
    def _():
        pltpu.make_async_copy(
            zero_ref, drive_ref.at[pl.ds(x_rows + RADIUS, RADIUS)], local_sem.at[3]
        ).start()

    for t in range(groups):
        src, dst = piece_copy(t, me)

        @pl.when(me != t)
        def _():
            pltpu.make_async_remote_copy(
                src, dst, send_a.at[t], recv_a.at[me], device_id=(t, s), device_id_type=mesh
            ).wait_send()

    @pl.when(s < spaces - 1)
    def _():
        pltpu.make_async_remote_copy(
            own_ref.at[pl.ds(x_rows - 1, 1)], stack_ref.at[me, pl.ds(0, 1)],
            send_h.at[0], recv_h.at[0, me], device_id=(0, (s + 1) % spaces), device_id_type=mesh,
        ).wait_send()

    @pl.when(s > 0)
    def _():
        pltpu.make_async_remote_copy(
            own_ref.at[pl.ds(0, 1)], stack_ref.at[me, pl.ds(width - 1, 1)],
            send_h.at[1], recv_h.at[1, me], device_id=(groups - 1, (s + spaces - 1) % spaces), device_id_type=mesh,
        ).wait_send()

    for g in range(groups):
        src, dst = main_copy(g)

        @pl.when(me == g)
        def _():
            pltpu.make_async_copy(src, dst, local_sem.at[1]).wait()

        @pl.when(me != g)
        def _():
            pltpu.make_async_remote_copy(
                src, dst, send_b.at[g], recv_b.at[me], device_id=(g, s), device_id_type=mesh
            ).wait_send()

        for owner, exists, offset, index, hsrc, hdst in halo_copies(g):
            @pl.when((me == owner) & exists)
            def _():
                pltpu.make_async_remote_copy(
                    hsrc, hdst, send_c.at[index, g], recv_c.at[index],
                    device_id=(g, (s + offset + spaces) % spaces), device_id_type=mesh,
                ).wait_send()

    for t in range(groups):
        @pl.when(me != t)
        def _():
            pltpu.make_async_remote_copy(
                out_ref.at[0], drive_ref.at[pl.ds(RADIUS + t * rows, rows)],
                send_b.at[0], recv_b.at[t], device_id=(t, s), device_id_type=mesh,
            ).wait_recv()

    for owner, exists, offset, index, hsrc, hdst in halo_copies(0):
        @pl.when(((offset == 1) & (s > 0)) | ((offset == -1) & (s < spaces - 1)))
        def _():
            pltpu.make_async_remote_copy(
                hsrc, hdst, send_c.at[index, 0], recv_c.at[index],
                device_id=(owner, s), device_id_type=mesh,
            ).wait_recv()

    @pl.when(s == 0)
    def _():
        pltpu.make_async_copy(zero_ref, drive_ref.at[pl.ds(0, RADIUS)], local_sem.at[2]).wait()

    @pl.when(s == spaces - 1)
    def _():
        pltpu.make_async_copy(
            zero_ref, drive_ref.at[pl.ds(x_rows + RADIUS, RADIUS)], local_sem.at[3]
        ).wait()


def front_stage(own, pairings, groups):
    x_rows, y_rows, z_rows = own.shape
    rows = x_rows // groups
    shape = (groups, rows, y_rows, z_rows)
    halos = len(row_groups(x_rows - RADIUS, RADIUS, rows)) + len(row_groups(0, RADIUS, rows))
    dma = pltpu.SemaphoreType.DMA
    return pl.pallas_call(
        front_kernel,
        out_shape=jax.ShapeDtypeStruct((x_rows + 2 * RADIUS, y_rows, z_rows), jnp.float32),
        in_specs=[
            pl.BlockSpec(memory_space=pltpu.SMEM),
            pl.BlockSpec(memory_space=pltpu.VMEM),
        ],
        out_specs=pl.BlockSpec(memory_space=pl.ANY),
        scratch_shapes=[
            pltpu.VMEM((groups, rows + 2, y_rows, z_rows), jnp.float32),
            pltpu.VMEM(shape, jnp.float32),
            pltpu.VMEM(shape, jnp.float32),
            pltpu.VMEM(shape, jnp.float32),
            pltpu.VMEM((RADIUS, y_rows, z_rows), jnp.float32),
            dma((groups,)),
            dma((groups,)),
            dma((2,)),
            dma((2, groups)),
            dma((groups,)),
            dma((groups,)),
            dma((halos, groups)),
            dma((halos,)),
            dma((4,)),
        ],
        compiler_params=pltpu.CompilerParams(collective_id=0, has_side_effects=True),
    )(pairings, own)


def shifted(value, offset, axis):
    length = value.shape[axis]
    rolled = pltpu.roll(value, (-offset) % length, axis)
    index = lax.broadcasted_iota(jnp.int32, value.shape, axis) + offset
    return jnp.where((index >= 0) & (index < length), rolled, 0.0)


def post_kernel(drive_ref, own_ref, wz_ref, vel_ref, adv_ref, force_ref, pass_ref):
    extended, y_rows, _ = drive_ref.shape
    x_rows = vel_ref.shape[1]
    taps = gauss_taps(RADIUS)

    def plane(c, r, count):
        return pl.ds(pl.multiple_of((c * count + r) * y_rows, 8), y_rows)

    def force_row(r, carry):
        value = own_ref[r + 1]
        drive = drive_ref[r]
        force_ref[plane(0, r, extended)] = drive * ((own_ref[r + 2] - own_ref[r]) * 0.5)
        force_ref[plane(1, r, extended)] = drive * (
            (shifted(value, 1, 0) - shifted(value, -1, 0)) * 0.5
        )
        force_ref[plane(2, r, extended)] = drive * (
            (shifted(value, 1, 1) - shifted(value, -1, 1)) * 0.5
        )
        return carry

    lax.fori_loop(0, extended, force_row, 0)

    def x_pass(x, carry):
        for c in range(3):
            acc = taps[0] * force_ref[plane(c, x, extended)]
            for t in range(1, len(taps)):
                acc = acc + taps[t] * force_ref[plane(c, x + t, extended)]
            pass_ref[plane(c, x, x_rows)] = acc
        return carry

    lax.fori_loop(0, x_rows, x_pass, 0)
    wz = wz_ref[...]
    chunk = 8 * y_rows
    chunks = pass_ref.shape[0] // chunk

    def z_pass(i, carry):
        rows = pl.ds(pl.multiple_of(i * chunk, 8), chunk)
        pass_ref[rows] = jnp.dot(
            pass_ref[rows], wz, precision=lax.Precision.HIGHEST,
            preferred_element_type=jnp.float32,
        )
        return carry

    lax.fori_loop(0, chunks, z_pass, 0)

    def out_row(x, carry):
        value = own_ref[x + RADIUS + 1]
        change = None
        for c in range(3):
            smoothed_z = pass_ref[plane(c, x, x_rows)]
            acc = taps[0] * shifted(smoothed_z, -RADIUS, 0)
            for t in range(1, len(taps)):
                acc = acc + taps[t] * shifted(smoothed_z, t - RADIUS, 0)
            speed = step_scale * acc
            vel_ref[c, x] = speed
            if c == 0:
                backward = value - own_ref[x + RADIUS]
                forward = own_ref[x + RADIUS + 2] - value
            else:
                backward = value - shifted(value, -1, c - 1)
                forward = shifted(value, 1, c - 1) - value
            part = jnp.maximum(speed, 0.0) * backward + jnp.minimum(speed, 0.0) * forward
            change = part if change is None else change + part
        adv_ref[x] = value - change
        return carry

    lax.fori_loop(0, x_rows, out_row, 0)


def band(length, taps):
    radius = len(taps) // 2
    matrix = np.zeros((length, length), np.float32)
    for i in range(length):
        for t in range(-radius, radius + 1):
            if 0 <= i + t < length:
                matrix[i, i + t] = taps[t + radius]
    return matrix


def post_stage(drive_ext, own_ext):
    extended, y_rows, z_rows = drive_ext.shape
    x_rows = extended - 2 * RADIUS
    taps = gauss_taps(RADIUS)
    wz = jnp.asarray(band(z_rows, taps).T)
    vmem = pl.BlockSpec(memory_space=pltpu.VMEM)
    return pl.pallas_call(
        post_kernel,
        out_shape=(
            jax.ShapeDtypeStruct((3, x_rows, y_rows, z_rows), jnp.float32),
            jax.ShapeDtypeStruct((x_rows, y_rows, z_rows), jnp.float32),
        ),
        in_specs=[vmem] * 3,
        out_specs=(vmem, vmem),
        scratch_shapes=[
            pltpu.VMEM((3 * extended * y_rows, z_rows), jnp.float32),
            pltpu.VMEM((3 * x_rows * y_rows, z_rows), jnp.float32),
        ],
    )(drive_ext, own_ext, wz)


def shards(images, pairings):
    weights = gauss_taps(RADIUS)
    groups = lax.axis_size("img")
    own = images[0]
    x_rows, y_rows, _ = own.shape
    own_ext = halo_rows(own, RADIUS + 1)
    drive_ext = front_stage(own, pairings, groups)
    velocity, advected = post_stage(drive_ext, own_ext)
    return (advected[None], velocity[None])


def solution(mesh):
    return jax.shard_map(
        shards,
        mesh=mesh,
        in_specs=(P("img", "space", None, None), P()),
        out_specs=(P("img", "space", None, None), P("img", None, "space", None, None)),
        check_vma=False,
    )
```

```python
import math

import jax
import numpy as np
import jax.numpy as jnp
from jax import lax
from jax.experimental import pallas as pl
from jax.experimental.pallas import tpu as pltpu
from jax.sharding import PartitionSpec as P

RADIUS = 4
PAIRINGS = 3

gauss_sigma = 1.5
step_scale = 8.0
floor_product = 0.25
floor_variance = 0.5


def gauss_taps(radius):
    raw_taps = [
        math.exp(-(offset * offset) / (2.0 * gauss_sigma * gauss_sigma))
        for offset in range(-radius, radius + 1)
    ]
    total_weight = sum(raw_taps)
    return [raw_weight / total_weight for raw_weight in raw_taps]


def halo_rows(value, width):
    peers = lax.axis_size("space")
    up = [(i, i + 1) for i in range(peers - 1)]
    down = [(i + 1, i) for i in range(peers - 1)]
    before = lax.ppermute(value[-width:], "space", up)
    after = lax.ppermute(value[:width], "space", down)
    return jnp.concatenate([before, value, after], axis=0)


def padded_along(volume, dimension, margin):
    widths = [(0, 0)] * volume.ndim
    widths[dimension] = (margin, margin)
    return jnp.pad(volume, widths)


def window(padded, dimension, offset, length):
    return lax.slice_in_dim(padded, offset, offset + length, axis=dimension)


def central(volume, dimension):
    length = volume.shape[dimension]
    padded = padded_along(volume, dimension, 1)
    return (window(padded, dimension, 2, length) - window(padded, dimension, 0, length)) * 0.5


def smooth_along(volume, dimension, weights):
    length = volume.shape[dimension]
    padded = padded_along(volume, dimension, len(weights) // 2)
    result = weights[0] * window(padded, dimension, 0, length)
    for tap_index in range(1, len(weights)):
        result = result + weights[tap_index] * window(padded, dimension, tap_index, length)
    return result


def smooth_rows(extended, weights):
    length = extended.shape[1] - len(weights) + 1
    result = weights[0] * window(extended, 1, 0, length)
    for tap_index in range(1, len(weights)):
        result = result + weights[tap_index] * window(extended, 1, tap_index, length)
    return result


def box_rows(volume):
    sx = volume[:-2] + volume[1:-1] + volume[2:]
    last = sx.shape[1] - 1
    row = lax.broadcasted_iota(jnp.int32, sx.shape, 1)
    before = jnp.where(row >= 1, pltpu.roll(sx, 1, 1), 0.0)
    after = jnp.where(row < last, pltpu.roll(sx, last, 1), 0.0)
    return (before + sx + after) / 9.0


def pair_terms(g, pair_ref, stack_ref, mean_ref, spread_ref):
    own = stack_ref[g]
    mean_own = mean_ref[g]
    spread_own = spread_ref[g]
    center_own = own[1:-1] - mean_own
    guarded_spread = jnp.maximum(spread_own, floor_variance)
    drive_sum = None
    for pairing_row in range(PAIRINGS):
        h = pair_ref[pairing_row, g]
        partner = stack_ref[h]
        mean_partner = mean_ref[h]
        spread_partner = spread_ref[h]
        cross_term = box_rows(own * partner) - mean_own * mean_partner
        factor = 2.0 * cross_term / jnp.maximum(spread_own * spread_partner, floor_product)
        ratio_term = cross_term / guarded_spread
        pair_term = factor * (partner[1:-1] - mean_partner - ratio_term * center_own)
        drive_sum = pair_term if drive_sum is None else drive_sum + pair_term
    return drive_sum


def row_groups(first, count, rows):
    groups = []
    for r in range(first, first + count):
        owner = r // rows
        if groups and groups[-1][0] == owner:
            groups[-1][2] += 1
        else:
            groups.append([owner, r - owner * rows, 1, r - first])
    return groups


def front_kernel(
    pair_ref, own_ref, drive_ref, stack_ref, mean_ref, spread_ref, out_ref, zero_ref,
    send_a, recv_a, send_h, recv_h, send_b, recv_b, send_c, recv_c, local_sem,
):
    mesh = pl.DeviceIdType.MESH
    groups, width, y_rows, z_rows = stack_ref.shape
    rows = width - 2
    x_rows = own_ref.shape[0]
    spaces = lax.axis_size("space")
    me = lax.axis_index("img")
    s = lax.axis_index("space")
    has_lo = (s + spaces - 1) // spaces
    has_hi = (2 * spaces - 2 - s) // spaces

    barrier = pltpu.get_barrier_semaphore()
    for offset in (-1, 0, 1):
        exists = {-1: s > 0, 0: s >= 0, 1: s < spaces - 1}[offset]
        for g in range(groups):
            @pl.when(exists & ((offset != 0) | (me != g)))
            def _():
                pl.semaphore_signal(barrier, inc=1, device_id=(g, (s + offset + spaces) % spaces), device_id_type=mesh)
    pl.semaphore_wait(barrier, groups * (1 + has_lo + has_hi) - 1)

    zero_ref[...] = jnp.zeros(zero_ref.shape, jnp.float32)

    def piece(t):
        lo = max(t * rows - 1, 0)
        hi = min(t * rows + rows + 1, x_rows)
        return own_ref.at[pl.ds(lo, hi - lo)], lo - (t * rows - 1), hi - lo

    def piece_copy(t, src_image):
        src, dst_lo, count = piece(t)
        dst = stack_ref.at[src_image, pl.ds(dst_lo, count)]
        return src, dst

    def forward_copy(t_dyn, wait):
        for kind in range(3):
            cond = {0: t_dyn == 0, 1: t_dyn == groups - 1, 2: (t_dyn > 0) & (t_dyn < groups - 1)}[kind]

            @pl.when(cond & (t_dyn != me))
            def _():
                if kind == 0:
                    src, dst_lo, count = own_ref.at[pl.ds(0, rows + 1)], 1, rows + 1
                elif kind == 1:
                    src, dst_lo, count = own_ref.at[pl.ds(x_rows - rows - 1, rows + 1)], 0, rows + 1
                else:
                    src, dst_lo, count = own_ref.at[pl.ds(t_dyn * rows - 1, rows + 2)], 0, rows + 2
                copy = pltpu.make_async_remote_copy(
                    src, stack_ref.at[me, pl.ds(dst_lo, count)], send_a.at[t_dyn], recv_a.at[me],
                    device_id=(t_dyn, s), device_id_type=mesh,
                )
                if wait:
                    copy.wait_send()
                else:
                    copy.start()

    for t in range(groups):
        src, dst = piece_copy(t, me)

        @pl.when(me == t)
        def _():
            pltpu.make_async_copy(src, dst, local_sem.at[0]).start()

    for i in range(1, groups):
        forward_copy((me + i) % groups, False)

    @pl.when(s < spaces - 1)
    def _():
        pltpu.make_async_remote_copy(
            own_ref.at[pl.ds(x_rows - 1, 1)], stack_ref.at[me, pl.ds(0, 1)],
            send_h.at[0], recv_h.at[0, me], device_id=(0, (s + 1) % spaces), device_id_type=mesh,
        ).start()

    @pl.when(s > 0)
    def _():
        pltpu.make_async_remote_copy(
            own_ref.at[pl.ds(0, 1)], stack_ref.at[me, pl.ds(width - 1, 1)],
            send_h.at[1], recv_h.at[1, me], device_id=(groups - 1, (s + spaces - 1) % spaces), device_id_type=mesh,
        ).start()

    def stats(g):
        value = stack_ref[g]
        mean = box_rows(value)
        mean_ref[g] = mean
        spread_ref[g] = box_rows(value * value) - mean * mean

    @pl.when((me == 0) & (s == 0))
    def _():
        stack_ref[:, 0] = jnp.zeros((groups, y_rows, z_rows), jnp.float32)

    @pl.when((me == groups - 1) & (s == spaces - 1))
    def _():
        stack_ref[:, width - 1] = jnp.zeros((groups, y_rows, z_rows), jnp.float32)

    def arrive(i, carry):
        g = (me + groups - i) % groups

        @pl.when(i == 0)
        def _():
            for t in range(groups):
                src, dst = piece_copy(t, me)

                @pl.when(me == t)
                def _():
                    pltpu.make_async_copy(src, dst, local_sem.at[0]).wait()

        @pl.when(i != 0)
        def _():
            for t in range(groups):
                src, dst = piece_copy(t, 0)

                @pl.when(me == t)
                def _():
                    pltpu.make_async_remote_copy(
                        src, stack_ref.at[g, pl.ds(piece(t)[1], piece(t)[2])],
                        send_a.at[0], recv_a.at[g], device_id=(g, s), device_id_type=mesh,
                    ).wait_recv()

        @pl.when((me == 0) & (s > 0))
        def _():
            pltpu.make_async_remote_copy(
                own_ref.at[pl.ds(0, 1)], stack_ref.at[g, pl.ds(0, 1)],
                send_h.at[0], recv_h.at[0, g], device_id=(0, s), device_id_type=mesh,
            ).wait_recv()

        @pl.when((me == groups - 1) & (s < spaces - 1))
        def _():
            pltpu.make_async_remote_copy(
                own_ref.at[pl.ds(0, 1)], stack_ref.at[g, pl.ds(width - 1, 1)],
                send_h.at[1], recv_h.at[1, g], device_id=(0, s), device_id_type=mesh,
            ).wait_recv()

        stats(g)
        return carry

    lax.fori_loop(0, groups, arrive, 0)

    below = row_groups(x_rows - RADIUS, RADIUS, rows)
    above = row_groups(0, RADIUS, rows)

    def main_copy(g):
        src = out_ref.at[g]
        dst = drive_ref.at[pl.ds(RADIUS + me * rows, rows)]
        return src, dst

    def halo_copies(g):
        copies = []
        for index, (owner, src_lo, count, dst_lo) in enumerate(below):
            copies.append((owner, s < spaces - 1, 1, index, out_ref.at[g, pl.ds(src_lo, count)],
                           drive_ref.at[pl.ds(dst_lo, count)]))
        for index, (owner, src_lo, count, dst_lo) in enumerate(above):
            copies.append((owner, s > 0, -1, len(below) + index, out_ref.at[g, pl.ds(src_lo, count)],
                           drive_ref.at[pl.ds(x_rows + RADIUS + dst_lo, count)]))
        return copies

    def pairs(i, carry):
        g = (me + i) % groups
        out_ref[g] = pair_terms(g, pair_ref, stack_ref, mean_ref, spread_ref)
        src, dst = main_copy(g)

        @pl.when(me == g)
        def _():
            pltpu.make_async_copy(src, dst, local_sem.at[1]).start()

        @pl.when(me != g)
        def _():
            pltpu.make_async_remote_copy(
                src, dst, send_b.at[g], recv_b.at[me], device_id=(g, s), device_id_type=mesh
            ).start()

        for owner, exists, offset, index, hsrc, hdst in halo_copies(g):
            @pl.when((me == owner) & exists)
            def _():
                pltpu.make_async_remote_copy(
                    hsrc, hdst, send_c.at[index, g], recv_c.at[index],
                    device_id=(g, (s + offset + spaces) % spaces), device_id_type=mesh,
                ).start()
        return carry

    lax.fori_loop(0, groups, pairs, 0)

    @pl.when(s == 0)
    def _():
        pltpu.make_async_copy(zero_ref, drive_ref.at[pl.ds(0, RADIUS)], local_sem.at[2]).start()

    @pl.when(s == spaces - 1)
    def _():
        pltpu.make_async_copy(
            zero_ref, drive_ref.at[pl.ds(x_rows + RADIUS, RADIUS)], local_sem.at[3]
        ).start()

    for i in range(1, groups):
        forward_copy((me + i) % groups, True)

    @pl.when(s < spaces - 1)
    def _():
        pltpu.make_async_remote_copy(
            own_ref.at[pl.ds(x_rows - 1, 1)], stack_ref.at[me, pl.ds(0, 1)],
            send_h.at[0], recv_h.at[0, me], device_id=(0, (s + 1) % spaces), device_id_type=mesh,
        ).wait_send()

    @pl.when(s > 0)
    def _():
        pltpu.make_async_remote_copy(
            own_ref.at[pl.ds(0, 1)], stack_ref.at[me, pl.ds(width - 1, 1)],
            send_h.at[1], recv_h.at[1, me], device_id=(groups - 1, (s + spaces - 1) % spaces), device_id_type=mesh,
        ).wait_send()

    for g in range(groups):
        src, dst = main_copy(g)

        @pl.when(me == g)
        def _():
            pltpu.make_async_copy(src, dst, local_sem.at[1]).wait()

        @pl.when(me != g)
        def _():
            pltpu.make_async_remote_copy(
                src, dst, send_b.at[g], recv_b.at[me], device_id=(g, s), device_id_type=mesh
            ).wait_send()

        for owner, exists, offset, index, hsrc, hdst in halo_copies(g):
            @pl.when((me == owner) & exists)
            def _():
                pltpu.make_async_remote_copy(
                    hsrc, hdst, send_c.at[index, g], recv_c.at[index],
                    device_id=(g, (s + offset + spaces) % spaces), device_id_type=mesh,
                ).wait_send()

    for t in range(groups):
        @pl.when(me != t)
        def _():
            pltpu.make_async_remote_copy(
                out_ref.at[0], drive_ref.at[pl.ds(RADIUS + t * rows, rows)],
                send_b.at[0], recv_b.at[t], device_id=(t, s), device_id_type=mesh,
            ).wait_recv()

    for owner, exists, offset, index, hsrc, hdst in halo_copies(0):
        @pl.when(((offset == 1) & (s > 0)) | ((offset == -1) & (s < spaces - 1)))
        def _():
            pltpu.make_async_remote_copy(
                hsrc, hdst, send_c.at[index, 0], recv_c.at[index],
                device_id=(owner, s), device_id_type=mesh,
            ).wait_recv()

    @pl.when(s == 0)
    def _():
        pltpu.make_async_copy(zero_ref, drive_ref.at[pl.ds(0, RADIUS)], local_sem.at[2]).wait()

    @pl.when(s == spaces - 1)
    def _():
        pltpu.make_async_copy(
            zero_ref, drive_ref.at[pl.ds(x_rows + RADIUS, RADIUS)], local_sem.at[3]
        ).wait()


def front_stage(own, pairings, groups):
    x_rows, y_rows, z_rows = own.shape
    rows = x_rows // groups
    shape = (groups, rows, y_rows, z_rows)
    halos = len(row_groups(x_rows - RADIUS, RADIUS, rows)) + len(row_groups(0, RADIUS, rows))
    dma = pltpu.SemaphoreType.DMA
    return pl.pallas_call(
        front_kernel,
        out_shape=jax.ShapeDtypeStruct((x_rows + 2 * RADIUS, y_rows, z_rows), jnp.float32),
        in_specs=[
            pl.BlockSpec(memory_space=pltpu.SMEM),
            pl.BlockSpec(memory_space=pltpu.VMEM),
        ],
        out_specs=pl.BlockSpec(memory_space=pl.ANY),
        scratch_shapes=[
            pltpu.VMEM((groups, rows + 2, y_rows, z_rows), jnp.float32),
            pltpu.VMEM(shape, jnp.float32),
            pltpu.VMEM(shape, jnp.float32),
            pltpu.VMEM(shape, jnp.float32),
            pltpu.VMEM((RADIUS, y_rows, z_rows), jnp.float32),
            dma((groups,)),
            dma((groups,)),
            dma((2,)),
            dma((2, groups)),
            dma((groups,)),
            dma((groups,)),
            dma((halos, groups)),
            dma((halos,)),
            dma((4,)),
        ],
        compiler_params=pltpu.CompilerParams(collective_id=0, has_side_effects=True),
    )(pairings, own)


def shifted(value, offset, axis):
    length = value.shape[axis]
    rolled = pltpu.roll(value, (-offset) % length, axis)
    index = lax.broadcasted_iota(jnp.int32, value.shape, axis) + offset
    return jnp.where((index >= 0) & (index < length), rolled, 0.0)


def post_kernel(drive_ref, own_ref, wz_ref, vel_ref, adv_ref, force_ref, pass_ref):
    extended, y_rows, _ = drive_ref.shape
    x_rows = vel_ref.shape[1]
    taps = gauss_taps(RADIUS)

    def plane(c, r, count):
        return pl.ds(pl.multiple_of((c * count + r) * y_rows, 8), y_rows)

    def force_row(r, carry):
        value = own_ref[r + 1]
        drive = drive_ref[r]
        force_ref[plane(0, r, extended)] = drive * ((own_ref[r + 2] - own_ref[r]) * 0.5)
        force_ref[plane(1, r, extended)] = drive * (
            (shifted(value, 1, 0) - shifted(value, -1, 0)) * 0.5
        )
        force_ref[plane(2, r, extended)] = drive * (
            (shifted(value, 1, 1) - shifted(value, -1, 1)) * 0.5
        )
        return carry

    lax.fori_loop(0, extended, force_row, 0)

    def x_pass(x, carry):
        for c in range(3):
            acc = taps[0] * force_ref[plane(c, x, extended)]
            for t in range(1, len(taps)):
                acc = acc + taps[t] * force_ref[plane(c, x + t, extended)]
            pass_ref[plane(c, x, x_rows)] = acc
        return carry

    lax.fori_loop(0, x_rows, x_pass, 0)
    wz = wz_ref[...]
    chunk = 8 * y_rows
    chunks = pass_ref.shape[0] // chunk

    def z_pass(i, carry):
        rows = pl.ds(pl.multiple_of(i * chunk, 8), chunk)
        pass_ref[rows] = jnp.dot(
            pass_ref[rows], wz, precision=lax.Precision.HIGHEST,
            preferred_element_type=jnp.float32,
        )
        return carry

    lax.fori_loop(0, chunks, z_pass, 0)

    def out_row(x, carry):
        value = own_ref[x + RADIUS + 1]
        change = None
        for c in range(3):
            smoothed_z = pass_ref[plane(c, x, x_rows)]
            acc = taps[0] * shifted(smoothed_z, -RADIUS, 0)
            for t in range(1, len(taps)):
                acc = acc + taps[t] * shifted(smoothed_z, t - RADIUS, 0)
            speed = step_scale * acc
            vel_ref[c, x] = speed
            if c == 0:
                backward = value - own_ref[x + RADIUS]
                forward = own_ref[x + RADIUS + 2] - value
            else:
                backward = value - shifted(value, -1, c - 1)
                forward = shifted(value, 1, c - 1) - value
            part = jnp.maximum(speed, 0.0) * backward + jnp.minimum(speed, 0.0) * forward
            change = part if change is None else change + part
        adv_ref[x] = value - change
        return carry

    lax.fori_loop(0, x_rows, out_row, 0)


def band(length, taps):
    radius = len(taps) // 2
    matrix = np.zeros((length, length), np.float32)
    for i in range(length):
        for t in range(-radius, radius + 1):
            if 0 <= i + t < length:
                matrix[i, i + t] = taps[t + radius]
    return matrix


def post_stage(drive_ext, own_ext):
    extended, y_rows, z_rows = drive_ext.shape
    x_rows = extended - 2 * RADIUS
    taps = gauss_taps(RADIUS)
    wz = jnp.asarray(band(z_rows, taps).T)
    vmem = pl.BlockSpec(memory_space=pltpu.VMEM)
    return pl.pallas_call(
        post_kernel,
        out_shape=(
            jax.ShapeDtypeStruct((3, x_rows, y_rows, z_rows), jnp.float32),
            jax.ShapeDtypeStruct((x_rows, y_rows, z_rows), jnp.float32),
        ),
        in_specs=[vmem] * 3,
        out_specs=(vmem, vmem),
        scratch_shapes=[
            pltpu.VMEM((3 * extended * y_rows, z_rows), jnp.float32),
            pltpu.VMEM((3 * x_rows * y_rows, z_rows), jnp.float32),
        ],
    )(drive_ext, own_ext, wz)


def shards(images, pairings):
    weights = gauss_taps(RADIUS)
    groups = lax.axis_size("img")
    own = images[0]
    x_rows, y_rows, _ = own.shape
    own_ext = halo_rows(own, RADIUS + 1)
    drive_ext = front_stage(own, pairings, groups)
    velocity, advected = post_stage(drive_ext, own_ext)
    return (advected[None], velocity[None])


def solution(mesh):
    return jax.shard_map(
        shards,
        mesh=mesh,
        in_specs=(P("img", "space", None, None), P()),
        out_specs=(P("img", "space", None, None), P("img", None, "space", None, None)),
        check_vma=False,
    )
```

```python
import math

import jax
import numpy as np
import jax.numpy as jnp
from jax import lax
from jax.experimental import pallas as pl
from jax.experimental.pallas import tpu as pltpu
from jax.sharding import PartitionSpec as P

RADIUS = 4
PAIRINGS = 3

gauss_sigma = 1.5
step_scale = 8.0
floor_product = 0.25
floor_variance = 0.5


def gauss_taps(radius):
    raw_taps = [
        math.exp(-(offset * offset) / (2.0 * gauss_sigma * gauss_sigma))
        for offset in range(-radius, radius + 1)
    ]
    total_weight = sum(raw_taps)
    return [raw_weight / total_weight for raw_weight in raw_taps]


def halo_rows(value, width):
    peers = lax.axis_size("space")
    up = [(i, i + 1) for i in range(peers - 1)]
    down = [(i + 1, i) for i in range(peers - 1)]
    before = lax.ppermute(value[-width:], "space", up)
    after = lax.ppermute(value[:width], "space", down)
    return jnp.concatenate([before, value, after], axis=0)


def padded_along(volume, dimension, margin):
    widths = [(0, 0)] * volume.ndim
    widths[dimension] = (margin, margin)
    return jnp.pad(volume, widths)


def window(padded, dimension, offset, length):
    return lax.slice_in_dim(padded, offset, offset + length, axis=dimension)


def central(volume, dimension):
    length = volume.shape[dimension]
    padded = padded_along(volume, dimension, 1)
    return (window(padded, dimension, 2, length) - window(padded, dimension, 0, length)) * 0.5


def smooth_along(volume, dimension, weights):
    length = volume.shape[dimension]
    padded = padded_along(volume, dimension, len(weights) // 2)
    result = weights[0] * window(padded, dimension, 0, length)
    for tap_index in range(1, len(weights)):
        result = result + weights[tap_index] * window(padded, dimension, tap_index, length)
    return result


def smooth_rows(extended, weights):
    length = extended.shape[1] - len(weights) + 1
    result = weights[0] * window(extended, 1, 0, length)
    for tap_index in range(1, len(weights)):
        result = result + weights[tap_index] * window(extended, 1, tap_index, length)
    return result


def box_rows(volume):
    sx = volume[:-2] + volume[1:-1] + volume[2:]
    last = sx.shape[1] - 1
    row = lax.broadcasted_iota(jnp.int32, sx.shape, 1)
    before = jnp.where(row >= 1, pltpu.roll(sx, 1, 1), 0.0)
    after = jnp.where(row < last, pltpu.roll(sx, last, 1), 0.0)
    return (before + sx + after) / 9.0


def pair_terms(g, pair_ref, stack_ref, mean_ref, spread_ref):
    own = stack_ref[g]
    mean_own = mean_ref[g]
    spread_own = spread_ref[g]
    center_own = own[1:-1] - mean_own
    guarded_spread = jnp.maximum(spread_own, floor_variance)
    drive_sum = None
    for pairing_row in range(PAIRINGS):
        h = pair_ref[pairing_row, g]
        partner = stack_ref[h]
        mean_partner = mean_ref[h]
        spread_partner = spread_ref[h]
        cross_term = box_rows(own * partner) - mean_own * mean_partner
        factor = 2.0 * cross_term / jnp.maximum(spread_own * spread_partner, floor_product)
        ratio_term = cross_term / guarded_spread
        pair_term = factor * (partner[1:-1] - mean_partner - ratio_term * center_own)
        drive_sum = pair_term if drive_sum is None else drive_sum + pair_term
    return drive_sum


def row_groups(first, count, rows):
    groups = []
    for r in range(first, first + count):
        owner = r // rows
        if groups and groups[-1][0] == owner:
            groups[-1][2] += 1
        else:
            groups.append([owner, r - owner * rows, 1, r - first])
    return groups


def front_kernel(
    pair_ref, own_ref, drive_ref, stack_ref, mean_ref, spread_ref, out_ref, zero_ref,
    send_a, recv_a, send_h, recv_h, send_b, recv_b, send_c, recv_c, local_sem,
):
    mesh = pl.DeviceIdType.MESH
    groups, width, y_rows, z_rows = stack_ref.shape
    rows = width - 2
    x_rows = own_ref.shape[0]
    spaces = lax.axis_size("space")
    me = lax.axis_index("img")
    s = lax.axis_index("space")
    has_lo = (s + spaces - 1) // spaces
    has_hi = (2 * spaces - 2 - s) // spaces

    barrier = pltpu.get_barrier_semaphore()
    for offset in (-1, 0, 1):
        exists = {-1: s > 0, 0: s >= 0, 1: s < spaces - 1}[offset]
        for g in range(groups):
            @pl.when(exists & ((offset != 0) | (me != g)))
            def _():
                pl.semaphore_signal(barrier, inc=1, device_id=(g, (s + offset + spaces) % spaces), device_id_type=mesh)
    pl.semaphore_wait(barrier, groups * (1 + has_lo + has_hi) - 1)

    zero_ref[...] = jnp.zeros(zero_ref.shape, jnp.float32)

    def piece(t):
        lo = max(t * rows - 1, 0)
        hi = min(t * rows + rows + 1, x_rows)
        return own_ref.at[pl.ds(lo, hi - lo)], lo - (t * rows - 1), hi - lo

    def piece_copy(t, src_image):
        src, dst_lo, count = piece(t)
        dst = stack_ref.at[src_image, pl.ds(dst_lo, count)]
        return src, dst

    def forward_copy(t_dyn, wait):
        for kind in range(3):
            cond = {0: t_dyn == 0, 1: t_dyn == groups - 1, 2: (t_dyn > 0) & (t_dyn < groups - 1)}[kind]

            @pl.when(cond & (t_dyn != me))
            def _():
                if kind == 0:
                    src, dst_lo, count = own_ref.at[pl.ds(0, rows + 1)], 1, rows + 1
                elif kind == 1:
                    src, dst_lo, count = own_ref.at[pl.ds(x_rows - rows - 1, rows + 1)], 0, rows + 1
                else:
                    src, dst_lo, count = own_ref.at[pl.ds(t_dyn * rows - 1, rows + 2)], 0, rows + 2
                copy = pltpu.make_async_remote_copy(
                    src, stack_ref.at[me, pl.ds(dst_lo, count)], send_a.at[t_dyn], recv_a.at[me],
                    device_id=(t_dyn, s), device_id_type=mesh,
                )
                if wait:
                    copy.wait_send()
                else:
                    copy.start()

    for t in range(groups):
        src, dst = piece_copy(t, me)

        @pl.when(me == t)
        def _():
            pltpu.make_async_copy(src, dst, local_sem.at[0]).start()

    for i in range(1, groups):
        forward_copy((me + i) % groups, False)

    @pl.when(s < spaces - 1)
    def _():
        pltpu.make_async_remote_copy(
            own_ref.at[pl.ds(x_rows - 1, 1)], stack_ref.at[me, pl.ds(0, 1)],
            send_h.at[0], recv_h.at[0, me], device_id=(0, (s + 1) % spaces), device_id_type=mesh,
        ).start()

    @pl.when(s > 0)
    def _():
        pltpu.make_async_remote_copy(
            own_ref.at[pl.ds(0, 1)], stack_ref.at[me, pl.ds(width - 1, 1)],
            send_h.at[1], recv_h.at[1, me], device_id=(groups - 1, (s + spaces - 1) % spaces), device_id_type=mesh,
        ).start()

    def stats(g):
        value = stack_ref[g]
        mean = box_rows(value)
        mean_ref[g] = mean
        spread_ref[g] = box_rows(value * value) - mean * mean

    @pl.when((me == 0) & (s == 0))
    def _():
        stack_ref[:, 0] = jnp.zeros((groups, y_rows, z_rows), jnp.float32)

    @pl.when((me == groups - 1) & (s == spaces - 1))
    def _():
        stack_ref[:, width - 1] = jnp.zeros((groups, y_rows, z_rows), jnp.float32)

    def arrive(i, carry):
        g = (me + groups - i) % groups

        @pl.when(i == 0)
        def _():
            for t in range(groups):
                src, dst = piece_copy(t, me)

                @pl.when(me == t)
                def _():
                    pltpu.make_async_copy(src, dst, local_sem.at[0]).wait()

        @pl.when(i != 0)
        def _():
            for t in range(groups):
                src, dst = piece_copy(t, 0)

                @pl.when(me == t)
                def _():
                    pltpu.make_async_remote_copy(
                        src, stack_ref.at[g, pl.ds(piece(t)[1], piece(t)[2])],
                        send_a.at[0], recv_a.at[g], device_id=(g, s), device_id_type=mesh,
                    ).wait_recv()

        @pl.when((me == 0) & (s > 0))
        def _():
            pltpu.make_async_remote_copy(
                own_ref.at[pl.ds(0, 1)], stack_ref.at[g, pl.ds(0, 1)],
                send_h.at[0], recv_h.at[0, g], device_id=(0, s), device_id_type=mesh,
            ).wait_recv()

        @pl.when((me == groups - 1) & (s < spaces - 1))
        def _():
            pltpu.make_async_remote_copy(
                own_ref.at[pl.ds(0, 1)], stack_ref.at[g, pl.ds(width - 1, 1)],
                send_h.at[1], recv_h.at[1, g], device_id=(0, s), device_id_type=mesh,
            ).wait_recv()

        stats(g)
        return carry

    lax.fori_loop(0, groups, arrive, 0)

    below = row_groups(x_rows - RADIUS, RADIUS, rows)
    above = row_groups(0, RADIUS, rows)

    def main_copy(g):
        src = out_ref.at[g]
        dst = drive_ref.at[pl.ds(RADIUS + me * rows, rows)]
        return src, dst

    def halo_copies(g):
        copies = []
        for index, (owner, src_lo, count, dst_lo) in enumerate(below):
            copies.append((owner, s < spaces - 1, 1, index, out_ref.at[g, pl.ds(src_lo, count)],
                           drive_ref.at[pl.ds(dst_lo, count)]))
        for index, (owner, src_lo, count, dst_lo) in enumerate(above):
            copies.append((owner, s > 0, -1, len(below) + index, out_ref.at[g, pl.ds(src_lo, count)],
                           drive_ref.at[pl.ds(x_rows + RADIUS + dst_lo, count)]))
        return copies

    def pairs(i, carry):
        g = (me + i) % groups
        out_ref[g] = pair_terms(g, pair_ref, stack_ref, mean_ref, spread_ref)
        src, dst = main_copy(g)

        @pl.when(me == g)
        def _():
            pltpu.make_async_copy(src, dst, local_sem.at[1]).start()

        @pl.when(me != g)
        def _():
            pltpu.make_async_remote_copy(
                src, dst, send_b.at[g], recv_b.at[me], device_id=(g, s), device_id_type=mesh
            ).start()

        for owner, exists, offset, index, hsrc, hdst in halo_copies(g):
            @pl.when((me == owner) & exists)
            def _():
                pltpu.make_async_remote_copy(
                    hsrc, hdst, send_c.at[index, g], recv_c.at[index],
                    device_id=(g, (s + offset + spaces) % spaces), device_id_type=mesh,
                ).start()
        return carry

    lax.fori_loop(0, groups, pairs, 0)

    @pl.when(s == 0)
    def _():
        pltpu.make_async_copy(zero_ref, drive_ref.at[pl.ds(0, RADIUS)], local_sem.at[2]).start()

    @pl.when(s == spaces - 1)
    def _():
        pltpu.make_async_copy(
            zero_ref, drive_ref.at[pl.ds(x_rows + RADIUS, RADIUS)], local_sem.at[3]
        ).start()

    for i in range(1, groups):
        forward_copy((me + i) % groups, True)

    @pl.when(s < spaces - 1)
    def _():
        pltpu.make_async_remote_copy(
            own_ref.at[pl.ds(x_rows - 1, 1)], stack_ref.at[me, pl.ds(0, 1)],
            send_h.at[0], recv_h.at[0, me], device_id=(0, (s + 1) % spaces), device_id_type=mesh,
        ).wait_send()

    @pl.when(s > 0)
    def _():
        pltpu.make_async_remote_copy(
            own_ref.at[pl.ds(0, 1)], stack_ref.at[me, pl.ds(width - 1, 1)],
            send_h.at[1], recv_h.at[1, me], device_id=(groups - 1, (s + spaces - 1) % spaces), device_id_type=mesh,
        ).wait_send()

    for g in range(groups):
        src, dst = main_copy(g)

        @pl.when(me == g)
        def _():
            pltpu.make_async_copy(src, dst, local_sem.at[1]).wait()

        @pl.when(me != g)
        def _():
            pltpu.make_async_remote_copy(
                src, dst, send_b.at[g], recv_b.at[me], device_id=(g, s), device_id_type=mesh
            ).wait_send()

        for owner, exists, offset, index, hsrc, hdst in halo_copies(g):
            @pl.when((me == owner) & exists)
            def _():
                pltpu.make_async_remote_copy(
                    hsrc, hdst, send_c.at[index, g], recv_c.at[index],
                    device_id=(g, (s + offset + spaces) % spaces), device_id_type=mesh,
                ).wait_send()

    for t in range(groups):
        @pl.when(me != t)
        def _():
            pltpu.make_async_remote_copy(
                out_ref.at[0], drive_ref.at[pl.ds(RADIUS + t * rows, rows)],
                send_b.at[0], recv_b.at[t], device_id=(t, s), device_id_type=mesh,
            ).wait_recv()

    for owner, exists, offset, index, hsrc, hdst in halo_copies(0):
        @pl.when(((offset == 1) & (s > 0)) | ((offset == -1) & (s < spaces - 1)))
        def _():
            pltpu.make_async_remote_copy(
                hsrc, hdst, send_c.at[index, 0], recv_c.at[index],
                device_id=(owner, s), device_id_type=mesh,
            ).wait_recv()

    @pl.when(s == 0)
    def _():
        pltpu.make_async_copy(zero_ref, drive_ref.at[pl.ds(0, RADIUS)], local_sem.at[2]).wait()

    @pl.when(s == spaces - 1)
    def _():
        pltpu.make_async_copy(
            zero_ref, drive_ref.at[pl.ds(x_rows + RADIUS, RADIUS)], local_sem.at[3]
        ).wait()


def front_stage(own, pairings, groups):
    x_rows, y_rows, z_rows = own.shape
    rows = x_rows // groups
    shape = (groups, rows, y_rows, z_rows)
    halos = len(row_groups(x_rows - RADIUS, RADIUS, rows)) + len(row_groups(0, RADIUS, rows))
    dma = pltpu.SemaphoreType.DMA
    return pl.pallas_call(
        front_kernel,
        out_shape=jax.ShapeDtypeStruct((x_rows + 2 * RADIUS, y_rows, z_rows), jnp.float32),
        in_specs=[
            pl.BlockSpec(memory_space=pltpu.SMEM),
            pl.BlockSpec(memory_space=pltpu.VMEM),
        ],
        out_specs=pl.BlockSpec(memory_space=pl.ANY),
        scratch_shapes=[
            pltpu.VMEM((groups, rows + 2, y_rows, z_rows), jnp.float32),
            pltpu.VMEM(shape, jnp.float32),
            pltpu.VMEM(shape, jnp.float32),
            pltpu.VMEM(shape, jnp.float32),
            pltpu.VMEM((RADIUS, y_rows, z_rows), jnp.float32),
            dma((groups,)),
            dma((groups,)),
            dma((2,)),
            dma((2, groups)),
            dma((groups,)),
            dma((groups,)),
            dma((halos, groups)),
            dma((halos,)),
            dma((4,)),
        ],
        compiler_params=pltpu.CompilerParams(collective_id=0, has_side_effects=True),
    )(pairings, own)


def shifted(value, offset, axis):
    length = value.shape[axis]
    rolled = pltpu.roll(value, (-offset) % length, axis)
    index = lax.broadcasted_iota(jnp.int32, value.shape, axis) + offset
    return jnp.where((index >= 0) & (index < length), rolled, 0.0)


PAD = 8


def post_kernel(drive_ref, own_ref, wz_ref, vel_ref, adv_ref, own_pad, force_ref, pass_ref):
    extended, y_rows, z_rows = drive_ref.shape
    x_rows = vel_ref.shape[1]
    padded = y_rows + 2 * PAD
    taps = gauss_taps(RADIUS)
    zeros = jnp.zeros((PAD, z_rows), jnp.float32)

    def inner(r, offset=0):
        return (r, pl.ds(PAD + offset, y_rows))

    def fill(r, carry):
        own_pad[r, pl.ds(0, PAD)] = zeros
        own_pad[r, pl.ds(PAD + y_rows, PAD)] = zeros
        own_pad[inner(r)] = own_ref[r]
        return carry

    lax.fori_loop(0, own_ref.shape[0], fill, 0)

    def plane(c, r, count):
        return pl.ds(pl.multiple_of((c * count + r) * y_rows, 8), y_rows)

    def force_row(r, carry):
        value = own_pad[inner(r + 1)]
        drive = drive_ref[r]
        force_ref[plane(0, r, extended)] = drive * ((own_pad[inner(r + 2)] - own_pad[inner(r)]) * 0.5)
        force_ref[plane(1, r, extended)] = drive * (
            (own_pad[inner(r + 1, 1)] - own_pad[inner(r + 1, -1)]) * 0.5
        )
        force_ref[plane(2, r, extended)] = drive * (
            (shifted(value, 1, 1) - shifted(value, -1, 1)) * 0.5
        )
        return carry

    lax.fori_loop(0, extended, force_row, 0)

    def slot(c, x):
        return pl.multiple_of((c * x_rows + x) * padded, 8)

    def x_pass(x, carry):
        for c in range(3):
            acc = taps[0] * force_ref[plane(c, x, extended)]
            for t in range(1, len(taps)):
                acc = acc + taps[t] * force_ref[plane(c, x + t, extended)]
            base = slot(c, x)
            pass_ref[pl.ds(base, PAD)] = zeros
            pass_ref[pl.ds(base + PAD, y_rows)] = acc
            pass_ref[pl.ds(base + PAD + y_rows, PAD)] = zeros
        return carry

    lax.fori_loop(0, x_rows, x_pass, 0)
    wz = wz_ref[...]
    chunk = 8 * padded
    chunks = pass_ref.shape[0] // chunk

    def z_pass(i, carry):
        rows = pl.ds(pl.multiple_of(i * chunk, 8), chunk)
        pass_ref[rows] = jnp.dot(
            pass_ref[rows], wz, precision=lax.Precision.HIGHEST,
            preferred_element_type=jnp.float32,
        )
        return carry

    lax.fori_loop(0, chunks, z_pass, 0)

    def out_row(x, carry):
        r = x + RADIUS + 1
        value = own_pad[inner(r)]
        change = None
        for c in range(3):
            base = slot(c, x) + PAD - RADIUS
            acc = taps[0] * pass_ref[pl.ds(base, y_rows)]
            for t in range(1, len(taps)):
                acc = acc + taps[t] * pass_ref[pl.ds(base + t, y_rows)]
            speed = step_scale * acc
            vel_ref[c, x] = speed
            if c == 0:
                backward = value - own_pad[inner(r - 1)]
                forward = own_pad[inner(r + 1)] - value
            elif c == 1:
                backward = value - own_pad[inner(r, -1)]
                forward = own_pad[inner(r, 1)] - value
            else:
                backward = value - shifted(value, -1, 1)
                forward = shifted(value, 1, 1) - value
            part = jnp.maximum(speed, 0.0) * backward + jnp.minimum(speed, 0.0) * forward
            change = part if change is None else change + part
        adv_ref[x] = value - change
        return carry

    lax.fori_loop(0, x_rows, out_row, 0)


def band(length, taps):
    radius = len(taps) // 2
    matrix = np.zeros((length, length), np.float32)
    for i in range(length):
        for t in range(-radius, radius + 1):
            if 0 <= i + t < length:
                matrix[i, i + t] = taps[t + radius]
    return matrix


def post_stage(drive_ext, own_ext):
    extended, y_rows, z_rows = drive_ext.shape
    x_rows = extended - 2 * RADIUS
    taps = gauss_taps(RADIUS)
    wz = jnp.asarray(band(z_rows, taps).T)
    vmem = pl.BlockSpec(memory_space=pltpu.VMEM)
    return pl.pallas_call(
        post_kernel,
        out_shape=(
            jax.ShapeDtypeStruct((3, x_rows, y_rows, z_rows), jnp.float32),
            jax.ShapeDtypeStruct((x_rows, y_rows, z_rows), jnp.float32),
        ),
        in_specs=[vmem] * 3,
        out_specs=(vmem, vmem),
        scratch_shapes=[
            pltpu.VMEM((extended + 2, y_rows + 2 * PAD, z_rows), jnp.float32),
            pltpu.VMEM((3 * extended * y_rows, z_rows), jnp.float32),
            pltpu.VMEM((3 * x_rows * (y_rows + 2 * PAD), z_rows), jnp.float32),
        ],
    )(drive_ext, own_ext, wz)


def shards(images, pairings):
    weights = gauss_taps(RADIUS)
    groups = lax.axis_size("img")
    own = images[0]
    x_rows, y_rows, _ = own.shape
    own_ext = halo_rows(own, RADIUS + 1)
    drive_ext = front_stage(own, pairings, groups)
    velocity, advected = post_stage(drive_ext, own_ext)
    return (advected[None], velocity[None])


def solution(mesh):
    return jax.shard_map(
        shards,
        mesh=mesh,
        in_specs=(P("img", "space", None, None), P()),
        out_specs=(P("img", "space", None, None), P("img", None, "space", None, None)),
        check_vma=False,
    )
```

```python
import math

import jax
import numpy as np
import jax.numpy as jnp
from jax import lax
from jax.experimental import pallas as pl
from jax.experimental.pallas import tpu as pltpu
from jax.sharding import PartitionSpec as P

RADIUS = 4
PAIRINGS = 3

gauss_sigma = 1.5
step_scale = 8.0
floor_product = 0.25
floor_variance = 0.5


def gauss_taps(radius):
    raw_taps = [
        math.exp(-(offset * offset) / (2.0 * gauss_sigma * gauss_sigma))
        for offset in range(-radius, radius + 1)
    ]
    total_weight = sum(raw_taps)
    return [raw_weight / total_weight for raw_weight in raw_taps]


def halo_rows(value, width):
    peers = lax.axis_size("space")
    up = [(i, i + 1) for i in range(peers - 1)]
    down = [(i + 1, i) for i in range(peers - 1)]
    before = lax.ppermute(value[-width:], "space", up)
    after = lax.ppermute(value[:width], "space", down)
    return jnp.concatenate([before, value, after], axis=0)


def padded_along(volume, dimension, margin):
    widths = [(0, 0)] * volume.ndim
    widths[dimension] = (margin, margin)
    return jnp.pad(volume, widths)


def window(padded, dimension, offset, length):
    return lax.slice_in_dim(padded, offset, offset + length, axis=dimension)


def central(volume, dimension):
    length = volume.shape[dimension]
    padded = padded_along(volume, dimension, 1)
    return (window(padded, dimension, 2, length) - window(padded, dimension, 0, length)) * 0.5


def smooth_along(volume, dimension, weights):
    length = volume.shape[dimension]
    padded = padded_along(volume, dimension, len(weights) // 2)
    result = weights[0] * window(padded, dimension, 0, length)
    for tap_index in range(1, len(weights)):
        result = result + weights[tap_index] * window(padded, dimension, tap_index, length)
    return result


def smooth_rows(extended, weights):
    length = extended.shape[1] - len(weights) + 1
    result = weights[0] * window(extended, 1, 0, length)
    for tap_index in range(1, len(weights)):
        result = result + weights[tap_index] * window(extended, 1, tap_index, length)
    return result


def box_rows(volume):
    sx = volume[:-2] + volume[1:-1] + volume[2:]
    last = sx.shape[1] - 1
    row = lax.broadcasted_iota(jnp.int32, sx.shape, 1)
    before = jnp.where(row >= 1, pltpu.roll(sx, 1, 1), 0.0)
    after = jnp.where(row < last, pltpu.roll(sx, last, 1), 0.0)
    return (before + sx + after) / 9.0


def pair_terms(g, pair_ref, stack_ref, mean_ref, spread_ref):
    own = stack_ref[g]
    mean_own = mean_ref[g]
    spread_own = spread_ref[g]
    center_own = own[1:-1] - mean_own
    guarded_spread = jnp.maximum(spread_own, floor_variance)
    drive_sum = None
    for pairing_row in range(PAIRINGS):
        h = pair_ref[pairing_row, g]
        partner = stack_ref[h]
        mean_partner = mean_ref[h]
        spread_partner = spread_ref[h]
        cross_term = box_rows(own * partner) - mean_own * mean_partner
        factor = 2.0 * cross_term / jnp.maximum(spread_own * spread_partner, floor_product)
        ratio_term = cross_term / guarded_spread
        pair_term = factor * (partner[1:-1] - mean_partner - ratio_term * center_own)
        drive_sum = pair_term if drive_sum is None else drive_sum + pair_term
    return drive_sum


def row_groups(first, count, rows):
    groups = []
    for r in range(first, first + count):
        owner = r // rows
        if groups and groups[-1][0] == owner:
            groups[-1][2] += 1
        else:
            groups.append([owner, r - owner * rows, 1, r - first])
    return groups


def front_kernel(
    pair_ref, own_ref, drive_ref, stack_ref, mean_ref, spread_ref, out_ref, zero_ref,
    send_a, recv_a, send_h, recv_h, send_b, recv_b, send_c, recv_c, local_sem,
):
    mesh = pl.DeviceIdType.MESH
    groups, width, y_rows, z_rows = stack_ref.shape
    rows = width - 2
    x_rows = own_ref.shape[0]
    spaces = lax.axis_size("space")
    me = lax.axis_index("img")
    s = lax.axis_index("space")
    has_lo = (s + spaces - 1) // spaces
    has_hi = (2 * spaces - 2 - s) // spaces

    barrier = pltpu.get_barrier_semaphore()
    for offset in (-1, 0, 1):
        exists = {-1: s > 0, 0: s >= 0, 1: s < spaces - 1}[offset]
        for g in range(groups):
            @pl.when(exists & ((offset != 0) | (me != g)))
            def _():
                pl.semaphore_signal(barrier, inc=1, device_id=(g, (s + offset + spaces) % spaces), device_id_type=mesh)
    pl.semaphore_wait(barrier, groups * (1 + has_lo + has_hi) - 1)

    zero_ref[...] = jnp.zeros(zero_ref.shape, jnp.float32)

    def piece(t):
        lo = max(t * rows - 1, 0)
        hi = min(t * rows + rows + 1, x_rows)
        return own_ref.at[pl.ds(lo, hi - lo)], lo - (t * rows - 1), hi - lo

    def piece_copy(t, src_image):
        src, dst_lo, count = piece(t)
        dst = stack_ref.at[src_image, pl.ds(dst_lo, count)]
        return src, dst

    def forward_copy(t_dyn, wait):
        for kind in range(3):
            cond = {0: t_dyn == 0, 1: t_dyn == groups - 1, 2: (t_dyn > 0) & (t_dyn < groups - 1)}[kind]

            @pl.when(cond & (t_dyn != me))
            def _():
                if kind == 0:
                    src, dst_lo, count = own_ref.at[pl.ds(0, rows + 1)], 1, rows + 1
                elif kind == 1:
                    src, dst_lo, count = own_ref.at[pl.ds(x_rows - rows - 1, rows + 1)], 0, rows + 1
                else:
                    src, dst_lo, count = own_ref.at[pl.ds(t_dyn * rows - 1, rows + 2)], 0, rows + 2
                copy = pltpu.make_async_remote_copy(
                    src, stack_ref.at[me, pl.ds(dst_lo, count)], send_a.at[t_dyn], recv_a.at[me],
                    device_id=(t_dyn, s), device_id_type=mesh,
                )
                if wait:
                    copy.wait_send()
                else:
                    copy.start()

    for t in range(groups):
        src, dst = piece_copy(t, me)

        @pl.when(me == t)
        def _():
            pltpu.make_async_copy(src, dst, local_sem.at[0]).start()

    for i in range(1, groups):
        forward_copy((me + i) % groups, False)

    @pl.when(s < spaces - 1)
    def _():
        pltpu.make_async_remote_copy(
            own_ref.at[pl.ds(x_rows - 1, 1)], stack_ref.at[me, pl.ds(0, 1)],
            send_h.at[0], recv_h.at[0, me], device_id=(0, (s + 1) % spaces), device_id_type=mesh,
        ).start()

    @pl.when(s > 0)
    def _():
        pltpu.make_async_remote_copy(
            own_ref.at[pl.ds(0, 1)], stack_ref.at[me, pl.ds(width - 1, 1)],
            send_h.at[1], recv_h.at[1, me], device_id=(groups - 1, (s + spaces - 1) % spaces), device_id_type=mesh,
        ).start()

    def stats(g):
        value = stack_ref[g]
        mean = box_rows(value)
        mean_ref[g] = mean
        spread_ref[g] = box_rows(value * value) - mean * mean

    @pl.when((me == 0) & (s == 0))
    def _():
        stack_ref[:, 0] = jnp.zeros((groups, y_rows, z_rows), jnp.float32)

    @pl.when((me == groups - 1) & (s == spaces - 1))
    def _():
        stack_ref[:, width - 1] = jnp.zeros((groups, y_rows, z_rows), jnp.float32)

    def arrive(i, carry):
        g = (me + groups - i) % groups

        @pl.when(i == 0)
        def _():
            for t in range(groups):
                src, dst = piece_copy(t, me)

                @pl.when(me == t)
                def _():
                    pltpu.make_async_copy(src, dst, local_sem.at[0]).wait()

        @pl.when(i != 0)
        def _():
            for t in range(groups):
                src, dst = piece_copy(t, 0)

                @pl.when(me == t)
                def _():
                    pltpu.make_async_remote_copy(
                        src, stack_ref.at[g, pl.ds(piece(t)[1], piece(t)[2])],
                        send_a.at[0], recv_a.at[g], device_id=(g, s), device_id_type=mesh,
                    ).wait_recv()

        @pl.when((me == 0) & (s > 0))
        def _():
            pltpu.make_async_remote_copy(
                own_ref.at[pl.ds(0, 1)], stack_ref.at[g, pl.ds(0, 1)],
                send_h.at[0], recv_h.at[0, g], device_id=(0, s), device_id_type=mesh,
            ).wait_recv()

        @pl.when((me == groups - 1) & (s < spaces - 1))
        def _():
            pltpu.make_async_remote_copy(
                own_ref.at[pl.ds(0, 1)], stack_ref.at[g, pl.ds(width - 1, 1)],
                send_h.at[1], recv_h.at[1, g], device_id=(0, s), device_id_type=mesh,
            ).wait_recv()

        stats(g)
        return carry

    lax.fori_loop(0, groups, arrive, 0)

    below = row_groups(x_rows - RADIUS, RADIUS, rows)
    above = row_groups(0, RADIUS, rows)

    def main_copy(g):
        src = out_ref.at[g]
        dst = drive_ref.at[pl.ds(RADIUS + me * rows, rows)]
        return src, dst

    def halo_copies(g):
        copies = []
        for index, (owner, src_lo, count, dst_lo) in enumerate(below):
            copies.append((owner, s < spaces - 1, 1, index, out_ref.at[g, pl.ds(src_lo, count)],
                           drive_ref.at[pl.ds(dst_lo, count)]))
        for index, (owner, src_lo, count, dst_lo) in enumerate(above):
            copies.append((owner, s > 0, -1, len(below) + index, out_ref.at[g, pl.ds(src_lo, count)],
                           drive_ref.at[pl.ds(x_rows + RADIUS + dst_lo, count)]))
        return copies

    def pairs(i, carry):
        g = (me + i) % groups
        out_ref[g] = pair_terms(g, pair_ref, stack_ref, mean_ref, spread_ref)
        src, dst = main_copy(g)

        @pl.when(me == g)
        def _():
            pltpu.make_async_copy(src, dst, local_sem.at[1]).start()

        @pl.when(me != g)
        def _():
            pltpu.make_async_remote_copy(
                src, dst, send_b.at[g], recv_b.at[me], device_id=(g, s), device_id_type=mesh
            ).start()

        for owner, exists, offset, index, hsrc, hdst in halo_copies(g):
            @pl.when((me == owner) & exists)
            def _():
                pltpu.make_async_remote_copy(
                    hsrc, hdst, send_c.at[index, g], recv_c.at[index],
                    device_id=(g, (s + offset + spaces) % spaces), device_id_type=mesh,
                ).start()
        return carry

    lax.fori_loop(0, groups, pairs, 0)

    @pl.when(s == 0)
    def _():
        pltpu.make_async_copy(zero_ref, drive_ref.at[pl.ds(0, RADIUS)], local_sem.at[2]).start()

    @pl.when(s == spaces - 1)
    def _():
        pltpu.make_async_copy(
            zero_ref, drive_ref.at[pl.ds(x_rows + RADIUS, RADIUS)], local_sem.at[3]
        ).start()

    for i in range(1, groups):
        forward_copy((me + i) % groups, True)

    @pl.when(s < spaces - 1)
    def _():
        pltpu.make_async_remote_copy(
            own_ref.at[pl.ds(x_rows - 1, 1)], stack_ref.at[me, pl.ds(0, 1)],
            send_h.at[0], recv_h.at[0, me], device_id=(0, (s + 1) % spaces), device_id_type=mesh,
        ).wait_send()

    @pl.when(s > 0)
    def _():
        pltpu.make_async_remote_copy(
            own_ref.at[pl.ds(0, 1)], stack_ref.at[me, pl.ds(width - 1, 1)],
            send_h.at[1], recv_h.at[1, me], device_id=(groups - 1, (s + spaces - 1) % spaces), device_id_type=mesh,
        ).wait_send()

    for g in range(groups):
        src, dst = main_copy(g)

        @pl.when(me == g)
        def _():
            pltpu.make_async_copy(src, dst, local_sem.at[1]).wait()

        @pl.when(me != g)
        def _():
            pltpu.make_async_remote_copy(
                src, dst, send_b.at[g], recv_b.at[me], device_id=(g, s), device_id_type=mesh
            ).wait_send()

        for owner, exists, offset, index, hsrc, hdst in halo_copies(g):
            @pl.when((me == owner) & exists)
            def _():
                pltpu.make_async_remote_copy(
                    hsrc, hdst, send_c.at[index, g], recv_c.at[index],
                    device_id=(g, (s + offset + spaces) % spaces), device_id_type=mesh,
                ).wait_send()

    for t in range(groups):
        @pl.when(me != t)
        def _():
            pltpu.make_async_remote_copy(
                out_ref.at[0], drive_ref.at[pl.ds(RADIUS + t * rows, rows)],
                send_b.at[0], recv_b.at[t], device_id=(t, s), device_id_type=mesh,
            ).wait_recv()

    for owner, exists, offset, index, hsrc, hdst in halo_copies(0):
        @pl.when(((offset == 1) & (s > 0)) | ((offset == -1) & (s < spaces - 1)))
        def _():
            pltpu.make_async_remote_copy(
                hsrc, hdst, send_c.at[index, 0], recv_c.at[index],
                device_id=(owner, s), device_id_type=mesh,
            ).wait_recv()

    @pl.when(s == 0)
    def _():
        pltpu.make_async_copy(zero_ref, drive_ref.at[pl.ds(0, RADIUS)], local_sem.at[2]).wait()

    @pl.when(s == spaces - 1)
    def _():
        pltpu.make_async_copy(
            zero_ref, drive_ref.at[pl.ds(x_rows + RADIUS, RADIUS)], local_sem.at[3]
        ).wait()


def front_stage(own, pairings, groups):
    x_rows, y_rows, z_rows = own.shape
    rows = x_rows // groups
    shape = (groups, rows, y_rows, z_rows)
    halos = len(row_groups(x_rows - RADIUS, RADIUS, rows)) + len(row_groups(0, RADIUS, rows))
    dma = pltpu.SemaphoreType.DMA
    return pl.pallas_call(
        front_kernel,
        out_shape=jax.ShapeDtypeStruct((x_rows + 2 * RADIUS, y_rows, z_rows), jnp.float32),
        in_specs=[
            pl.BlockSpec(memory_space=pltpu.SMEM),
            pl.BlockSpec(memory_space=pltpu.VMEM),
        ],
        out_specs=pl.BlockSpec(memory_space=pl.ANY),
        scratch_shapes=[
            pltpu.VMEM((groups, rows + 2, y_rows, z_rows), jnp.float32),
            pltpu.VMEM(shape, jnp.float32),
            pltpu.VMEM(shape, jnp.float32),
            pltpu.VMEM(shape, jnp.float32),
            pltpu.VMEM((RADIUS, y_rows, z_rows), jnp.float32),
            dma((groups,)),
            dma((groups,)),
            dma((2,)),
            dma((2, groups)),
            dma((groups,)),
            dma((groups,)),
            dma((halos, groups)),
            dma((halos,)),
            dma((4,)),
        ],
        compiler_params=pltpu.CompilerParams(collective_id=0, has_side_effects=True),
    )(pairings, own)


def shifted(value, offset, axis):
    length = value.shape[axis]
    rolled = pltpu.roll(value, (-offset) % length, axis)
    index = lax.broadcasted_iota(jnp.int32, value.shape, axis) + offset
    return jnp.where((index >= 0) & (index < length), rolled, 0.0)


PAD = 8


def post_kernel(drive_ref, own_ref, wz_ref, vel_ref, adv_ref, own_pad, force_ref, pass_ref):
    extended, y_rows, z_rows = drive_ref.shape
    x_rows = vel_ref.shape[1]
    padded = y_rows + 2 * PAD
    taps = gauss_taps(RADIUS)
    zeros = jnp.zeros((PAD, z_rows), jnp.float32)

    def inner(r, offset=0):
        return (r, pl.ds(PAD + offset, y_rows))

    def fill(r, carry):
        own_pad[r, pl.ds(0, PAD)] = zeros
        own_pad[r, pl.ds(PAD + y_rows, PAD)] = zeros
        own_pad[inner(r)] = own_ref[r]
        return carry

    lax.fori_loop(0, own_ref.shape[0], fill, 0)

    def plane(c, r, count):
        return pl.ds(pl.multiple_of((c * count + r) * y_rows, 8), y_rows)

    def force_row(r, carry):
        value = own_pad[inner(r + 1)]
        drive = drive_ref[r]
        force_ref[plane(0, r, extended)] = drive * ((own_pad[inner(r + 2)] - own_pad[inner(r)]) * 0.5)
        force_ref[plane(1, r, extended)] = drive * (
            (own_pad[inner(r + 1, 1)] - own_pad[inner(r + 1, -1)]) * 0.5
        )
        force_ref[plane(2, r, extended)] = drive * (
            (shifted(value, 1, 1) - shifted(value, -1, 1)) * 0.5
        )
        return carry

    lax.fori_loop(0, extended, force_row, 0)

    def slot(c, x):
        return pl.multiple_of((c * x_rows + x) * padded, 8)

    def x_pass(x, carry):
        for c in range(3):
            acc = taps[0] * force_ref[plane(c, x, extended)]
            for t in range(1, len(taps)):
                acc = acc + taps[t] * force_ref[plane(c, x + t, extended)]
            base = slot(c, x)
            pass_ref[pl.ds(base, PAD)] = zeros
            pass_ref[pl.ds(base + PAD, y_rows)] = acc
            pass_ref[pl.ds(base + PAD + y_rows, PAD)] = zeros
        return carry

    lax.fori_loop(0, x_rows, x_pass, 0)
    wz = wz_ref[...]
    chunk = 8 * padded
    chunks = pass_ref.shape[0] // chunk

    def z_pass(i, carry):
        rows = pl.ds(pl.multiple_of(i * chunk, 8), chunk)
        pass_ref[rows] = jnp.dot(
            pass_ref[rows], wz, precision=lax.Precision.HIGH,
            preferred_element_type=jnp.float32,
        )
        return carry

    lax.fori_loop(0, chunks, z_pass, 0)

    def out_row(x, carry):
        r = x + RADIUS + 1
        value = own_pad[inner(r)]
        change = None
        for c in range(3):
            base = slot(c, x) + PAD - RADIUS
            acc = taps[0] * pass_ref[pl.ds(base, y_rows)]
            for t in range(1, len(taps)):
                acc = acc + taps[t] * pass_ref[pl.ds(base + t, y_rows)]
            speed = step_scale * acc
            vel_ref[c, x] = speed
            if c == 0:
                backward = value - own_pad[inner(r - 1)]
                forward = own_pad[inner(r + 1)] - value
            elif c == 1:
                backward = value - own_pad[inner(r, -1)]
                forward = own_pad[inner(r, 1)] - value
            else:
                backward = value - shifted(value, -1, 1)
                forward = shifted(value, 1, 1) - value
            part = jnp.maximum(speed, 0.0) * backward + jnp.minimum(speed, 0.0) * forward
            change = part if change is None else change + part
        adv_ref[x] = value - change
        return carry

    lax.fori_loop(0, x_rows, out_row, 0)


def band(length, taps):
    radius = len(taps) // 2
    matrix = np.zeros((length, length), np.float32)
    for i in range(length):
        for t in range(-radius, radius + 1):
            if 0 <= i + t < length:
                matrix[i, i + t] = taps[t + radius]
    return matrix


def post_stage(drive_ext, own_ext):
    extended, y_rows, z_rows = drive_ext.shape
    x_rows = extended - 2 * RADIUS
    taps = gauss_taps(RADIUS)
    wz = jnp.asarray(band(z_rows, taps).T)
    vmem = pl.BlockSpec(memory_space=pltpu.VMEM)
    return pl.pallas_call(
        post_kernel,
        out_shape=(
            jax.ShapeDtypeStruct((3, x_rows, y_rows, z_rows), jnp.float32),
            jax.ShapeDtypeStruct((x_rows, y_rows, z_rows), jnp.float32),
        ),
        in_specs=[vmem] * 3,
        out_specs=(vmem, vmem),
        scratch_shapes=[
            pltpu.VMEM((extended + 2, y_rows + 2 * PAD, z_rows), jnp.float32),
            pltpu.VMEM((3 * extended * y_rows, z_rows), jnp.float32),
            pltpu.VMEM((3 * x_rows * (y_rows + 2 * PAD), z_rows), jnp.float32),
        ],
    )(drive_ext, own_ext, wz)


def shards(images, pairings):
    weights = gauss_taps(RADIUS)
    groups = lax.axis_size("img")
    own = images[0]
    x_rows, y_rows, _ = own.shape
    own_ext = halo_rows(own, RADIUS + 1)
    drive_ext = front_stage(own, pairings, groups)
    velocity, advected = post_stage(drive_ext, own_ext)
    return (advected[None], velocity[None])


def solution(mesh):
    return jax.shard_map(
        shards,
        mesh=mesh,
        in_specs=(P("img", "space", None, None), P()),
        out_specs=(P("img", "space", None, None), P("img", None, "space", None, None)),
        check_vma=False,
    )
```

```python
import math

import jax
import numpy as np
import jax.numpy as jnp
from jax import lax
from jax.experimental import pallas as pl
from jax.experimental.pallas import tpu as pltpu
from jax.sharding import PartitionSpec as P

RADIUS = 4
PAIRINGS = 3

gauss_sigma = 1.5
step_scale = 8.0
floor_product = 0.25
floor_variance = 0.5


def gauss_taps(radius):
    raw_taps = [
        math.exp(-(offset * offset) / (2.0 * gauss_sigma * gauss_sigma))
        for offset in range(-radius, radius + 1)
    ]
    total_weight = sum(raw_taps)
    return [raw_weight / total_weight for raw_weight in raw_taps]


def halo_rows(value, width):
    peers = lax.axis_size("space")
    up = [(i, i + 1) for i in range(peers - 1)]
    down = [(i + 1, i) for i in range(peers - 1)]
    before = lax.ppermute(value[-width:], "space", up)
    after = lax.ppermute(value[:width], "space", down)
    return jnp.concatenate([before, value, after], axis=0)


def padded_along(volume, dimension, margin):
    widths = [(0, 0)] * volume.ndim
    widths[dimension] = (margin, margin)
    return jnp.pad(volume, widths)


def window(padded, dimension, offset, length):
    return lax.slice_in_dim(padded, offset, offset + length, axis=dimension)


def central(volume, dimension):
    length = volume.shape[dimension]
    padded = padded_along(volume, dimension, 1)
    return (window(padded, dimension, 2, length) - window(padded, dimension, 0, length)) * 0.5


def smooth_along(volume, dimension, weights):
    length = volume.shape[dimension]
    padded = padded_along(volume, dimension, len(weights) // 2)
    result = weights[0] * window(padded, dimension, 0, length)
    for tap_index in range(1, len(weights)):
        result = result + weights[tap_index] * window(padded, dimension, tap_index, length)
    return result


def smooth_rows(extended, weights):
    length = extended.shape[1] - len(weights) + 1
    result = weights[0] * window(extended, 1, 0, length)
    for tap_index in range(1, len(weights)):
        result = result + weights[tap_index] * window(extended, 1, tap_index, length)
    return result


def box_rows(volume):
    sx = volume[:-2] + volume[1:-1] + volume[2:]
    last = sx.shape[1] - 1
    row = lax.broadcasted_iota(jnp.int32, sx.shape, 1)
    before = jnp.where(row >= 1, pltpu.roll(sx, 1, 1), 0.0)
    after = jnp.where(row < last, pltpu.roll(sx, last, 1), 0.0)
    return (before + sx + after) / 9.0


def pair_terms(g, pair_ref, stack_ref, mean_ref, spread_ref):
    own = stack_ref[g]
    mean_own = mean_ref[g]
    spread_own = spread_ref[g]
    center_own = own[1:-1] - mean_own
    guarded_spread = jnp.maximum(spread_own, floor_variance)
    drive_sum = None
    for pairing_row in range(PAIRINGS):
        h = pair_ref[pairing_row, g]
        partner = stack_ref[h]
        mean_partner = mean_ref[h]
        spread_partner = spread_ref[h]
        cross_term = box_rows(own * partner) - mean_own * mean_partner
        factor = 2.0 * cross_term / jnp.maximum(spread_own * spread_partner, floor_product)
        ratio_term = cross_term / guarded_spread
        pair_term = factor * (partner[1:-1] - mean_partner - ratio_term * center_own)
        drive_sum = pair_term if drive_sum is None else drive_sum + pair_term
    return drive_sum


def row_groups(first, count, rows):
    groups = []
    for r in range(first, first + count):
        owner = r // rows
        if groups and groups[-1][0] == owner:
            groups[-1][2] += 1
        else:
            groups.append([owner, r - owner * rows, 1, r - first])
    return groups


def front_kernel(
    pair_ref, own_ref, drive_ref, ext_ref, stack_ref, mean_ref, spread_ref, out_ref, zero_ref,
    send_a, recv_a, send_h, recv_h, send_b, recv_b, send_c, recv_c, local_sem, send_o, recv_o,
):
    mesh = pl.DeviceIdType.MESH
    groups, width, y_rows, z_rows = stack_ref.shape
    rows = width - 2
    x_rows = own_ref.shape[0]
    spaces = lax.axis_size("space")
    me = lax.axis_index("img")
    s = lax.axis_index("space")
    has_lo = (s + spaces - 1) // spaces
    has_hi = (2 * spaces - 2 - s) // spaces

    barrier = pltpu.get_barrier_semaphore()
    for offset in (-1, 0, 1):
        exists = {-1: s > 0, 0: s >= 0, 1: s < spaces - 1}[offset]
        for g in range(groups):
            @pl.when(exists & ((offset != 0) | (me != g)))
            def _():
                pl.semaphore_signal(barrier, inc=1, device_id=(g, (s + offset + spaces) % spaces), device_id_type=mesh)
    pl.semaphore_wait(barrier, groups * (1 + has_lo + has_hi) - 1)

    zero_ref[...] = jnp.zeros(zero_ref.shape, jnp.float32)
    margin = RADIUS + 1

    def own_halo(wait):
        copies = [
            (s < spaces - 1, own_ref.at[pl.ds(x_rows - margin, margin)], ext_ref.at[pl.ds(0, margin)],
             0, (s + 1) % spaces),
            (s > 0, own_ref.at[pl.ds(0, margin)], ext_ref.at[pl.ds(x_rows + margin, margin)],
             1, (s + spaces - 1) % spaces),
        ]
        for exists, src, dst, index, target in copies:
            @pl.when(exists)
            def _():
                copy = pltpu.make_async_remote_copy(
                    src, dst, send_o.at[index], recv_o.at[index],
                    device_id=(me, target), device_id_type=mesh,
                )
                if wait:
                    copy.wait_send()
                else:
                    copy.start()
        local = [
            (s >= 0, own_ref, ext_ref.at[pl.ds(margin, x_rows)], 2),
            (s == 0, zero_ref, ext_ref.at[pl.ds(0, margin)], 3),
            (s == spaces - 1, zero_ref, ext_ref.at[pl.ds(x_rows + margin, margin)], 4),
        ]
        for exists, src, dst, index in local:
            @pl.when(exists)
            def _():
                copy = pltpu.make_async_copy(src, dst, local_sem.at[index])
                if wait:
                    copy.wait()
                else:
                    copy.start()

    own_halo(False)

    def piece(t):
        lo = max(t * rows - 1, 0)
        hi = min(t * rows + rows + 1, x_rows)
        return own_ref.at[pl.ds(lo, hi - lo)], lo - (t * rows - 1), hi - lo

    def piece_copy(t, src_image):
        src, dst_lo, count = piece(t)
        dst = stack_ref.at[src_image, pl.ds(dst_lo, count)]
        return src, dst

    def forward_copy(t_dyn, wait):
        for kind in range(3):
            cond = {0: t_dyn == 0, 1: t_dyn == groups - 1, 2: (t_dyn > 0) & (t_dyn < groups - 1)}[kind]

            @pl.when(cond & (t_dyn != me))
            def _():
                if kind == 0:
                    src, dst_lo, count = own_ref.at[pl.ds(0, rows + 1)], 1, rows + 1
                elif kind == 1:
                    src, dst_lo, count = own_ref.at[pl.ds(x_rows - rows - 1, rows + 1)], 0, rows + 1
                else:
                    src, dst_lo, count = own_ref.at[pl.ds(t_dyn * rows - 1, rows + 2)], 0, rows + 2
                copy = pltpu.make_async_remote_copy(
                    src, stack_ref.at[me, pl.ds(dst_lo, count)], send_a.at[t_dyn], recv_a.at[me],
                    device_id=(t_dyn, s), device_id_type=mesh,
                )
                if wait:
                    copy.wait_send()
                else:
                    copy.start()

    for t in range(groups):
        src, dst = piece_copy(t, me)

        @pl.when(me == t)
        def _():
            pltpu.make_async_copy(src, dst, local_sem.at[0]).start()

    for i in range(1, groups):
        forward_copy((me + i) % groups, False)

    @pl.when(s < spaces - 1)
    def _():
        pltpu.make_async_remote_copy(
            own_ref.at[pl.ds(x_rows - 1, 1)], stack_ref.at[me, pl.ds(0, 1)],
            send_h.at[0], recv_h.at[0, me], device_id=(0, (s + 1) % spaces), device_id_type=mesh,
        ).start()

    @pl.when(s > 0)
    def _():
        pltpu.make_async_remote_copy(
            own_ref.at[pl.ds(0, 1)], stack_ref.at[me, pl.ds(width - 1, 1)],
            send_h.at[1], recv_h.at[1, me], device_id=(groups - 1, (s + spaces - 1) % spaces), device_id_type=mesh,
        ).start()

    def stats(g):
        value = stack_ref[g]
        mean = box_rows(value)
        mean_ref[g] = mean
        spread_ref[g] = box_rows(value * value) - mean * mean

    @pl.when((me == 0) & (s == 0))
    def _():
        stack_ref[:, 0] = jnp.zeros((groups, y_rows, z_rows), jnp.float32)

    @pl.when((me == groups - 1) & (s == spaces - 1))
    def _():
        stack_ref[:, width - 1] = jnp.zeros((groups, y_rows, z_rows), jnp.float32)

    def arrive(i, carry):
        g = (me + groups - i) % groups

        @pl.when(i == 0)
        def _():
            for t in range(groups):
                src, dst = piece_copy(t, me)

                @pl.when(me == t)
                def _():
                    pltpu.make_async_copy(src, dst, local_sem.at[0]).wait()

        @pl.when(i != 0)
        def _():
            for t in range(groups):
                src, dst = piece_copy(t, 0)

                @pl.when(me == t)
                def _():
                    pltpu.make_async_remote_copy(
                        src, stack_ref.at[g, pl.ds(piece(t)[1], piece(t)[2])],
                        send_a.at[0], recv_a.at[g], device_id=(g, s), device_id_type=mesh,
                    ).wait_recv()

        @pl.when((me == 0) & (s > 0))
        def _():
            pltpu.make_async_remote_copy(
                own_ref.at[pl.ds(0, 1)], stack_ref.at[g, pl.ds(0, 1)],
                send_h.at[0], recv_h.at[0, g], device_id=(0, s), device_id_type=mesh,
            ).wait_recv()

        @pl.when((me == groups - 1) & (s < spaces - 1))
        def _():
            pltpu.make_async_remote_copy(
                own_ref.at[pl.ds(0, 1)], stack_ref.at[g, pl.ds(width - 1, 1)],
                send_h.at[1], recv_h.at[1, g], device_id=(0, s), device_id_type=mesh,
            ).wait_recv()

        stats(g)
        return carry

    lax.fori_loop(0, groups, arrive, 0)

    below = row_groups(x_rows - RADIUS, RADIUS, rows)
    above = row_groups(0, RADIUS, rows)

    def main_copy(g):
        src = out_ref.at[g]
        dst = drive_ref.at[pl.ds(RADIUS + me * rows, rows)]
        return src, dst

    def halo_copies(g):
        copies = []
        for index, (owner, src_lo, count, dst_lo) in enumerate(below):
            copies.append((owner, s < spaces - 1, 1, index, out_ref.at[g, pl.ds(src_lo, count)],
                           drive_ref.at[pl.ds(dst_lo, count)]))
        for index, (owner, src_lo, count, dst_lo) in enumerate(above):
            copies.append((owner, s > 0, -1, len(below) + index, out_ref.at[g, pl.ds(src_lo, count)],
                           drive_ref.at[pl.ds(x_rows + RADIUS + dst_lo, count)]))
        return copies

    def pairs(i, carry):
        g = (me + i) % groups
        out_ref[g] = pair_terms(g, pair_ref, stack_ref, mean_ref, spread_ref)
        src, dst = main_copy(g)

        @pl.when(me == g)
        def _():
            pltpu.make_async_copy(src, dst, local_sem.at[1]).start()

        @pl.when(me != g)
        def _():
            pltpu.make_async_remote_copy(
                src, dst, send_b.at[g], recv_b.at[me], device_id=(g, s), device_id_type=mesh
            ).start()

        for owner, exists, offset, index, hsrc, hdst in halo_copies(g):
            @pl.when((me == owner) & exists)
            def _():
                pltpu.make_async_remote_copy(
                    hsrc, hdst, send_c.at[index, g], recv_c.at[index],
                    device_id=(g, (s + offset + spaces) % spaces), device_id_type=mesh,
                ).start()
        return carry

    lax.fori_loop(0, groups, pairs, 0)

    @pl.when(s == 0)
    def _():
        pltpu.make_async_copy(zero_ref.at[pl.ds(0, RADIUS)], drive_ref.at[pl.ds(0, RADIUS)], local_sem.at[5]).start()

    @pl.when(s == spaces - 1)
    def _():
        pltpu.make_async_copy(
            zero_ref.at[pl.ds(0, RADIUS)], drive_ref.at[pl.ds(x_rows + RADIUS, RADIUS)], local_sem.at[6]
        ).start()

    for i in range(1, groups):
        forward_copy((me + i) % groups, True)

    @pl.when(s < spaces - 1)
    def _():
        pltpu.make_async_remote_copy(
            own_ref.at[pl.ds(x_rows - 1, 1)], stack_ref.at[me, pl.ds(0, 1)],
            send_h.at[0], recv_h.at[0, me], device_id=(0, (s + 1) % spaces), device_id_type=mesh,
        ).wait_send()

    @pl.when(s > 0)
    def _():
        pltpu.make_async_remote_copy(
            own_ref.at[pl.ds(0, 1)], stack_ref.at[me, pl.ds(width - 1, 1)],
            send_h.at[1], recv_h.at[1, me], device_id=(groups - 1, (s + spaces - 1) % spaces), device_id_type=mesh,
        ).wait_send()

    for g in range(groups):
        src, dst = main_copy(g)

        @pl.when(me == g)
        def _():
            pltpu.make_async_copy(src, dst, local_sem.at[1]).wait()

        @pl.when(me != g)
        def _():
            pltpu.make_async_remote_copy(
                src, dst, send_b.at[g], recv_b.at[me], device_id=(g, s), device_id_type=mesh
            ).wait_send()

        for owner, exists, offset, index, hsrc, hdst in halo_copies(g):
            @pl.when((me == owner) & exists)
            def _():
                pltpu.make_async_remote_copy(
                    hsrc, hdst, send_c.at[index, g], recv_c.at[index],
                    device_id=(g, (s + offset + spaces) % spaces), device_id_type=mesh,
                ).wait_send()

    for t in range(groups):
        @pl.when(me != t)
        def _():
            pltpu.make_async_remote_copy(
                out_ref.at[0], drive_ref.at[pl.ds(RADIUS + t * rows, rows)],
                send_b.at[0], recv_b.at[t], device_id=(t, s), device_id_type=mesh,
            ).wait_recv()

    for owner, exists, offset, index, hsrc, hdst in halo_copies(0):
        @pl.when(((offset == 1) & (s > 0)) | ((offset == -1) & (s < spaces - 1)))
        def _():
            pltpu.make_async_remote_copy(
                hsrc, hdst, send_c.at[index, 0], recv_c.at[index],
                device_id=(owner, s), device_id_type=mesh,
            ).wait_recv()

    own_halo(True)
    for exists, dst, index in (
        (s > 0, ext_ref.at[pl.ds(0, margin)], 0),
        (s < spaces - 1, ext_ref.at[pl.ds(x_rows + margin, margin)], 1),
    ):
        @pl.when(exists)
        def _():
            pltpu.make_async_remote_copy(
                own_ref.at[pl.ds(0, margin)], dst, send_o.at[index], recv_o.at[index],
                device_id=(me, s), device_id_type=mesh,
            ).wait_recv()

    @pl.when(s == 0)
    def _():
        pltpu.make_async_copy(zero_ref.at[pl.ds(0, RADIUS)], drive_ref.at[pl.ds(0, RADIUS)], local_sem.at[5]).wait()

    @pl.when(s == spaces - 1)
    def _():
        pltpu.make_async_copy(
            zero_ref.at[pl.ds(0, RADIUS)], drive_ref.at[pl.ds(x_rows + RADIUS, RADIUS)], local_sem.at[6]
        ).wait()


def front_stage(own, pairings, groups):
    x_rows, y_rows, z_rows = own.shape
    rows = x_rows // groups
    shape = (groups, rows, y_rows, z_rows)
    halos = len(row_groups(x_rows - RADIUS, RADIUS, rows)) + len(row_groups(0, RADIUS, rows))
    dma = pltpu.SemaphoreType.DMA
    return pl.pallas_call(
        front_kernel,
        out_shape=(
            jax.ShapeDtypeStruct((x_rows + 2 * RADIUS, y_rows, z_rows), jnp.float32),
            jax.ShapeDtypeStruct((x_rows + 2 * RADIUS + 2, y_rows, z_rows), jnp.float32),
        ),
        in_specs=[
            pl.BlockSpec(memory_space=pltpu.SMEM),
            pl.BlockSpec(memory_space=pltpu.VMEM),
        ],
        out_specs=(pl.BlockSpec(memory_space=pl.ANY), pl.BlockSpec(memory_space=pl.ANY)),
        scratch_shapes=[
            pltpu.VMEM((groups, rows + 2, y_rows, z_rows), jnp.float32),
            pltpu.VMEM(shape, jnp.float32),
            pltpu.VMEM(shape, jnp.float32),
            pltpu.VMEM(shape, jnp.float32),
            pltpu.VMEM((RADIUS + 1, y_rows, z_rows), jnp.float32),
            dma((groups,)),
            dma((groups,)),
            dma((2,)),
            dma((2, groups)),
            dma((groups,)),
            dma((groups,)),
            dma((halos, groups)),
            dma((halos,)),
            dma((7,)),
            dma((2,)),
            dma((2,)),
        ],
        compiler_params=pltpu.CompilerParams(collective_id=0, has_side_effects=True),
    )(pairings, own)


def shifted(value, offset, axis):
    length = value.shape[axis]
    rolled = pltpu.roll(value, (-offset) % length, axis)
    index = lax.broadcasted_iota(jnp.int32, value.shape, axis) + offset
    return jnp.where((index >= 0) & (index < length), rolled, 0.0)


PAD = 8


def post_kernel(drive_ref, own_ref, wz_ref, vel_ref, adv_ref, own_pad, force_ref, pass_ref):
    extended, y_rows, z_rows = drive_ref.shape
    x_rows = vel_ref.shape[1]
    padded = y_rows + 2 * PAD
    taps = gauss_taps(RADIUS)
    zeros = jnp.zeros((PAD, z_rows), jnp.float32)

    def inner(r, offset=0):
        return (r, pl.ds(PAD + offset, y_rows))

    def fill(r, carry):
        own_pad[r, pl.ds(0, PAD)] = zeros
        own_pad[r, pl.ds(PAD + y_rows, PAD)] = zeros
        own_pad[inner(r)] = own_ref[r]
        return carry

    lax.fori_loop(0, own_ref.shape[0], fill, 0)

    def plane(c, r, count):
        return pl.ds(pl.multiple_of((c * count + r) * y_rows, 8), y_rows)

    def force_row(r, carry):
        value = own_pad[inner(r + 1)]
        drive = drive_ref[r]
        force_ref[plane(0, r, extended)] = drive * ((own_pad[inner(r + 2)] - own_pad[inner(r)]) * 0.5)
        force_ref[plane(1, r, extended)] = drive * (
            (own_pad[inner(r + 1, 1)] - own_pad[inner(r + 1, -1)]) * 0.5
        )
        force_ref[plane(2, r, extended)] = drive * (
            (shifted(value, 1, 1) - shifted(value, -1, 1)) * 0.5
        )
        return carry

    lax.fori_loop(0, extended, force_row, 0)

    def slot(c, x):
        return pl.multiple_of((c * x_rows + x) * padded, 8)

    def x_pass(x, carry):
        for c in range(3):
            acc = taps[0] * force_ref[plane(c, x, extended)]
            for t in range(1, len(taps)):
                acc = acc + taps[t] * force_ref[plane(c, x + t, extended)]
            base = slot(c, x)
            pass_ref[pl.ds(base, PAD)] = zeros
            pass_ref[pl.ds(base + PAD, y_rows)] = acc
            pass_ref[pl.ds(base + PAD + y_rows, PAD)] = zeros
        return carry

    lax.fori_loop(0, x_rows, x_pass, 0)
    wz = wz_ref[...]
    chunk = 8 * padded
    chunks = pass_ref.shape[0] // chunk

    def z_pass(i, carry):
        rows = pl.ds(pl.multiple_of(i * chunk, 8), chunk)
        pass_ref[rows] = jnp.dot(
            pass_ref[rows], wz, precision=lax.Precision.HIGH,
            preferred_element_type=jnp.float32,
        )
        return carry

    lax.fori_loop(0, chunks, z_pass, 0)

    def out_row(x, carry):
        r = x + RADIUS + 1
        value = own_pad[inner(r)]
        change = None
        for c in range(3):
            base = slot(c, x) + PAD - RADIUS
            acc = taps[0] * pass_ref[pl.ds(base, y_rows)]
            for t in range(1, len(taps)):
                acc = acc + taps[t] * pass_ref[pl.ds(base + t, y_rows)]
            speed = step_scale * acc
            vel_ref[c, x] = speed
            if c == 0:
                backward = value - own_pad[inner(r - 1)]
                forward = own_pad[inner(r + 1)] - value
            elif c == 1:
                backward = value - own_pad[inner(r, -1)]
                forward = own_pad[inner(r, 1)] - value
            else:
                backward = value - shifted(value, -1, 1)
                forward = shifted(value, 1, 1) - value
            part = jnp.maximum(speed, 0.0) * backward + jnp.minimum(speed, 0.0) * forward
            change = part if change is None else change + part
        adv_ref[x] = value - change
        return carry

    lax.fori_loop(0, x_rows, out_row, 0)


def band(length, taps):
    radius = len(taps) // 2
    matrix = np.zeros((length, length), np.float32)
    for i in range(length):
        for t in range(-radius, radius + 1):
            if 0 <= i + t < length:
                matrix[i, i + t] = taps[t + radius]
    return matrix


def post_stage(drive_ext, own_ext):
    extended, y_rows, z_rows = drive_ext.shape
    x_rows = extended - 2 * RADIUS
    taps = gauss_taps(RADIUS)
    wz = jnp.asarray(band(z_rows, taps).T)
    vmem = pl.BlockSpec(memory_space=pltpu.VMEM)
    return pl.pallas_call(
        post_kernel,
        out_shape=(
            jax.ShapeDtypeStruct((3, x_rows, y_rows, z_rows), jnp.float32),
            jax.ShapeDtypeStruct((x_rows, y_rows, z_rows), jnp.float32),
        ),
        in_specs=[vmem] * 3,
        out_specs=(vmem, vmem),
        scratch_shapes=[
            pltpu.VMEM((extended + 2, y_rows + 2 * PAD, z_rows), jnp.float32),
            pltpu.VMEM((3 * extended * y_rows, z_rows), jnp.float32),
            pltpu.VMEM((3 * x_rows * (y_rows + 2 * PAD), z_rows), jnp.float32),
        ],
    )(drive_ext, own_ext, wz)


def shards(images, pairings):
    weights = gauss_taps(RADIUS)
    groups = lax.axis_size("img")
    own = images[0]
    x_rows, y_rows, _ = own.shape
    drive_ext, own_ext = front_stage(own, pairings, groups)
    velocity, advected = post_stage(drive_ext, own_ext)
    return (advected[None], velocity[None])


def solution(mesh):
    return jax.shard_map(
        shards,
        mesh=mesh,
        in_specs=(P("img", "space", None, None), P()),
        out_specs=(P("img", "space", None, None), P("img", None, "space", None, None)),
        check_vma=False,
    )
```

```python
import math

import jax
import numpy as np
import jax.numpy as jnp
from jax import lax
from jax.experimental import pallas as pl
from jax.experimental.pallas import tpu as pltpu
from jax.sharding import PartitionSpec as P

RADIUS = 4
PAIRINGS = 3

gauss_sigma = 1.5
step_scale = 8.0
floor_product = 0.25
floor_variance = 0.5


def gauss_taps(radius):
    raw_taps = [
        math.exp(-(offset * offset) / (2.0 * gauss_sigma * gauss_sigma))
        for offset in range(-radius, radius + 1)
    ]
    total_weight = sum(raw_taps)
    return [raw_weight / total_weight for raw_weight in raw_taps]


def halo_rows(value, width):
    peers = lax.axis_size("space")
    up = [(i, i + 1) for i in range(peers - 1)]
    down = [(i + 1, i) for i in range(peers - 1)]
    before = lax.ppermute(value[-width:], "space", up)
    after = lax.ppermute(value[:width], "space", down)
    return jnp.concatenate([before, value, after], axis=0)


def padded_along(volume, dimension, margin):
    widths = [(0, 0)] * volume.ndim
    widths[dimension] = (margin, margin)
    return jnp.pad(volume, widths)


def window(padded, dimension, offset, length):
    return lax.slice_in_dim(padded, offset, offset + length, axis=dimension)


def central(volume, dimension):
    length = volume.shape[dimension]
    padded = padded_along(volume, dimension, 1)
    return (window(padded, dimension, 2, length) - window(padded, dimension, 0, length)) * 0.5


def smooth_along(volume, dimension, weights):
    length = volume.shape[dimension]
    padded = padded_along(volume, dimension, len(weights) // 2)
    result = weights[0] * window(padded, dimension, 0, length)
    for tap_index in range(1, len(weights)):
        result = result + weights[tap_index] * window(padded, dimension, tap_index, length)
    return result


def smooth_rows(extended, weights):
    length = extended.shape[1] - len(weights) + 1
    result = weights[0] * window(extended, 1, 0, length)
    for tap_index in range(1, len(weights)):
        result = result + weights[tap_index] * window(extended, 1, tap_index, length)
    return result


def box_rows(volume):
    sx = volume[:-2] + volume[1:-1] + volume[2:]
    last = sx.shape[1] - 1
    row = lax.broadcasted_iota(jnp.int32, sx.shape, 1)
    before = jnp.where(row >= 1, pltpu.roll(sx, 1, 1), 0.0)
    after = jnp.where(row < last, pltpu.roll(sx, last, 1), 0.0)
    return (before + sx + after) / 9.0


def pair_terms(g, pair_ref, stack_ref, mean_ref, spread_ref):
    own = stack_ref[g]
    mean_own = mean_ref[g]
    spread_own = spread_ref[g]
    center_own = own[1:-1] - mean_own
    guarded_spread = jnp.maximum(spread_own, floor_variance)
    drive_sum = None
    for pairing_row in range(PAIRINGS):
        h = pair_ref[pairing_row, g]
        partner = stack_ref[h]
        mean_partner = mean_ref[h]
        spread_partner = spread_ref[h]
        cross_term = box_rows(own * partner) - mean_own * mean_partner
        factor = 2.0 * cross_term / jnp.maximum(spread_own * spread_partner, floor_product)
        ratio_term = cross_term / guarded_spread
        pair_term = factor * (partner[1:-1] - mean_partner - ratio_term * center_own)
        drive_sum = pair_term if drive_sum is None else drive_sum + pair_term
    return drive_sum


def row_groups(first, count, rows):
    groups = []
    for r in range(first, first + count):
        owner = r // rows
        if groups and groups[-1][0] == owner:
            groups[-1][2] += 1
        else:
            groups.append([owner, r - owner * rows, 1, r - first])
    return groups


def front_kernel(
    pair_ref, own_ref, drive_ref, ext_ref, stack_ref, mean_ref, spread_ref, out_ref, zero_ref,
    send_a, recv_a, send_h, recv_h, send_b, recv_b, send_c, recv_c, local_sem, send_o, recv_o,
):
    mesh = pl.DeviceIdType.MESH
    groups, width, y_rows, z_rows = stack_ref.shape
    rows = width - 2
    x_rows = own_ref.shape[0]
    spaces = lax.axis_size("space")
    me = lax.axis_index("img")
    s = lax.axis_index("space")
    has_lo = (s + spaces - 1) // spaces
    has_hi = (2 * spaces - 2 - s) // spaces

    barrier = pltpu.get_barrier_semaphore()
    for offset in (-1, 0, 1):
        exists = {-1: s > 0, 0: s >= 0, 1: s < spaces - 1}[offset]
        for g in range(groups):
            @pl.when(exists & ((offset != 0) | (me != g)))
            def _():
                pl.semaphore_signal(barrier, inc=1, device_id=(g, (s + offset + spaces) % spaces), device_id_type=mesh)
    pl.semaphore_wait(barrier, groups * (1 + has_lo + has_hi) - 1)

    zero_ref[...] = jnp.zeros(zero_ref.shape, jnp.float32)
    margin = RADIUS + 1

    def own_halo(wait):
        copies = [
            (s < spaces - 1, own_ref.at[pl.ds(x_rows - margin, margin)], ext_ref.at[pl.ds(0, margin)],
             0, (s + 1) % spaces),
            (s > 0, own_ref.at[pl.ds(0, margin)], ext_ref.at[pl.ds(x_rows + margin, margin)],
             1, (s + spaces - 1) % spaces),
        ]
        for exists, src, dst, index, target in copies:
            @pl.when(exists)
            def _():
                copy = pltpu.make_async_remote_copy(
                    src, dst, send_o.at[index], recv_o.at[index],
                    device_id=(me, target), device_id_type=mesh,
                )
                if wait:
                    copy.wait_send()
                else:
                    copy.start()
        local = [
            (s >= 0, own_ref, ext_ref.at[pl.ds(margin, x_rows)], 2),
            (s == 0, zero_ref, ext_ref.at[pl.ds(0, margin)], 3),
            (s == spaces - 1, zero_ref, ext_ref.at[pl.ds(x_rows + margin, margin)], 4),
        ]
        for exists, src, dst, index in local:
            @pl.when(exists)
            def _():
                copy = pltpu.make_async_copy(src, dst, local_sem.at[index])
                if wait:
                    copy.wait()
                else:
                    copy.start()

    own_halo(False)

    def piece(t):
        lo = max(t * rows - 1, 0)
        hi = min(t * rows + rows + 1, x_rows)
        return own_ref.at[pl.ds(lo, hi - lo)], lo - (t * rows - 1), hi - lo

    def piece_copy(t, src_image):
        src, dst_lo, count = piece(t)
        dst = stack_ref.at[src_image, pl.ds(dst_lo, count)]
        return src, dst

    def forward_copy(t_dyn, wait):
        for kind in range(3):
            cond = {0: t_dyn == 0, 1: t_dyn == groups - 1, 2: (t_dyn > 0) & (t_dyn < groups - 1)}[kind]

            @pl.when(cond & (t_dyn != me))
            def _():
                if kind == 0:
                    src, dst_lo, count = own_ref.at[pl.ds(0, rows + 1)], 1, rows + 1
                elif kind == 1:
                    src, dst_lo, count = own_ref.at[pl.ds(x_rows - rows - 1, rows + 1)], 0, rows + 1
                else:
                    src, dst_lo, count = own_ref.at[pl.ds(t_dyn * rows - 1, rows + 2)], 0, rows + 2
                copy = pltpu.make_async_remote_copy(
                    src, stack_ref.at[me, pl.ds(dst_lo, count)], send_a.at[t_dyn], recv_a.at[me],
                    device_id=(t_dyn, s), device_id_type=mesh,
                )
                if wait:
                    copy.wait_send()
                else:
                    copy.start()

    for t in range(groups):
        src, dst = piece_copy(t, me)

        @pl.when(me == t)
        def _():
            pltpu.make_async_copy(src, dst, local_sem.at[0]).start()

    for i in range(1, groups):
        forward_copy((me + i) % groups, False)

    @pl.when(s < spaces - 1)
    def _():
        pltpu.make_async_remote_copy(
            own_ref.at[pl.ds(x_rows - 1, 1)], stack_ref.at[me, pl.ds(0, 1)],
            send_h.at[0], recv_h.at[0, me], device_id=(0, (s + 1) % spaces), device_id_type=mesh,
        ).start()

    @pl.when(s > 0)
    def _():
        pltpu.make_async_remote_copy(
            own_ref.at[pl.ds(0, 1)], stack_ref.at[me, pl.ds(width - 1, 1)],
            send_h.at[1], recv_h.at[1, me], device_id=(groups - 1, (s + spaces - 1) % spaces), device_id_type=mesh,
        ).start()

    def stats(g):
        value = stack_ref[g]
        mean = box_rows(value)
        mean_ref[g] = mean
        spread_ref[g] = box_rows(value * value) - mean * mean

    @pl.when((me == 0) & (s == 0))
    def _():
        stack_ref[:, 0] = jnp.zeros((groups, y_rows, z_rows), jnp.float32)

    @pl.when((me == groups - 1) & (s == spaces - 1))
    def _():
        stack_ref[:, width - 1] = jnp.zeros((groups, y_rows, z_rows), jnp.float32)

    def arrive(i, carry):
        g = (me + groups - i) % groups

        @pl.when(i == 0)
        def _():
            for t in range(groups):
                src, dst = piece_copy(t, me)

                @pl.when(me == t)
                def _():
                    pltpu.make_async_copy(src, dst, local_sem.at[0]).wait()

        @pl.when(i != 0)
        def _():
            for t in range(groups):
                src, dst = piece_copy(t, 0)

                @pl.when(me == t)
                def _():
                    pltpu.make_async_remote_copy(
                        src, stack_ref.at[g, pl.ds(piece(t)[1], piece(t)[2])],
                        send_a.at[0], recv_a.at[g], device_id=(g, s), device_id_type=mesh,
                    ).wait_recv()

        @pl.when((me == 0) & (s > 0))
        def _():
            pltpu.make_async_remote_copy(
                own_ref.at[pl.ds(0, 1)], stack_ref.at[g, pl.ds(0, 1)],
                send_h.at[0], recv_h.at[0, g], device_id=(0, s), device_id_type=mesh,
            ).wait_recv()

        @pl.when((me == groups - 1) & (s < spaces - 1))
        def _():
            pltpu.make_async_remote_copy(
                own_ref.at[pl.ds(0, 1)], stack_ref.at[g, pl.ds(width - 1, 1)],
                send_h.at[1], recv_h.at[1, g], device_id=(0, s), device_id_type=mesh,
            ).wait_recv()

        stats(g)
        return carry

    lax.fori_loop(0, groups, arrive, 0)

    below = row_groups(x_rows - RADIUS, RADIUS, rows)
    above = row_groups(0, RADIUS, rows)

    def main_copy(g):
        src = out_ref.at[g]
        dst = drive_ref.at[pl.ds(RADIUS + me * rows, rows)]
        return src, dst

    def halo_copies(g):
        copies = []
        for index, (owner, src_lo, count, dst_lo) in enumerate(below):
            copies.append((owner, s < spaces - 1, 1, index, out_ref.at[g, pl.ds(src_lo, count)],
                           drive_ref.at[pl.ds(dst_lo, count)]))
        for index, (owner, src_lo, count, dst_lo) in enumerate(above):
            copies.append((owner, s > 0, -1, len(below) + index, out_ref.at[g, pl.ds(src_lo, count)],
                           drive_ref.at[pl.ds(x_rows + RADIUS + dst_lo, count)]))
        return copies

    def pairs(i, carry):
        g = (me + i) % groups
        out_ref[g] = pair_terms(g, pair_ref, stack_ref, mean_ref, spread_ref)
        src, dst = main_copy(g)

        @pl.when(me == g)
        def _():
            pltpu.make_async_copy(src, dst, local_sem.at[1]).start()

        @pl.when(me != g)
        def _():
            pltpu.make_async_remote_copy(
                src, dst, send_b.at[g], recv_b.at[me], device_id=(g, s), device_id_type=mesh
            ).start()

        for owner, exists, offset, index, hsrc, hdst in halo_copies(g):
            @pl.when((me == owner) & exists)
            def _():
                pltpu.make_async_remote_copy(
                    hsrc, hdst, send_c.at[index, g], recv_c.at[index],
                    device_id=(g, (s + offset + spaces) % spaces), device_id_type=mesh,
                ).start()
        return carry

    lax.fori_loop(0, groups, pairs, 0)

    @pl.when(s == 0)
    def _():
        pltpu.make_async_copy(zero_ref.at[pl.ds(0, RADIUS)], drive_ref.at[pl.ds(0, RADIUS)], local_sem.at[5]).start()

    @pl.when(s == spaces - 1)
    def _():
        pltpu.make_async_copy(
            zero_ref.at[pl.ds(0, RADIUS)], drive_ref.at[pl.ds(x_rows + RADIUS, RADIUS)], local_sem.at[6]
        ).start()

    for i in range(1, groups):
        forward_copy((me + i) % groups, True)

    @pl.when(s < spaces - 1)
    def _():
        pltpu.make_async_remote_copy(
            own_ref.at[pl.ds(x_rows - 1, 1)], stack_ref.at[me, pl.ds(0, 1)],
            send_h.at[0], recv_h.at[0, me], device_id=(0, (s + 1) % spaces), device_id_type=mesh,
        ).wait_send()

    @pl.when(s > 0)
    def _():
        pltpu.make_async_remote_copy(
            own_ref.at[pl.ds(0, 1)], stack_ref.at[me, pl.ds(width - 1, 1)],
            send_h.at[1], recv_h.at[1, me], device_id=(groups - 1, (s + spaces - 1) % spaces), device_id_type=mesh,
        ).wait_send()

    for g in range(groups):
        src, dst = main_copy(g)

        @pl.when(me == g)
        def _():
            pltpu.make_async_copy(src, dst, local_sem.at[1]).wait()

        @pl.when(me != g)
        def _():
            pltpu.make_async_remote_copy(
                src, dst, send_b.at[g], recv_b.at[me], device_id=(g, s), device_id_type=mesh
            ).wait_send()

        for owner, exists, offset, index, hsrc, hdst in halo_copies(g):
            @pl.when((me == owner) & exists)
            def _():
                pltpu.make_async_remote_copy(
                    hsrc, hdst, send_c.at[index, g], recv_c.at[index],
                    device_id=(g, (s + offset + spaces) % spaces), device_id_type=mesh,
                ).wait_send()

    for t in range(groups):
        @pl.when(me != t)
        def _():
            pltpu.make_async_remote_copy(
                out_ref.at[0], drive_ref.at[pl.ds(RADIUS + t * rows, rows)],
                send_b.at[0], recv_b.at[t], device_id=(t, s), device_id_type=mesh,
            ).wait_recv()

    for owner, exists, offset, index, hsrc, hdst in halo_copies(0):
        @pl.when(((offset == 1) & (s > 0)) | ((offset == -1) & (s < spaces - 1)))
        def _():
            pltpu.make_async_remote_copy(
                hsrc, hdst, send_c.at[index, 0], recv_c.at[index],
                device_id=(owner, s), device_id_type=mesh,
            ).wait_recv()

    own_halo(True)
    for exists, dst, index in (
        (s > 0, ext_ref.at[pl.ds(0, margin)], 0),
        (s < spaces - 1, ext_ref.at[pl.ds(x_rows + margin, margin)], 1),
    ):
        @pl.when(exists)
        def _():
            pltpu.make_async_remote_copy(
                own_ref.at[pl.ds(0, margin)], dst, send_o.at[index], recv_o.at[index],
                device_id=(me, s), device_id_type=mesh,
            ).wait_recv()

    @pl.when(s == 0)
    def _():
        pltpu.make_async_copy(zero_ref.at[pl.ds(0, RADIUS)], drive_ref.at[pl.ds(0, RADIUS)], local_sem.at[5]).wait()

    @pl.when(s == spaces - 1)
    def _():
        pltpu.make_async_copy(
            zero_ref.at[pl.ds(0, RADIUS)], drive_ref.at[pl.ds(x_rows + RADIUS, RADIUS)], local_sem.at[6]
        ).wait()


def front_stage(own, pairings, groups):
    x_rows, y_rows, z_rows = own.shape
    rows = x_rows // groups
    shape = (groups, rows, y_rows, z_rows)
    halos = len(row_groups(x_rows - RADIUS, RADIUS, rows)) + len(row_groups(0, RADIUS, rows))
    dma = pltpu.SemaphoreType.DMA
    return pl.pallas_call(
        front_kernel,
        out_shape=(
            jax.ShapeDtypeStruct((x_rows + 2 * RADIUS, y_rows, z_rows), jnp.float32),
            jax.ShapeDtypeStruct((x_rows + 2 * RADIUS + 2, y_rows, z_rows), jnp.float32),
        ),
        in_specs=[
            pl.BlockSpec(memory_space=pltpu.SMEM),
            pl.BlockSpec(memory_space=pltpu.VMEM),
        ],
        out_specs=(pl.BlockSpec(memory_space=pl.ANY), pl.BlockSpec(memory_space=pl.ANY)),
        scratch_shapes=[
            pltpu.VMEM((groups, rows + 2, y_rows, z_rows), jnp.float32),
            pltpu.VMEM(shape, jnp.float32),
            pltpu.VMEM(shape, jnp.float32),
            pltpu.VMEM(shape, jnp.float32),
            pltpu.VMEM((RADIUS + 1, y_rows, z_rows), jnp.float32),
            dma((groups,)),
            dma((groups,)),
            dma((2,)),
            dma((2, groups)),
            dma((groups,)),
            dma((groups,)),
            dma((halos, groups)),
            dma((halos,)),
            dma((7,)),
            dma((2,)),
            dma((2,)),
        ],
        compiler_params=pltpu.CompilerParams(collective_id=0, has_side_effects=True),
    )(pairings, own)


def shifted(value, offset, axis):
    length = value.shape[axis]
    rolled = pltpu.roll(value, (-offset) % length, axis)
    index = lax.broadcasted_iota(jnp.int32, value.shape, axis) + offset
    return jnp.where((index >= 0) & (index < length), rolled, 0.0)


PAD = 8


def post_kernel(drive_ref, own_ref, wz_ref, vel_ref, adv_ref, own_pad, force_ref, pass_ref):
    extended, y_rows, z_rows = drive_ref.shape
    x_rows = vel_ref.shape[1]
    padded = y_rows + 2 * PAD
    taps = gauss_taps(RADIUS)
    zeros = jnp.zeros((PAD, z_rows), jnp.float32)

    def inner(r, offset=0):
        return (r, pl.ds(PAD + offset, y_rows))

    def fill(r, carry):
        own_pad[r, pl.ds(0, PAD)] = zeros
        own_pad[r, pl.ds(PAD + y_rows, PAD)] = zeros
        own_pad[inner(r)] = own_ref[r]
        return carry

    lax.fori_loop(0, own_ref.shape[0], fill, 0)

    def plane(c, r, count):
        return pl.ds(pl.multiple_of((c * count + r) * y_rows, 8), y_rows)

    def force_row(r, carry):
        value = own_pad[inner(r + 1)]
        drive = drive_ref[r]
        force_ref[plane(0, r, extended)] = drive * ((own_pad[inner(r + 2)] - own_pad[inner(r)]) * 0.5)
        force_ref[plane(1, r, extended)] = drive * (
            (own_pad[inner(r + 1, 1)] - own_pad[inner(r + 1, -1)]) * 0.5
        )
        force_ref[plane(2, r, extended)] = drive * (
            (shifted(value, 1, 1) - shifted(value, -1, 1)) * 0.5
        )
        return carry

    lax.fori_loop(0, extended, force_row, 0)

    def slot(c, x):
        return pl.multiple_of((c * x_rows + x) * padded, 8)

    def x_pass(x, carry):
        for c in range(3):
            acc = taps[RADIUS] * force_ref[plane(c, x + RADIUS, extended)]
            for t in range(RADIUS):
                pair = force_ref[plane(c, x + t, extended)] + force_ref[plane(c, x + 2 * RADIUS - t, extended)]
                acc = acc + taps[t] * pair
            base = slot(c, x)
            pass_ref[pl.ds(base, PAD)] = zeros
            pass_ref[pl.ds(base + PAD, y_rows)] = acc
            pass_ref[pl.ds(base + PAD + y_rows, PAD)] = zeros
        return carry

    lax.fori_loop(0, x_rows, x_pass, 0)
    wz = wz_ref[...]
    chunk = 8 * padded
    chunks = pass_ref.shape[0] // chunk

    def z_pass(i, carry):
        rows = pl.ds(pl.multiple_of(i * chunk, 8), chunk)
        pass_ref[rows] = jnp.dot(
            pass_ref[rows], wz, precision=lax.Precision.HIGH,
            preferred_element_type=jnp.float32,
        )
        return carry

    lax.fori_loop(0, chunks, z_pass, 0)

    def out_row(x, carry):
        r = x + RADIUS + 1
        value = own_pad[inner(r)]
        change = None
        for c in range(3):
            base = slot(c, x) + PAD - RADIUS
            acc = taps[RADIUS] * pass_ref[pl.ds(base + RADIUS, y_rows)]
            for t in range(RADIUS):
                pair = pass_ref[pl.ds(base + t, y_rows)] + pass_ref[pl.ds(base + 2 * RADIUS - t, y_rows)]
                acc = acc + taps[t] * pair
            speed = step_scale * acc
            vel_ref[c, x] = speed
            if c == 0:
                backward = value - own_pad[inner(r - 1)]
                forward = own_pad[inner(r + 1)] - value
            elif c == 1:
                backward = value - own_pad[inner(r, -1)]
                forward = own_pad[inner(r, 1)] - value
            else:
                backward = value - shifted(value, -1, 1)
                forward = shifted(value, 1, 1) - value
            part = jnp.maximum(speed, 0.0) * backward + jnp.minimum(speed, 0.0) * forward
            change = part if change is None else change + part
        adv_ref[x] = value - change
        return carry

    lax.fori_loop(0, x_rows, out_row, 0)


def band(length, taps):
    radius = len(taps) // 2
    matrix = np.zeros((length, length), np.float32)
    for i in range(length):
        for t in range(-radius, radius + 1):
            if 0 <= i + t < length:
                matrix[i, i + t] = taps[t + radius]
    return matrix


def post_stage(drive_ext, own_ext):
    extended, y_rows, z_rows = drive_ext.shape
    x_rows = extended - 2 * RADIUS
    taps = gauss_taps(RADIUS)
    wz = jnp.asarray(band(z_rows, taps).T)
    vmem = pl.BlockSpec(memory_space=pltpu.VMEM)
    return pl.pallas_call(
        post_kernel,
        out_shape=(
            jax.ShapeDtypeStruct((3, x_rows, y_rows, z_rows), jnp.float32),
            jax.ShapeDtypeStruct((x_rows, y_rows, z_rows), jnp.float32),
        ),
        in_specs=[vmem] * 3,
        out_specs=(vmem, vmem),
        scratch_shapes=[
            pltpu.VMEM((extended + 2, y_rows + 2 * PAD, z_rows), jnp.float32),
            pltpu.VMEM((3 * extended * y_rows, z_rows), jnp.float32),
            pltpu.VMEM((3 * x_rows * (y_rows + 2 * PAD), z_rows), jnp.float32),
        ],
    )(drive_ext, own_ext, wz)


def shards(images, pairings):
    weights = gauss_taps(RADIUS)
    groups = lax.axis_size("img")
    own = images[0]
    x_rows, y_rows, _ = own.shape
    drive_ext, own_ext = front_stage(own, pairings, groups)
    velocity, advected = post_stage(drive_ext, own_ext)
    return (advected[None], velocity[None])


def solution(mesh):
    return jax.shard_map(
        shards,
        mesh=mesh,
        in_specs=(P("img", "space", None, None), P()),
        out_specs=(P("img", "space", None, None), P("img", None, "space", None, None)),
        check_vma=False,
    )
```

```python
import math

import jax
import numpy as np
import jax.numpy as jnp
from jax import lax
from jax.experimental import pallas as pl
from jax.experimental.pallas import tpu as pltpu
from jax.sharding import PartitionSpec as P

RADIUS = 4
PAIRINGS = 3

gauss_sigma = 1.5
step_scale = 8.0
floor_product = 0.25
floor_variance = 0.5


def gauss_taps(radius):
    raw_taps = [
        math.exp(-(offset * offset) / (2.0 * gauss_sigma * gauss_sigma))
        for offset in range(-radius, radius + 1)
    ]
    total_weight = sum(raw_taps)
    return [raw_weight / total_weight for raw_weight in raw_taps]


def halo_rows(value, width):
    peers = lax.axis_size("space")
    up = [(i, i + 1) for i in range(peers - 1)]
    down = [(i + 1, i) for i in range(peers - 1)]
    before = lax.ppermute(value[-width:], "space", up)
    after = lax.ppermute(value[:width], "space", down)
    return jnp.concatenate([before, value, after], axis=0)


def padded_along(volume, dimension, margin):
    widths = [(0, 0)] * volume.ndim
    widths[dimension] = (margin, margin)
    return jnp.pad(volume, widths)


def window(padded, dimension, offset, length):
    return lax.slice_in_dim(padded, offset, offset + length, axis=dimension)


def central(volume, dimension):
    length = volume.shape[dimension]
    padded = padded_along(volume, dimension, 1)
    return (window(padded, dimension, 2, length) - window(padded, dimension, 0, length)) * 0.5


def smooth_along(volume, dimension, weights):
    length = volume.shape[dimension]
    padded = padded_along(volume, dimension, len(weights) // 2)
    result = weights[0] * window(padded, dimension, 0, length)
    for tap_index in range(1, len(weights)):
        result = result + weights[tap_index] * window(padded, dimension, tap_index, length)
    return result


def smooth_rows(extended, weights):
    length = extended.shape[1] - len(weights) + 1
    result = weights[0] * window(extended, 1, 0, length)
    for tap_index in range(1, len(weights)):
        result = result + weights[tap_index] * window(extended, 1, tap_index, length)
    return result


def box_rows(volume):
    sx = volume[:-2] + volume[1:-1] + volume[2:]
    last = sx.shape[1] - 1
    row = lax.broadcasted_iota(jnp.int32, sx.shape, 1)
    before = jnp.where(row >= 1, pltpu.roll(sx, 1, 1), 0.0)
    after = jnp.where(row < last, pltpu.roll(sx, last, 1), 0.0)
    return (before + sx + after) / 9.0


def pair_terms(g, pair_ref, stack_ref, mean_ref, spread_ref):
    own = stack_ref[g]
    mean_own = mean_ref[g]
    spread_own = spread_ref[g]
    center_own = own[1:-1] - mean_own
    guarded_spread = jnp.maximum(spread_own, floor_variance)
    drive_sum = None
    for pairing_row in range(PAIRINGS):
        h = pair_ref[pairing_row, g]
        partner = stack_ref[h]
        mean_partner = mean_ref[h]
        spread_partner = spread_ref[h]
        cross_term = box_rows(own * partner) - mean_own * mean_partner
        factor = 2.0 * cross_term / jnp.maximum(spread_own * spread_partner, floor_product)
        ratio_term = cross_term / guarded_spread
        pair_term = factor * (partner[1:-1] - mean_partner - ratio_term * center_own)
        drive_sum = pair_term if drive_sum is None else drive_sum + pair_term
    return drive_sum


def row_groups(first, count, rows):
    groups = []
    for r in range(first, first + count):
        owner = r // rows
        if groups and groups[-1][0] == owner:
            groups[-1][2] += 1
        else:
            groups.append([owner, r - owner * rows, 1, r - first])
    return groups


def front_kernel(
    pair_ref, own_ref, drive_ref, ext_ref, stack_ref, mean_ref, spread_ref, out_ref, zero_ref,
    send_a, recv_a, send_h, recv_h, send_b, recv_b, send_c, recv_c, local_sem, send_o, recv_o,
):
    mesh = pl.DeviceIdType.MESH
    groups, width, y_rows, z_rows = stack_ref.shape
    rows = width - 2
    x_rows = own_ref.shape[0]
    spaces = lax.axis_size("space")
    me = lax.axis_index("img")
    s = lax.axis_index("space")
    has_lo = (s + spaces - 1) // spaces
    has_hi = (2 * spaces - 2 - s) // spaces

    barrier = pltpu.get_barrier_semaphore()
    for offset in (-1, 0, 1):
        exists = {-1: s > 0, 0: s >= 0, 1: s < spaces - 1}[offset]
        for g in range(groups):
            @pl.when(exists & ((offset != 0) | (me != g)))
            def _():
                pl.semaphore_signal(barrier, inc=1, device_id=(g, (s + offset + spaces) % spaces), device_id_type=mesh)
    pl.semaphore_wait(barrier, groups * (1 + has_lo + has_hi) - 1)

    zero_ref[...] = jnp.zeros(zero_ref.shape, jnp.float32)
    margin = RADIUS + 1

    def own_halo(wait):
        copies = [
            (s < spaces - 1, own_ref.at[pl.ds(x_rows - margin, margin)], ext_ref.at[pl.ds(0, margin)],
             0, (s + 1) % spaces),
            (s > 0, own_ref.at[pl.ds(0, margin)], ext_ref.at[pl.ds(x_rows + margin, margin)],
             1, (s + spaces - 1) % spaces),
        ]
        for exists, src, dst, index, target in copies:
            @pl.when(exists)
            def _():
                copy = pltpu.make_async_remote_copy(
                    src, dst, send_o.at[index], recv_o.at[index],
                    device_id=(me, target), device_id_type=mesh,
                )
                if wait:
                    copy.wait_send()
                else:
                    copy.start()
        local = [
            (s >= 0, own_ref, ext_ref.at[pl.ds(margin, x_rows)], 2),
            (s == 0, zero_ref, ext_ref.at[pl.ds(0, margin)], 3),
            (s == spaces - 1, zero_ref, ext_ref.at[pl.ds(x_rows + margin, margin)], 4),
        ]
        for exists, src, dst, index in local:
            @pl.when(exists)
            def _():
                copy = pltpu.make_async_copy(src, dst, local_sem.at[index])
                if wait:
                    copy.wait()
                else:
                    copy.start()

    own_halo(False)

    def piece(t):
        lo = max(t * rows - 1, 0)
        hi = min(t * rows + rows + 1, x_rows)
        return own_ref.at[pl.ds(lo, hi - lo)], lo - (t * rows - 1), hi - lo

    def piece_copy(t, src_image):
        src, dst_lo, count = piece(t)
        dst = stack_ref.at[src_image, pl.ds(dst_lo, count)]
        return src, dst

    def forward_copy(t_dyn, wait):
        for kind in range(3):
            cond = {0: t_dyn == 0, 1: t_dyn == groups - 1, 2: (t_dyn > 0) & (t_dyn < groups - 1)}[kind]

            @pl.when(cond & (t_dyn != me))
            def _():
                if kind == 0:
                    src, dst_lo, count = own_ref.at[pl.ds(0, rows + 1)], 1, rows + 1
                elif kind == 1:
                    src, dst_lo, count = own_ref.at[pl.ds(x_rows - rows - 1, rows + 1)], 0, rows + 1
                else:
                    src, dst_lo, count = own_ref.at[pl.ds(t_dyn * rows - 1, rows + 2)], 0, rows + 2
                copy = pltpu.make_async_remote_copy(
                    src, stack_ref.at[me, pl.ds(dst_lo, count)], send_a.at[t_dyn], recv_a.at[me],
                    device_id=(t_dyn, s), device_id_type=mesh,
                )
                if wait:
                    copy.wait_send()
                else:
                    copy.start()

    for t in range(groups):
        src, dst = piece_copy(t, me)

        @pl.when(me == t)
        def _():
            pltpu.make_async_copy(src, dst, local_sem.at[0]).start()

    for i in range(1, groups):
        forward_copy((me + i) % groups, False)

    @pl.when(s < spaces - 1)
    def _():
        pltpu.make_async_remote_copy(
            own_ref.at[pl.ds(x_rows - 1, 1)], stack_ref.at[me, pl.ds(0, 1)],
            send_h.at[0], recv_h.at[0, me], device_id=(0, (s + 1) % spaces), device_id_type=mesh,
        ).start()

    @pl.when(s > 0)
    def _():
        pltpu.make_async_remote_copy(
            own_ref.at[pl.ds(0, 1)], stack_ref.at[me, pl.ds(width - 1, 1)],
            send_h.at[1], recv_h.at[1, me], device_id=(groups - 1, (s + spaces - 1) % spaces), device_id_type=mesh,
        ).start()

    def stats(g):
        value = stack_ref[g]
        mean = box_rows(value)
        mean_ref[g] = mean
        spread_ref[g] = box_rows(value * value) - mean * mean

    @pl.when((me == 0) & (s == 0))
    def _():
        stack_ref[:, 0] = jnp.zeros((groups, y_rows, z_rows), jnp.float32)

    @pl.when((me == groups - 1) & (s == spaces - 1))
    def _():
        stack_ref[:, width - 1] = jnp.zeros((groups, y_rows, z_rows), jnp.float32)

    def arrive(i, carry):
        g = (me + groups - i) % groups

        @pl.when(i == 0)
        def _():
            for t in range(groups):
                src, dst = piece_copy(t, me)

                @pl.when(me == t)
                def _():
                    pltpu.make_async_copy(src, dst, local_sem.at[0]).wait()

        @pl.when(i != 0)
        def _():
            for t in range(groups):
                src, dst = piece_copy(t, 0)

                @pl.when(me == t)
                def _():
                    pltpu.make_async_remote_copy(
                        src, stack_ref.at[g, pl.ds(piece(t)[1], piece(t)[2])],
                        send_a.at[0], recv_a.at[g], device_id=(g, s), device_id_type=mesh,
                    ).wait_recv()

        @pl.when((me == 0) & (s > 0))
        def _():
            pltpu.make_async_remote_copy(
                own_ref.at[pl.ds(0, 1)], stack_ref.at[g, pl.ds(0, 1)],
                send_h.at[0], recv_h.at[0, g], device_id=(0, s), device_id_type=mesh,
            ).wait_recv()

        @pl.when((me == groups - 1) & (s < spaces - 1))
        def _():
            pltpu.make_async_remote_copy(
                own_ref.at[pl.ds(0, 1)], stack_ref.at[g, pl.ds(width - 1, 1)],
                send_h.at[1], recv_h.at[1, g], device_id=(0, s), device_id_type=mesh,
            ).wait_recv()

        stats(g)
        return carry

    lax.fori_loop(0, groups, arrive, 0)

    below = row_groups(x_rows - RADIUS, RADIUS, rows)
    above = row_groups(0, RADIUS, rows)

    def main_copy(g):
        src = out_ref.at[g]
        dst = drive_ref.at[pl.ds(RADIUS + me * rows, rows)]
        return src, dst

    def halo_copies(g):
        copies = []
        for index, (owner, src_lo, count, dst_lo) in enumerate(below):
            copies.append((owner, s < spaces - 1, 1, index, out_ref.at[g, pl.ds(src_lo, count)],
                           drive_ref.at[pl.ds(dst_lo, count)]))
        for index, (owner, src_lo, count, dst_lo) in enumerate(above):
            copies.append((owner, s > 0, -1, len(below) + index, out_ref.at[g, pl.ds(src_lo, count)],
                           drive_ref.at[pl.ds(x_rows + RADIUS + dst_lo, count)]))
        return copies

    def pairs(i, carry):
        g = (me + i) % groups
        out_ref[g] = pair_terms(g, pair_ref, stack_ref, mean_ref, spread_ref)
        src, dst = main_copy(g)

        @pl.when(me == g)
        def _():
            pltpu.make_async_copy(src, dst, local_sem.at[1]).start()

        @pl.when(me != g)
        def _():
            pltpu.make_async_remote_copy(
                src, dst, send_b.at[g], recv_b.at[me], device_id=(g, s), device_id_type=mesh
            ).start()

        for owner, exists, offset, index, hsrc, hdst in halo_copies(g):
            @pl.when((me == owner) & exists)
            def _():
                pltpu.make_async_remote_copy(
                    hsrc, hdst, send_c.at[index, g], recv_c.at[index],
                    device_id=(g, (s + offset + spaces) % spaces), device_id_type=mesh,
                ).start()
        return carry

    lax.fori_loop(0, groups, pairs, 0)

    @pl.when(s == 0)
    def _():
        pltpu.make_async_copy(zero_ref.at[pl.ds(0, RADIUS)], drive_ref.at[pl.ds(0, RADIUS)], local_sem.at[5]).start()

    @pl.when(s == spaces - 1)
    def _():
        pltpu.make_async_copy(
            zero_ref.at[pl.ds(0, RADIUS)], drive_ref.at[pl.ds(x_rows + RADIUS, RADIUS)], local_sem.at[6]
        ).start()

    for i in range(1, groups):
        forward_copy((me + i) % groups, True)

    @pl.when(s < spaces - 1)
    def _():
        pltpu.make_async_remote_copy(
            own_ref.at[pl.ds(x_rows - 1, 1)], stack_ref.at[me, pl.ds(0, 1)],
            send_h.at[0], recv_h.at[0, me], device_id=(0, (s + 1) % spaces), device_id_type=mesh,
        ).wait_send()

    @pl.when(s > 0)
    def _():
        pltpu.make_async_remote_copy(
            own_ref.at[pl.ds(0, 1)], stack_ref.at[me, pl.ds(width - 1, 1)],
            send_h.at[1], recv_h.at[1, me], device_id=(groups - 1, (s + spaces - 1) % spaces), device_id_type=mesh,
        ).wait_send()

    for g in range(groups):
        src, dst = main_copy(g)

        @pl.when(me == g)
        def _():
            pltpu.make_async_copy(src, dst, local_sem.at[1]).wait()

        @pl.when(me != g)
        def _():
            pltpu.make_async_remote_copy(
                src, dst, send_b.at[g], recv_b.at[me], device_id=(g, s), device_id_type=mesh
            ).wait_send()

        for owner, exists, offset, index, hsrc, hdst in halo_copies(g):
            @pl.when((me == owner) & exists)
            def _():
                pltpu.make_async_remote_copy(
                    hsrc, hdst, send_c.at[index, g], recv_c.at[index],
                    device_id=(g, (s + offset + spaces) % spaces), device_id_type=mesh,
                ).wait_send()

    for t in range(groups):
        @pl.when(me != t)
        def _():
            pltpu.make_async_remote_copy(
                out_ref.at[0], drive_ref.at[pl.ds(RADIUS + t * rows, rows)],
                send_b.at[0], recv_b.at[t], device_id=(t, s), device_id_type=mesh,
            ).wait_recv()

    for owner, exists, offset, index, hsrc, hdst in halo_copies(0):
        @pl.when(((offset == 1) & (s > 0)) | ((offset == -1) & (s < spaces - 1)))
        def _():
            pltpu.make_async_remote_copy(
                hsrc, hdst, send_c.at[index, 0], recv_c.at[index],
                device_id=(owner, s), device_id_type=mesh,
            ).wait_recv()

    own_halo(True)
    for exists, dst, index in (
        (s > 0, ext_ref.at[pl.ds(0, margin)], 0),
        (s < spaces - 1, ext_ref.at[pl.ds(x_rows + margin, margin)], 1),
    ):
        @pl.when(exists)
        def _():
            pltpu.make_async_remote_copy(
                own_ref.at[pl.ds(0, margin)], dst, send_o.at[index], recv_o.at[index],
                device_id=(me, s), device_id_type=mesh,
            ).wait_recv()

    @pl.when(s == 0)
    def _():
        pltpu.make_async_copy(zero_ref.at[pl.ds(0, RADIUS)], drive_ref.at[pl.ds(0, RADIUS)], local_sem.at[5]).wait()

    @pl.when(s == spaces - 1)
    def _():
        pltpu.make_async_copy(
            zero_ref.at[pl.ds(0, RADIUS)], drive_ref.at[pl.ds(x_rows + RADIUS, RADIUS)], local_sem.at[6]
        ).wait()


def front_stage(own, pairings, groups):
    x_rows, y_rows, z_rows = own.shape
    rows = x_rows // groups
    shape = (groups, rows, y_rows, z_rows)
    halos = len(row_groups(x_rows - RADIUS, RADIUS, rows)) + len(row_groups(0, RADIUS, rows))
    dma = pltpu.SemaphoreType.DMA
    return pl.pallas_call(
        front_kernel,
        out_shape=(
            jax.ShapeDtypeStruct((x_rows + 2 * RADIUS, y_rows, z_rows), jnp.float32),
            jax.ShapeDtypeStruct((x_rows + 2 * RADIUS + 2, y_rows, z_rows), jnp.float32),
        ),
        in_specs=[
            pl.BlockSpec(memory_space=pltpu.SMEM),
            pl.BlockSpec(memory_space=pltpu.VMEM),
        ],
        out_specs=(pl.BlockSpec(memory_space=pl.ANY), pl.BlockSpec(memory_space=pl.ANY)),
        scratch_shapes=[
            pltpu.VMEM((groups, rows + 2, y_rows, z_rows), jnp.float32),
            pltpu.VMEM(shape, jnp.float32),
            pltpu.VMEM(shape, jnp.float32),
            pltpu.VMEM(shape, jnp.float32),
            pltpu.VMEM((RADIUS + 1, y_rows, z_rows), jnp.float32),
            dma((groups,)),
            dma((groups,)),
            dma((2,)),
            dma((2, groups)),
            dma((groups,)),
            dma((groups,)),
            dma((halos, groups)),
            dma((halos,)),
            dma((7,)),
            dma((2,)),
            dma((2,)),
        ],
        compiler_params=pltpu.CompilerParams(collective_id=0, has_side_effects=True),
    )(pairings, own)


def shifted(value, offset, axis):
    length = value.shape[axis]
    rolled = pltpu.roll(value, (-offset) % length, axis)
    index = lax.broadcasted_iota(jnp.int32, value.shape, axis) + offset
    return jnp.where((index >= 0) & (index < length), rolled, 0.0)


PAD = 8


def post_kernel(
    drive_ref, own_ref, wz_ref, vel_ref, adv_ref, own_pad, force_ref, pass_ref, vel_buf, adv_buf, sems
):
    extended, y_rows, z_rows = drive_ref.shape
    x_rows = vel_ref.shape[1]
    padded = y_rows + 2 * PAD
    taps = gauss_taps(RADIUS)
    zeros = jnp.zeros((PAD, z_rows), jnp.float32)

    def inner(r, offset=0):
        return (r, pl.ds(PAD + offset, y_rows))

    def fill(r, carry):
        own_pad[r, pl.ds(0, PAD)] = zeros
        own_pad[r, pl.ds(PAD + y_rows, PAD)] = zeros
        own_pad[inner(r)] = own_ref[r]
        return carry

    lax.fori_loop(0, own_ref.shape[0], fill, 0)

    def plane(c, r, count):
        return pl.ds(pl.multiple_of((c * count + r) * y_rows, 8), y_rows)

    def force_row(r, carry):
        value = own_pad[inner(r + 1)]
        drive = drive_ref[r]
        force_ref[plane(0, r, extended)] = drive * ((own_pad[inner(r + 2)] - own_pad[inner(r)]) * 0.5)
        force_ref[plane(1, r, extended)] = drive * (
            (own_pad[inner(r + 1, 1)] - own_pad[inner(r + 1, -1)]) * 0.5
        )
        force_ref[plane(2, r, extended)] = drive * (
            (shifted(value, 1, 1) - shifted(value, -1, 1)) * 0.5
        )
        return carry

    lax.fori_loop(0, extended, force_row, 0)

    def slot(c, x):
        return pl.multiple_of((c * x_rows + x) * padded, 8)

    def x_pass(x, carry):
        for c in range(3):
            acc = taps[RADIUS] * force_ref[plane(c, x + RADIUS, extended)]
            for t in range(RADIUS):
                pair = force_ref[plane(c, x + t, extended)] + force_ref[plane(c, x + 2 * RADIUS - t, extended)]
                acc = acc + taps[t] * pair
            base = slot(c, x)
            pass_ref[pl.ds(base, PAD)] = zeros
            pass_ref[pl.ds(base + PAD, y_rows)] = acc
            pass_ref[pl.ds(base + PAD + y_rows, PAD)] = zeros
        return carry

    lax.fori_loop(0, x_rows, x_pass, 0)
    wz = wz_ref[...]
    chunk = 8 * padded
    chunks = pass_ref.shape[0] // chunk

    def z_pass(i, carry):
        rows = pl.ds(pl.multiple_of(i * chunk, 8), chunk)
        pass_ref[rows] = jnp.dot(
            pass_ref[rows], wz, precision=lax.Precision.HIGH,
            preferred_element_type=jnp.float32,
        )
        return carry

    lax.fori_loop(0, chunks, z_pass, 0)

    def out_row(x, carry):
        r = x + RADIUS + 1
        value = own_pad[inner(r)]
        change = None
        for c in range(3):
            base = slot(c, x) + PAD - RADIUS
            acc = taps[RADIUS] * pass_ref[pl.ds(base + RADIUS, y_rows)]
            for t in range(RADIUS):
                pair = pass_ref[pl.ds(base + t, y_rows)] + pass_ref[pl.ds(base + 2 * RADIUS - t, y_rows)]
                acc = acc + taps[t] * pair
            speed = step_scale * acc
            vel_buf[c, x] = speed
            if c == 0:
                backward = value - own_pad[inner(r - 1)]
                forward = own_pad[inner(r + 1)] - value
            elif c == 1:
                backward = value - own_pad[inner(r, -1)]
                forward = own_pad[inner(r, 1)] - value
            else:
                backward = value - shifted(value, -1, 1)
                forward = shifted(value, 1, 1) - value
            part = jnp.maximum(speed, 0.0) * backward + jnp.minimum(speed, 0.0) * forward
            change = part if change is None else change + part
        adv_buf[x] = value - change
        row = pl.ds(x, 1)
        pltpu.make_async_copy(vel_buf.at[:, row], vel_ref.at[:, row], sems.at[0]).start()
        pltpu.make_async_copy(adv_buf.at[row], adv_ref.at[row], sems.at[1]).start()
        return carry

    lax.fori_loop(0, x_rows, out_row, 0)
    pltpu.make_async_copy(vel_buf, vel_ref, sems.at[0]).wait()
    pltpu.make_async_copy(adv_buf, adv_ref, sems.at[1]).wait()


def band(length, taps):
    radius = len(taps) // 2
    matrix = np.zeros((length, length), np.float32)
    for i in range(length):
        for t in range(-radius, radius + 1):
            if 0 <= i + t < length:
                matrix[i, i + t] = taps[t + radius]
    return matrix


def post_stage(drive_ext, own_ext):
    extended, y_rows, z_rows = drive_ext.shape
    x_rows = extended - 2 * RADIUS
    taps = gauss_taps(RADIUS)
    wz = jnp.asarray(band(z_rows, taps).T)
    vmem = pl.BlockSpec(memory_space=pltpu.VMEM)
    return pl.pallas_call(
        post_kernel,
        out_shape=(
            jax.ShapeDtypeStruct((3, x_rows, y_rows, z_rows), jnp.float32),
            jax.ShapeDtypeStruct((x_rows, y_rows, z_rows), jnp.float32),
        ),
        in_specs=[vmem] * 3,
        out_specs=(pl.BlockSpec(memory_space=pl.ANY), pl.BlockSpec(memory_space=pl.ANY)),
        scratch_shapes=[
            pltpu.VMEM((extended + 2, y_rows + 2 * PAD, z_rows), jnp.float32),
            pltpu.VMEM((3 * extended * y_rows, z_rows), jnp.float32),
            pltpu.VMEM((3 * x_rows * (y_rows + 2 * PAD), z_rows), jnp.float32),
            pltpu.VMEM((3, x_rows, y_rows, z_rows), jnp.float32),
            pltpu.VMEM((x_rows, y_rows, z_rows), jnp.float32),
            pltpu.SemaphoreType.DMA((2,)),
        ],
    )(drive_ext, own_ext, wz)


def shards(images, pairings):
    weights = gauss_taps(RADIUS)
    groups = lax.axis_size("img")
    own = images[0]
    x_rows, y_rows, _ = own.shape
    drive_ext, own_ext = front_stage(own, pairings, groups)
    velocity, advected = post_stage(drive_ext, own_ext)
    return (advected[None], velocity[None])


def solution(mesh):
    return jax.shard_map(
        shards,
        mesh=mesh,
        in_specs=(P("img", "space", None, None), P()),
        out_specs=(P("img", "space", None, None), P("img", None, "space", None, None)),
        check_vma=False,
    )
```

```python
import math

import jax
import numpy as np
import jax.numpy as jnp
from jax import lax
from jax.experimental import pallas as pl
from jax.experimental.pallas import tpu as pltpu
from jax.sharding import PartitionSpec as P

RADIUS = 4
PAIRINGS = 3

gauss_sigma = 1.5
step_scale = 8.0
floor_product = 0.25
floor_variance = 0.5


def gauss_taps(radius):
    raw_taps = [
        math.exp(-(offset * offset) / (2.0 * gauss_sigma * gauss_sigma))
        for offset in range(-radius, radius + 1)
    ]
    total_weight = sum(raw_taps)
    return [raw_weight / total_weight for raw_weight in raw_taps]


def halo_rows(value, width):
    peers = lax.axis_size("space")
    up = [(i, i + 1) for i in range(peers - 1)]
    down = [(i + 1, i) for i in range(peers - 1)]
    before = lax.ppermute(value[-width:], "space", up)
    after = lax.ppermute(value[:width], "space", down)
    return jnp.concatenate([before, value, after], axis=0)


def padded_along(volume, dimension, margin):
    widths = [(0, 0)] * volume.ndim
    widths[dimension] = (margin, margin)
    return jnp.pad(volume, widths)


def window(padded, dimension, offset, length):
    return lax.slice_in_dim(padded, offset, offset + length, axis=dimension)


def central(volume, dimension):
    length = volume.shape[dimension]
    padded = padded_along(volume, dimension, 1)
    return (window(padded, dimension, 2, length) - window(padded, dimension, 0, length)) * 0.5


def smooth_along(volume, dimension, weights):
    length = volume.shape[dimension]
    padded = padded_along(volume, dimension, len(weights) // 2)
    result = weights[0] * window(padded, dimension, 0, length)
    for tap_index in range(1, len(weights)):
        result = result + weights[tap_index] * window(padded, dimension, tap_index, length)
    return result


def smooth_rows(extended, weights):
    length = extended.shape[1] - len(weights) + 1
    result = weights[0] * window(extended, 1, 0, length)
    for tap_index in range(1, len(weights)):
        result = result + weights[tap_index] * window(extended, 1, tap_index, length)
    return result


def box_rows(volume):
    sx = volume[:-2] + volume[1:-1] + volume[2:]
    last = sx.shape[1] - 1
    row = lax.broadcasted_iota(jnp.int32, sx.shape, 1)
    before = jnp.where(row >= 1, pltpu.roll(sx, 1, 1), 0.0)
    after = jnp.where(row < last, pltpu.roll(sx, last, 1), 0.0)
    return (before + sx + after) / 9.0


def pair_terms(g, pair_ref, stack_ref, mean_ref, spread_ref):
    own = stack_ref[g]
    mean_own = mean_ref[g]
    spread_own = spread_ref[g]
    center_own = own[1:-1] - mean_own
    guarded_spread = jnp.maximum(spread_own, floor_variance)
    drive_sum = None
    for pairing_row in range(PAIRINGS):
        h = pair_ref[pairing_row, g]
        partner = stack_ref[h]
        mean_partner = mean_ref[h]
        spread_partner = spread_ref[h]
        cross_term = box_rows(own * partner) - mean_own * mean_partner
        factor = 2.0 * cross_term / jnp.maximum(spread_own * spread_partner, floor_product)
        ratio_term = cross_term / guarded_spread
        pair_term = factor * (partner[1:-1] - mean_partner - ratio_term * center_own)
        drive_sum = pair_term if drive_sum is None else drive_sum + pair_term
    return drive_sum


def row_groups(first, count, rows):
    groups = []
    for r in range(first, first + count):
        owner = r // rows
        if groups and groups[-1][0] == owner:
            groups[-1][2] += 1
        else:
            groups.append([owner, r - owner * rows, 1, r - first])
    return groups


def front_kernel(
    pair_ref, own_ref, drive_ref, ext_ref, stack_ref, mean_ref, spread_ref, out_ref, zero_ref,
    send_a, recv_a, send_h, recv_h, send_b, recv_b, send_c, recv_c, local_sem, send_o, recv_o,
):
    mesh = pl.DeviceIdType.MESH
    groups, width, y_rows, z_rows = stack_ref.shape
    rows = width - 2
    x_rows = own_ref.shape[0]
    spaces = lax.axis_size("space")
    me = lax.axis_index("img")
    s = lax.axis_index("space")
    has_lo = (s + spaces - 1) // spaces
    has_hi = (2 * spaces - 2 - s) // spaces

    barrier = pltpu.get_barrier_semaphore()
    for offset in (-1, 0, 1):
        exists = {-1: s > 0, 0: s >= 0, 1: s < spaces - 1}[offset]
        for g in range(groups):
            @pl.when(exists & ((offset != 0) | (me != g)))
            def _():
                pl.semaphore_signal(barrier, inc=1, device_id=(g, (s + offset + spaces) % spaces), device_id_type=mesh)
    pl.semaphore_wait(barrier, groups * (1 + has_lo + has_hi) - 1)

    zero_ref[...] = jnp.zeros(zero_ref.shape, jnp.float32)
    margin = RADIUS + 1

    def own_halo(wait):
        copies = [
            (s < spaces - 1, own_ref.at[pl.ds(x_rows - margin, margin)], ext_ref.at[pl.ds(0, margin)],
             0, (s + 1) % spaces),
            (s > 0, own_ref.at[pl.ds(0, margin)], ext_ref.at[pl.ds(x_rows + margin, margin)],
             1, (s + spaces - 1) % spaces),
        ]
        for exists, src, dst, index, target in copies:
            @pl.when(exists)
            def _():
                copy = pltpu.make_async_remote_copy(
                    src, dst, send_o.at[index], recv_o.at[index],
                    device_id=(me, target), device_id_type=mesh,
                )
                if wait:
                    copy.wait_send()
                else:
                    copy.start()
        local = [
            (s >= 0, own_ref, ext_ref.at[pl.ds(margin, x_rows)], 2),
            (s == 0, zero_ref, ext_ref.at[pl.ds(0, margin)], 3),
            (s == spaces - 1, zero_ref, ext_ref.at[pl.ds(x_rows + margin, margin)], 4),
        ]
        for exists, src, dst, index in local:
            @pl.when(exists)
            def _():
                copy = pltpu.make_async_copy(src, dst, local_sem.at[index])
                if wait:
                    copy.wait()
                else:
                    copy.start()

    own_halo(False)

    def piece(t):
        lo = max(t * rows - 1, 0)
        hi = min(t * rows + rows + 1, x_rows)
        return own_ref.at[pl.ds(lo, hi - lo)], lo - (t * rows - 1), hi - lo

    def piece_copy(t, src_image):
        src, dst_lo, count = piece(t)
        dst = stack_ref.at[src_image, pl.ds(dst_lo, count)]
        return src, dst

    def forward_copy(t_dyn, wait):
        for kind in range(3):
            cond = {0: t_dyn == 0, 1: t_dyn == groups - 1, 2: (t_dyn > 0) & (t_dyn < groups - 1)}[kind]

            @pl.when(cond & (t_dyn != me))
            def _():
                if kind == 0:
                    src, dst_lo, count = own_ref.at[pl.ds(0, rows + 1)], 1, rows + 1
                elif kind == 1:
                    src, dst_lo, count = own_ref.at[pl.ds(x_rows - rows - 1, rows + 1)], 0, rows + 1
                else:
                    src, dst_lo, count = own_ref.at[pl.ds(t_dyn * rows - 1, rows + 2)], 0, rows + 2
                copy = pltpu.make_async_remote_copy(
                    src, stack_ref.at[me, pl.ds(dst_lo, count)], send_a.at[t_dyn], recv_a.at[me],
                    device_id=(t_dyn, s), device_id_type=mesh,
                )
                if wait:
                    copy.wait_send()
                else:
                    copy.start()

    for t in range(groups):
        src, dst = piece_copy(t, me)

        @pl.when(me == t)
        def _():
            pltpu.make_async_copy(src, dst, local_sem.at[0]).start()

    for i in range(1, groups):
        forward_copy((me + i) % groups, False)

    @pl.when(s < spaces - 1)
    def _():
        pltpu.make_async_remote_copy(
            own_ref.at[pl.ds(x_rows - 1, 1)], stack_ref.at[me, pl.ds(0, 1)],
            send_h.at[0], recv_h.at[0, me], device_id=(0, (s + 1) % spaces), device_id_type=mesh,
        ).start()

    @pl.when(s > 0)
    def _():
        pltpu.make_async_remote_copy(
            own_ref.at[pl.ds(0, 1)], stack_ref.at[me, pl.ds(width - 1, 1)],
            send_h.at[1], recv_h.at[1, me], device_id=(groups - 1, (s + spaces - 1) % spaces), device_id_type=mesh,
        ).start()

    def stats(g):
        value = stack_ref[g]
        mean = box_rows(value)
        mean_ref[g] = mean
        spread_ref[g] = box_rows(value * value) - mean * mean

    @pl.when((me == 0) & (s == 0))
    def _():
        stack_ref[:, 0] = jnp.zeros((groups, y_rows, z_rows), jnp.float32)

    @pl.when((me == groups - 1) & (s == spaces - 1))
    def _():
        stack_ref[:, width - 1] = jnp.zeros((groups, y_rows, z_rows), jnp.float32)

    def arrive(i, carry):
        g = (me + groups - i) % groups

        @pl.when(i == 0)
        def _():
            for t in range(groups):
                src, dst = piece_copy(t, me)

                @pl.when(me == t)
                def _():
                    pltpu.make_async_copy(src, dst, local_sem.at[0]).wait()

        @pl.when(i != 0)
        def _():
            for t in range(groups):
                src, dst = piece_copy(t, 0)

                @pl.when(me == t)
                def _():
                    pltpu.make_async_remote_copy(
                        src, stack_ref.at[g, pl.ds(piece(t)[1], piece(t)[2])],
                        send_a.at[0], recv_a.at[g], device_id=(g, s), device_id_type=mesh,
                    ).wait_recv()

        @pl.when((me == 0) & (s > 0))
        def _():
            pltpu.make_async_remote_copy(
                own_ref.at[pl.ds(0, 1)], stack_ref.at[g, pl.ds(0, 1)],
                send_h.at[0], recv_h.at[0, g], device_id=(0, s), device_id_type=mesh,
            ).wait_recv()

        @pl.when((me == groups - 1) & (s < spaces - 1))
        def _():
            pltpu.make_async_remote_copy(
                own_ref.at[pl.ds(0, 1)], stack_ref.at[g, pl.ds(width - 1, 1)],
                send_h.at[1], recv_h.at[1, g], device_id=(0, s), device_id_type=mesh,
            ).wait_recv()

        stats(g)
        return carry

    lax.fori_loop(0, groups, arrive, 0)

    below = row_groups(x_rows - RADIUS, RADIUS, rows)
    above = row_groups(0, RADIUS, rows)

    def main_copy(g):
        src = out_ref.at[g]
        dst = drive_ref.at[pl.ds(RADIUS + me * rows, rows)]
        return src, dst

    def halo_copies(g):
        copies = []
        for index, (owner, src_lo, count, dst_lo) in enumerate(below):
            copies.append((owner, s < spaces - 1, 1, index, out_ref.at[g, pl.ds(src_lo, count)],
                           drive_ref.at[pl.ds(dst_lo, count)]))
        for index, (owner, src_lo, count, dst_lo) in enumerate(above):
            copies.append((owner, s > 0, -1, len(below) + index, out_ref.at[g, pl.ds(src_lo, count)],
                           drive_ref.at[pl.ds(x_rows + RADIUS + dst_lo, count)]))
        return copies

    def pairs(i, carry):
        g = (me + i) % groups
        out_ref[g] = pair_terms(g, pair_ref, stack_ref, mean_ref, spread_ref)
        src, dst = main_copy(g)

        @pl.when(me == g)
        def _():
            pltpu.make_async_copy(src, dst, local_sem.at[1]).start()

        @pl.when(me != g)
        def _():
            pltpu.make_async_remote_copy(
                src, dst, send_b.at[g], recv_b.at[me], device_id=(g, s), device_id_type=mesh
            ).start()

        for owner, exists, offset, index, hsrc, hdst in halo_copies(g):
            @pl.when((me == owner) & exists)
            def _():
                pltpu.make_async_remote_copy(
                    hsrc, hdst, send_c.at[index, g], recv_c.at[index],
                    device_id=(g, (s + offset + spaces) % spaces), device_id_type=mesh,
                ).start()
        return carry

    lax.fori_loop(0, groups, pairs, 0)

    @pl.when(s == 0)
    def _():
        pltpu.make_async_copy(zero_ref.at[pl.ds(0, RADIUS)], drive_ref.at[pl.ds(0, RADIUS)], local_sem.at[5]).start()

    @pl.when(s == spaces - 1)
    def _():
        pltpu.make_async_copy(
            zero_ref.at[pl.ds(0, RADIUS)], drive_ref.at[pl.ds(x_rows + RADIUS, RADIUS)], local_sem.at[6]
        ).start()

    for i in range(1, groups):
        forward_copy((me + i) % groups, True)

    @pl.when(s < spaces - 1)
    def _():
        pltpu.make_async_remote_copy(
            own_ref.at[pl.ds(x_rows - 1, 1)], stack_ref.at[me, pl.ds(0, 1)],
            send_h.at[0], recv_h.at[0, me], device_id=(0, (s + 1) % spaces), device_id_type=mesh,
        ).wait_send()

    @pl.when(s > 0)
    def _():
        pltpu.make_async_remote_copy(
            own_ref.at[pl.ds(0, 1)], stack_ref.at[me, pl.ds(width - 1, 1)],
            send_h.at[1], recv_h.at[1, me], device_id=(groups - 1, (s + spaces - 1) % spaces), device_id_type=mesh,
        ).wait_send()

    for g in range(groups):
        src, dst = main_copy(g)

        @pl.when(me == g)
        def _():
            pltpu.make_async_copy(src, dst, local_sem.at[1]).wait()

        @pl.when(me != g)
        def _():
            pltpu.make_async_remote_copy(
                src, dst, send_b.at[g], recv_b.at[me], device_id=(g, s), device_id_type=mesh
            ).wait_send()

        for owner, exists, offset, index, hsrc, hdst in halo_copies(g):
            @pl.when((me == owner) & exists)
            def _():
                pltpu.make_async_remote_copy(
                    hsrc, hdst, send_c.at[index, g], recv_c.at[index],
                    device_id=(g, (s + offset + spaces) % spaces), device_id_type=mesh,
                ).wait_send()

    for t in range(groups):
        @pl.when(me != t)
        def _():
            pltpu.make_async_remote_copy(
                out_ref.at[0], drive_ref.at[pl.ds(RADIUS + t * rows, rows)],
                send_b.at[0], recv_b.at[t], device_id=(t, s), device_id_type=mesh,
            ).wait_recv()

    for owner, exists, offset, index, hsrc, hdst in halo_copies(0):
        @pl.when(((offset == 1) & (s > 0)) | ((offset == -1) & (s < spaces - 1)))
        def _():
            pltpu.make_async_remote_copy(
                hsrc, hdst, send_c.at[index, 0], recv_c.at[index],
                device_id=(owner, s), device_id_type=mesh,
            ).wait_recv()

    own_halo(True)
    for exists, dst, index in (
        (s > 0, ext_ref.at[pl.ds(0, margin)], 0),
        (s < spaces - 1, ext_ref.at[pl.ds(x_rows + margin, margin)], 1),
    ):
        @pl.when(exists)
        def _():
            pltpu.make_async_remote_copy(
                own_ref.at[pl.ds(0, margin)], dst, send_o.at[index], recv_o.at[index],
                device_id=(me, s), device_id_type=mesh,
            ).wait_recv()

    @pl.when(s == 0)
    def _():
        pltpu.make_async_copy(zero_ref.at[pl.ds(0, RADIUS)], drive_ref.at[pl.ds(0, RADIUS)], local_sem.at[5]).wait()

    @pl.when(s == spaces - 1)
    def _():
        pltpu.make_async_copy(
            zero_ref.at[pl.ds(0, RADIUS)], drive_ref.at[pl.ds(x_rows + RADIUS, RADIUS)], local_sem.at[6]
        ).wait()


def front_stage(own, pairings, groups):
    x_rows, y_rows, z_rows = own.shape
    rows = x_rows // groups
    shape = (groups, rows, y_rows, z_rows)
    halos = len(row_groups(x_rows - RADIUS, RADIUS, rows)) + len(row_groups(0, RADIUS, rows))
    dma = pltpu.SemaphoreType.DMA
    return pl.pallas_call(
        front_kernel,
        out_shape=(
            jax.ShapeDtypeStruct((x_rows + 2 * RADIUS, y_rows, z_rows), jnp.float32),
            jax.ShapeDtypeStruct((x_rows + 2 * RADIUS + 2, y_rows, z_rows), jnp.float32),
        ),
        in_specs=[
            pl.BlockSpec(memory_space=pltpu.SMEM),
            pl.BlockSpec(memory_space=pltpu.VMEM),
        ],
        out_specs=(pl.BlockSpec(memory_space=pl.ANY), pl.BlockSpec(memory_space=pl.ANY)),
        scratch_shapes=[
            pltpu.VMEM((groups, rows + 2, y_rows, z_rows), jnp.float32),
            pltpu.VMEM(shape, jnp.float32),
            pltpu.VMEM(shape, jnp.float32),
            pltpu.VMEM(shape, jnp.float32),
            pltpu.VMEM((RADIUS + 1, y_rows, z_rows), jnp.float32),
            dma((groups,)),
            dma((groups,)),
            dma((2,)),
            dma((2, groups)),
            dma((groups,)),
            dma((groups,)),
            dma((halos, groups)),
            dma((halos,)),
            dma((7,)),
            dma((2,)),
            dma((2,)),
        ],
        compiler_params=pltpu.CompilerParams(collective_id=0, has_side_effects=True),
    )(pairings, own)


def shifted(value, offset, axis):
    length = value.shape[axis]
    rolled = pltpu.roll(value, (-offset) % length, axis)
    index = lax.broadcasted_iota(jnp.int32, value.shape, axis) + offset
    return jnp.where((index >= 0) & (index < length), rolled, 0.0)


PAD = 8


def post_kernel(
    drive_hbm, own_ref, wz_ref, vel_ref, adv_ref, own_pad, force_ref, pass_ref, vel_buf, adv_buf, sems,
    drive_ref, own_sems, drive_sems,
):
    extended, y_rows, z_rows = drive_ref.shape
    x_rows = vel_ref.shape[1]
    padded = y_rows + 2 * PAD
    taps = gauss_taps(RADIUS)
    zeros = jnp.zeros((PAD, z_rows), jnp.float32)

    def inner(r, offset=0):
        return (r, pl.ds(PAD + offset, y_rows))

    def own_copy(r):
        return pltpu.make_async_copy(own_ref.at[r], own_pad.at[inner(r)], own_sems.at[r])

    def drive_copy(r):
        return pltpu.make_async_copy(drive_hbm.at[r], drive_ref.at[r], drive_sems.at[r])

    def start(r, carry):
        own_copy(r).start()
        return carry

    def fill(r, carry):
        own_pad[r, pl.ds(0, PAD)] = zeros
        own_pad[r, pl.ds(PAD + y_rows, PAD)] = zeros
        return carry

    lax.fori_loop(0, own_ref.shape[0], fill, 0)
    lax.fori_loop(0, own_ref.shape[0], start, 0)

    def start_drive(r, carry):
        drive_copy(r).start()
        return carry

    lax.fori_loop(0, extended, start_drive, 0)
    own_copy(0).wait()
    own_copy(1).wait()

    def plane(c, r, count):
        return pl.ds(pl.multiple_of((c * count + r) * y_rows, 8), y_rows)

    def force_row(r, carry):
        own_copy(r + 2).wait()
        drive_copy(r).wait()
        value = own_pad[inner(r + 1)]
        drive = drive_ref[r]
        force_ref[plane(0, r, extended)] = drive * ((own_pad[inner(r + 2)] - own_pad[inner(r)]) * 0.5)
        force_ref[plane(1, r, extended)] = drive * (
            (own_pad[inner(r + 1, 1)] - own_pad[inner(r + 1, -1)]) * 0.5
        )
        force_ref[plane(2, r, extended)] = drive * (
            (shifted(value, 1, 1) - shifted(value, -1, 1)) * 0.5
        )
        return carry

    lax.fori_loop(0, extended, force_row, 0)

    def slot(c, x):
        return pl.multiple_of((c * x_rows + x) * padded, 8)

    def x_pass(x, carry):
        for c in range(3):
            acc = taps[RADIUS] * force_ref[plane(c, x + RADIUS, extended)]
            for t in range(RADIUS):
                pair = force_ref[plane(c, x + t, extended)] + force_ref[plane(c, x + 2 * RADIUS - t, extended)]
                acc = acc + taps[t] * pair
            base = slot(c, x)
            pass_ref[pl.ds(base, PAD)] = zeros
            pass_ref[pl.ds(base + PAD, y_rows)] = acc
            pass_ref[pl.ds(base + PAD + y_rows, PAD)] = zeros
        return carry

    lax.fori_loop(0, x_rows, x_pass, 0)
    wz = wz_ref[...]
    chunk = 8 * padded
    chunks = pass_ref.shape[0] // chunk

    def z_pass(i, carry):
        rows = pl.ds(pl.multiple_of(i * chunk, 8), chunk)
        pass_ref[rows] = jnp.dot(
            pass_ref[rows], wz, precision=lax.Precision.HIGH,
            preferred_element_type=jnp.float32,
        )
        return carry

    lax.fori_loop(0, chunks, z_pass, 0)

    def out_row(x, carry):
        r = x + RADIUS + 1
        value = own_pad[inner(r)]
        change = None
        for c in range(3):
            base = slot(c, x) + PAD - RADIUS
            acc = taps[RADIUS] * pass_ref[pl.ds(base + RADIUS, y_rows)]
            for t in range(RADIUS):
                pair = pass_ref[pl.ds(base + t, y_rows)] + pass_ref[pl.ds(base + 2 * RADIUS - t, y_rows)]
                acc = acc + taps[t] * pair
            speed = step_scale * acc
            vel_buf[c, x] = speed
            if c == 0:
                backward = value - own_pad[inner(r - 1)]
                forward = own_pad[inner(r + 1)] - value
            elif c == 1:
                backward = value - own_pad[inner(r, -1)]
                forward = own_pad[inner(r, 1)] - value
            else:
                backward = value - shifted(value, -1, 1)
                forward = shifted(value, 1, 1) - value
            part = jnp.maximum(speed, 0.0) * backward + jnp.minimum(speed, 0.0) * forward
            change = part if change is None else change + part
        adv_buf[x] = value - change
        row = pl.ds(x, 1)
        pltpu.make_async_copy(vel_buf.at[:, row], vel_ref.at[:, row], sems.at[0]).start()
        pltpu.make_async_copy(adv_buf.at[row], adv_ref.at[row], sems.at[1]).start()
        return carry

    lax.fori_loop(0, x_rows, out_row, 0)
    pltpu.make_async_copy(vel_buf, vel_ref, sems.at[0]).wait()
    pltpu.make_async_copy(adv_buf, adv_ref, sems.at[1]).wait()


def band(length, taps):
    radius = len(taps) // 2
    matrix = np.zeros((length, length), np.float32)
    for i in range(length):
        for t in range(-radius, radius + 1):
            if 0 <= i + t < length:
                matrix[i, i + t] = taps[t + radius]
    return matrix


def post_stage(drive_ext, own_ext):
    extended, y_rows, z_rows = drive_ext.shape
    x_rows = extended - 2 * RADIUS
    taps = gauss_taps(RADIUS)
    wz = jnp.asarray(band(z_rows, taps).T)
    vmem = pl.BlockSpec(memory_space=pltpu.VMEM)
    return pl.pallas_call(
        post_kernel,
        out_shape=(
            jax.ShapeDtypeStruct((3, x_rows, y_rows, z_rows), jnp.float32),
            jax.ShapeDtypeStruct((x_rows, y_rows, z_rows), jnp.float32),
        ),
        in_specs=[pl.BlockSpec(memory_space=pl.ANY), pl.BlockSpec(memory_space=pl.ANY), vmem],
        out_specs=(pl.BlockSpec(memory_space=pl.ANY), pl.BlockSpec(memory_space=pl.ANY)),
        scratch_shapes=[
            pltpu.VMEM((extended + 2, y_rows + 2 * PAD, z_rows), jnp.float32),
            pltpu.VMEM((3 * extended * y_rows, z_rows), jnp.float32),
            pltpu.VMEM((3 * x_rows * (y_rows + 2 * PAD), z_rows), jnp.float32),
            pltpu.VMEM((3, x_rows, y_rows, z_rows), jnp.float32),
            pltpu.VMEM((x_rows, y_rows, z_rows), jnp.float32),
            pltpu.SemaphoreType.DMA((2,)),
            pltpu.VMEM((extended, y_rows, z_rows), jnp.float32),
            pltpu.SemaphoreType.DMA((extended + 2,)),
            pltpu.SemaphoreType.DMA((extended,)),
        ],
    )(drive_ext, own_ext, wz)


def shards(images, pairings):
    weights = gauss_taps(RADIUS)
    groups = lax.axis_size("img")
    own = images[0]
    x_rows, y_rows, _ = own.shape
    drive_ext, own_ext = front_stage(own, pairings, groups)
    velocity, advected = post_stage(drive_ext, own_ext)
    return (advected[None], velocity[None])


def solution(mesh):
    return jax.shard_map(
        shards,
        mesh=mesh,
        in_specs=(P("img", "space", None, None), P()),
        out_specs=(P("img", "space", None, None), P("img", None, "space", None, None)),
        check_vma=False,
    )
```

```python
import math

import jax
import numpy as np
import jax.numpy as jnp
from jax import lax
from jax.experimental import pallas as pl
from jax.experimental.pallas import tpu as pltpu
from jax.sharding import PartitionSpec as P

RADIUS = 4
PAIRINGS = 3

gauss_sigma = 1.5
step_scale = 8.0
floor_product = 0.25
floor_variance = 0.5


def gauss_taps(radius):
    raw_taps = [
        math.exp(-(offset * offset) / (2.0 * gauss_sigma * gauss_sigma))
        for offset in range(-radius, radius + 1)
    ]
    total_weight = sum(raw_taps)
    return [raw_weight / total_weight for raw_weight in raw_taps]


def halo_rows(value, width):
    peers = lax.axis_size("space")
    up = [(i, i + 1) for i in range(peers - 1)]
    down = [(i + 1, i) for i in range(peers - 1)]
    before = lax.ppermute(value[-width:], "space", up)
    after = lax.ppermute(value[:width], "space", down)
    return jnp.concatenate([before, value, after], axis=0)


def padded_along(volume, dimension, margin):
    widths = [(0, 0)] * volume.ndim
    widths[dimension] = (margin, margin)
    return jnp.pad(volume, widths)


def window(padded, dimension, offset, length):
    return lax.slice_in_dim(padded, offset, offset + length, axis=dimension)


def central(volume, dimension):
    length = volume.shape[dimension]
    padded = padded_along(volume, dimension, 1)
    return (window(padded, dimension, 2, length) - window(padded, dimension, 0, length)) * 0.5


def smooth_along(volume, dimension, weights):
    length = volume.shape[dimension]
    padded = padded_along(volume, dimension, len(weights) // 2)
    result = weights[0] * window(padded, dimension, 0, length)
    for tap_index in range(1, len(weights)):
        result = result + weights[tap_index] * window(padded, dimension, tap_index, length)
    return result


def smooth_rows(extended, weights):
    length = extended.shape[1] - len(weights) + 1
    result = weights[0] * window(extended, 1, 0, length)
    for tap_index in range(1, len(weights)):
        result = result + weights[tap_index] * window(extended, 1, tap_index, length)
    return result


def box_rows(volume):
    sx = volume[:-2] + volume[1:-1] + volume[2:]
    last = sx.shape[1] - 1
    row = lax.broadcasted_iota(jnp.int32, sx.shape, 1)
    before = jnp.where(row >= 1, pltpu.roll(sx, 1, 1), 0.0)
    after = jnp.where(row < last, pltpu.roll(sx, last, 1), 0.0)
    return (before + sx + after) / 9.0


def pair_terms(g, pair_ref, stack_ref, mean_ref, spread_ref):
    own = stack_ref[g]
    mean_own = mean_ref[g]
    spread_own = spread_ref[g]
    center_own = own[1:-1] - mean_own
    guarded_spread = jnp.maximum(spread_own, floor_variance)
    drive_sum = None
    for pairing_row in range(PAIRINGS):
        h = pair_ref[pairing_row, g]
        partner = stack_ref[h]
        mean_partner = mean_ref[h]
        spread_partner = spread_ref[h]
        cross_term = box_rows(own * partner) - mean_own * mean_partner
        factor = 2.0 * cross_term / jnp.maximum(spread_own * spread_partner, floor_product)
        ratio_term = cross_term / guarded_spread
        pair_term = factor * (partner[1:-1] - mean_partner - ratio_term * center_own)
        drive_sum = pair_term if drive_sum is None else drive_sum + pair_term
    return drive_sum


def row_groups(first, count, rows):
    groups = []
    for r in range(first, first + count):
        owner = r // rows
        if groups and groups[-1][0] == owner:
            groups[-1][2] += 1
        else:
            groups.append([owner, r - owner * rows, 1, r - first])
    return groups


def front_kernel(
    pair_ref, own_ref, drive_ref, ext_ref, stack_ref, mean_ref, spread_ref, out_ref, zero_ref,
    send_a, recv_a, send_h, recv_h, send_b, recv_b, send_c, recv_c, local_sem, send_o, recv_o,
):
    mesh = pl.DeviceIdType.MESH
    groups, width, y_rows, z_rows = stack_ref.shape
    rows = width - 2
    x_rows = own_ref.shape[0]
    spaces = lax.axis_size("space")
    me = lax.axis_index("img")
    s = lax.axis_index("space")
    has_lo = (s + spaces - 1) // spaces
    has_hi = (2 * spaces - 2 - s) // spaces

    barrier = pltpu.get_barrier_semaphore()
    for offset in (-1, 0, 1):
        exists = {-1: s > 0, 0: s >= 0, 1: s < spaces - 1}[offset]
        for g in range(groups):
            @pl.when(exists & ((offset != 0) | (me != g)))
            def _():
                pl.semaphore_signal(barrier, inc=1, device_id=(g, (s + offset + spaces) % spaces), device_id_type=mesh)
    pl.semaphore_wait(barrier, groups * (1 + has_lo + has_hi) - 1)

    zero_ref[...] = jnp.zeros(zero_ref.shape, jnp.float32)
    margin = RADIUS + 1

    def own_halo(wait):
        copies = [
            (s < spaces - 1, own_ref.at[pl.ds(x_rows - margin, margin)], ext_ref.at[pl.ds(0, margin)],
             0, (s + 1) % spaces),
            (s > 0, own_ref.at[pl.ds(0, margin)], ext_ref.at[pl.ds(x_rows + margin, margin)],
             1, (s + spaces - 1) % spaces),
        ]
        for exists, src, dst, index, target in copies:
            @pl.when(exists)
            def _():
                copy = pltpu.make_async_remote_copy(
                    src, dst, send_o.at[index], recv_o.at[index],
                    device_id=(me, target), device_id_type=mesh,
                )
                if wait:
                    copy.wait_send()
                else:
                    copy.start()
        local = [
            (s >= 0, own_ref, ext_ref.at[pl.ds(margin, x_rows)], 2),
            (s == 0, zero_ref, ext_ref.at[pl.ds(0, margin)], 3),
            (s == spaces - 1, zero_ref, ext_ref.at[pl.ds(x_rows + margin, margin)], 4),
        ]
        for exists, src, dst, index in local:
            @pl.when(exists)
            def _():
                copy = pltpu.make_async_copy(src, dst, local_sem.at[index])
                if wait:
                    copy.wait()
                else:
                    copy.start()

    own_halo(False)

    def piece(t):
        lo = max(t * rows - 1, 0)
        hi = min(t * rows + rows + 1, x_rows)
        return own_ref.at[pl.ds(lo, hi - lo)], lo - (t * rows - 1), hi - lo

    def piece_copy(t, src_image):
        src, dst_lo, count = piece(t)
        dst = stack_ref.at[src_image, pl.ds(dst_lo, count)]
        return src, dst

    def forward_copy(t_dyn, wait):
        for kind in range(3):
            cond = {0: t_dyn == 0, 1: t_dyn == groups - 1, 2: (t_dyn > 0) & (t_dyn < groups - 1)}[kind]

            @pl.when(cond & (t_dyn != me))
            def _():
                if kind == 0:
                    src, dst_lo, count = own_ref.at[pl.ds(0, rows + 1)], 1, rows + 1
                elif kind == 1:
                    src, dst_lo, count = own_ref.at[pl.ds(x_rows - rows - 1, rows + 1)], 0, rows + 1
                else:
                    src, dst_lo, count = own_ref.at[pl.ds(t_dyn * rows - 1, rows + 2)], 0, rows + 2
                copy = pltpu.make_async_remote_copy(
                    src, stack_ref.at[me, pl.ds(dst_lo, count)], send_a.at[t_dyn], recv_a.at[me],
                    device_id=(t_dyn, s), device_id_type=mesh,
                )
                if wait:
                    copy.wait_send()
                else:
                    copy.start()

    for t in range(groups):
        src, dst = piece_copy(t, me)

        @pl.when(me == t)
        def _():
            pltpu.make_async_copy(src, dst, local_sem.at[0]).start()

    for i in range(1, groups):
        forward_copy((me + i) % groups, False)

    @pl.when(s < spaces - 1)
    def _():
        pltpu.make_async_remote_copy(
            own_ref.at[pl.ds(x_rows - 1, 1)], stack_ref.at[me, pl.ds(0, 1)],
            send_h.at[0], recv_h.at[0, me], device_id=(0, (s + 1) % spaces), device_id_type=mesh,
        ).start()

    @pl.when(s > 0)
    def _():
        pltpu.make_async_remote_copy(
            own_ref.at[pl.ds(0, 1)], stack_ref.at[me, pl.ds(width - 1, 1)],
            send_h.at[1], recv_h.at[1, me], device_id=(groups - 1, (s + spaces - 1) % spaces), device_id_type=mesh,
        ).start()

    def stats(g):
        value = stack_ref[g]
        mean = box_rows(value)
        mean_ref[g] = mean
        spread_ref[g] = box_rows(value * value) - mean * mean

    @pl.when((me == 0) & (s == 0))
    def _():
        stack_ref[:, 0] = jnp.zeros((groups, y_rows, z_rows), jnp.float32)

    @pl.when((me == groups - 1) & (s == spaces - 1))
    def _():
        stack_ref[:, width - 1] = jnp.zeros((groups, y_rows, z_rows), jnp.float32)

    def arrive(i, carry):
        g = (me + groups - i) % groups

        @pl.when(i == 0)
        def _():
            for t in range(groups):
                src, dst = piece_copy(t, me)

                @pl.when(me == t)
                def _():
                    pltpu.make_async_copy(src, dst, local_sem.at[0]).wait()

        @pl.when(i != 0)
        def _():
            for t in range(groups):
                src, dst = piece_copy(t, 0)

                @pl.when(me == t)
                def _():
                    pltpu.make_async_remote_copy(
                        src, stack_ref.at[g, pl.ds(piece(t)[1], piece(t)[2])],
                        send_a.at[0], recv_a.at[g], device_id=(g, s), device_id_type=mesh,
                    ).wait_recv()

        @pl.when((me == 0) & (s > 0))
        def _():
            pltpu.make_async_remote_copy(
                own_ref.at[pl.ds(0, 1)], stack_ref.at[g, pl.ds(0, 1)],
                send_h.at[0], recv_h.at[0, g], device_id=(0, s), device_id_type=mesh,
            ).wait_recv()

        @pl.when((me == groups - 1) & (s < spaces - 1))
        def _():
            pltpu.make_async_remote_copy(
                own_ref.at[pl.ds(0, 1)], stack_ref.at[g, pl.ds(width - 1, 1)],
                send_h.at[1], recv_h.at[1, g], device_id=(0, s), device_id_type=mesh,
            ).wait_recv()

        stats(g)
        return carry

    lax.fori_loop(0, groups, arrive, 0)

    below = row_groups(x_rows - RADIUS, RADIUS, rows)
    above = row_groups(0, RADIUS, rows)

    def main_copy(g):
        src = out_ref.at[g]
        dst = drive_ref.at[pl.ds(RADIUS + me * rows, rows)]
        return src, dst

    def halo_copies(g):
        copies = []
        for index, (owner, src_lo, count, dst_lo) in enumerate(below):
            copies.append((owner, s < spaces - 1, 1, index, out_ref.at[g, pl.ds(src_lo, count)],
                           drive_ref.at[pl.ds(dst_lo, count)]))
        for index, (owner, src_lo, count, dst_lo) in enumerate(above):
            copies.append((owner, s > 0, -1, len(below) + index, out_ref.at[g, pl.ds(src_lo, count)],
                           drive_ref.at[pl.ds(x_rows + RADIUS + dst_lo, count)]))
        return copies

    def pairs(i, carry):
        g = (me + i) % groups
        out_ref[g] = pair_terms(g, pair_ref, stack_ref, mean_ref, spread_ref)
        src, dst = main_copy(g)

        @pl.when(me == g)
        def _():
            pltpu.make_async_copy(src, dst, local_sem.at[1]).start()

        @pl.when(me != g)
        def _():
            pltpu.make_async_remote_copy(
                src, dst, send_b.at[g], recv_b.at[me], device_id=(g, s), device_id_type=mesh
            ).start()

        for owner, exists, offset, index, hsrc, hdst in halo_copies(g):
            @pl.when((me == owner) & exists)
            def _():
                pltpu.make_async_remote_copy(
                    hsrc, hdst, send_c.at[index, g], recv_c.at[index],
                    device_id=(g, (s + offset + spaces) % spaces), device_id_type=mesh,
                ).start()
        return carry

    lax.fori_loop(0, groups, pairs, 0)

    @pl.when(s == 0)
    def _():
        pltpu.make_async_copy(zero_ref.at[pl.ds(0, RADIUS)], drive_ref.at[pl.ds(0, RADIUS)], local_sem.at[5]).start()

    @pl.when(s == spaces - 1)
    def _():
        pltpu.make_async_copy(
            zero_ref.at[pl.ds(0, RADIUS)], drive_ref.at[pl.ds(x_rows + RADIUS, RADIUS)], local_sem.at[6]
        ).start()

    for i in range(1, groups):
        forward_copy((me + i) % groups, True)

    @pl.when(s < spaces - 1)
    def _():
        pltpu.make_async_remote_copy(
            own_ref.at[pl.ds(x_rows - 1, 1)], stack_ref.at[me, pl.ds(0, 1)],
            send_h.at[0], recv_h.at[0, me], device_id=(0, (s + 1) % spaces), device_id_type=mesh,
        ).wait_send()

    @pl.when(s > 0)
    def _():
        pltpu.make_async_remote_copy(
            own_ref.at[pl.ds(0, 1)], stack_ref.at[me, pl.ds(width - 1, 1)],
            send_h.at[1], recv_h.at[1, me], device_id=(groups - 1, (s + spaces - 1) % spaces), device_id_type=mesh,
        ).wait_send()

    for g in range(groups):
        src, dst = main_copy(g)

        @pl.when(me == g)
        def _():
            pltpu.make_async_copy(src, dst, local_sem.at[1]).wait()

        @pl.when(me != g)
        def _():
            pltpu.make_async_remote_copy(
                src, dst, send_b.at[g], recv_b.at[me], device_id=(g, s), device_id_type=mesh
            ).wait_send()

        for owner, exists, offset, index, hsrc, hdst in halo_copies(g):
            @pl.when((me == owner) & exists)
            def _():
                pltpu.make_async_remote_copy(
                    hsrc, hdst, send_c.at[index, g], recv_c.at[index],
                    device_id=(g, (s + offset + spaces) % spaces), device_id_type=mesh,
                ).wait_send()

    for t in range(groups):
        @pl.when(me != t)
        def _():
            pltpu.make_async_remote_copy(
                out_ref.at[0], drive_ref.at[pl.ds(RADIUS + t * rows, rows)],
                send_b.at[0], recv_b.at[t], device_id=(t, s), device_id_type=mesh,
            ).wait_recv()

    for owner, exists, offset, index, hsrc, hdst in halo_copies(0):
        @pl.when(((offset == 1) & (s > 0)) | ((offset == -1) & (s < spaces - 1)))
        def _():
            pltpu.make_async_remote_copy(
                hsrc, hdst, send_c.at[index, 0], recv_c.at[index],
                device_id=(owner, s), device_id_type=mesh,
            ).wait_recv()

    own_halo(True)
    for exists, dst, index in (
        (s > 0, ext_ref.at[pl.ds(0, margin)], 0),
        (s < spaces - 1, ext_ref.at[pl.ds(x_rows + margin, margin)], 1),
    ):
        @pl.when(exists)
        def _():
            pltpu.make_async_remote_copy(
                own_ref.at[pl.ds(0, margin)], dst, send_o.at[index], recv_o.at[index],
                device_id=(me, s), device_id_type=mesh,
            ).wait_recv()

    @pl.when(s == 0)
    def _():
        pltpu.make_async_copy(zero_ref.at[pl.ds(0, RADIUS)], drive_ref.at[pl.ds(0, RADIUS)], local_sem.at[5]).wait()

    @pl.when(s == spaces - 1)
    def _():
        pltpu.make_async_copy(
            zero_ref.at[pl.ds(0, RADIUS)], drive_ref.at[pl.ds(x_rows + RADIUS, RADIUS)], local_sem.at[6]
        ).wait()


def front_stage(own, pairings, groups):
    x_rows, y_rows, z_rows = own.shape
    rows = x_rows // groups
    shape = (groups, rows, y_rows, z_rows)
    halos = len(row_groups(x_rows - RADIUS, RADIUS, rows)) + len(row_groups(0, RADIUS, rows))
    dma = pltpu.SemaphoreType.DMA
    return pl.pallas_call(
        front_kernel,
        out_shape=(
            jax.ShapeDtypeStruct((x_rows + 2 * RADIUS, y_rows, z_rows), jnp.float32),
            jax.ShapeDtypeStruct((x_rows + 2 * RADIUS + 2, y_rows, z_rows), jnp.float32),
        ),
        in_specs=[
            pl.BlockSpec(memory_space=pltpu.SMEM),
            pl.BlockSpec(memory_space=pltpu.VMEM),
        ],
        out_specs=(pl.BlockSpec(memory_space=pl.ANY), pl.BlockSpec(memory_space=pl.ANY)),
        scratch_shapes=[
            pltpu.VMEM((groups, rows + 2, y_rows, z_rows), jnp.float32),
            pltpu.VMEM(shape, jnp.float32),
            pltpu.VMEM(shape, jnp.float32),
            pltpu.VMEM(shape, jnp.float32),
            pltpu.VMEM((RADIUS + 1, y_rows, z_rows), jnp.float32),
            dma((groups,)),
            dma((groups,)),
            dma((2,)),
            dma((2, groups)),
            dma((groups,)),
            dma((groups,)),
            dma((halos, groups)),
            dma((halos,)),
            dma((7,)),
            dma((2,)),
            dma((2,)),
        ],
        compiler_params=pltpu.CompilerParams(collective_id=0, has_side_effects=True),
    )(pairings, own)


def shifted(value, offset, axis):
    length = value.shape[axis]
    rolled = pltpu.roll(value, (-offset) % length, axis)
    index = lax.broadcasted_iota(jnp.int32, value.shape, axis) + offset
    return jnp.where((index >= 0) & (index < length), rolled, 0.0)


PAD = 8


def post_kernel(
    drive_ref, own_ref, wz_ref, vel_ref, adv_ref, own_pad, force_ref, pass_ref, vel_buf, adv_buf, sems,
    compact_ref,
):
    extended, y_rows, z_rows = drive_ref.shape
    x_rows = vel_ref.shape[1]
    padded = y_rows + 2 * PAD
    taps = gauss_taps(RADIUS)
    zeros = jnp.zeros((PAD, z_rows), jnp.float32)

    def inner(r, offset=0):
        return (r, pl.ds(PAD + offset, y_rows))

    def fill(r, carry):
        own_pad[r, pl.ds(0, PAD)] = zeros
        own_pad[r, pl.ds(PAD + y_rows, PAD)] = zeros
        own_pad[inner(r)] = own_ref[r]
        return carry

    lax.fori_loop(0, own_ref.shape[0], fill, 0)

    def plane(c, r, count):
        return pl.ds(pl.multiple_of((c * count + r) * y_rows, 8), y_rows)

    def force_row(r, carry):
        value = own_pad[inner(r + 1)]
        drive = drive_ref[r]
        force_ref[plane(0, r, extended)] = drive * ((own_pad[inner(r + 2)] - own_pad[inner(r)]) * 0.5)
        force_ref[plane(1, r, extended)] = drive * (
            (own_pad[inner(r + 1, 1)] - own_pad[inner(r + 1, -1)]) * 0.5
        )
        force_ref[plane(2, r, extended)] = drive * (
            (shifted(value, 1, 1) - shifted(value, -1, 1)) * 0.5
        )
        return carry

    lax.fori_loop(0, extended, force_row, 0)

    def slot(c, x):
        return pl.multiple_of((c * x_rows + x) * padded, 8)

    def x_pass(x, carry):
        for c in range(3):
            acc = taps[RADIUS] * force_ref[plane(c, x + RADIUS, extended)]
            for t in range(RADIUS):
                pair = force_ref[plane(c, x + t, extended)] + force_ref[plane(c, x + 2 * RADIUS - t, extended)]
                acc = acc + taps[t] * pair
            base = slot(c, x)
            pass_ref[pl.ds(base, PAD)] = zeros
            pass_ref[pl.ds(base + PAD + y_rows, PAD)] = zeros
            compact_ref[plane(c, x, x_rows)] = acc
        return carry

    lax.fori_loop(0, x_rows, x_pass, 0)
    wz = wz_ref[...]
    per_chunk = 8
    chunk = per_chunk * y_rows
    chunks = compact_ref.shape[0] // chunk

    def z_pass(i, carry):
        rows = pl.ds(pl.multiple_of(i * chunk, 8), chunk)
        result = jnp.dot(
            compact_ref[rows], wz, precision=lax.Precision.HIGH,
            preferred_element_type=jnp.float32,
        )
        for k in range(per_chunk):
            base = pl.multiple_of((i * per_chunk + k) * padded + PAD, 8)
            pass_ref[pl.ds(base, y_rows)] = result[k * y_rows:(k + 1) * y_rows]
        return carry

    lax.fori_loop(0, chunks, z_pass, 0)

    def out_row(x, carry):
        r = x + RADIUS + 1
        value = own_pad[inner(r)]
        change = None
        for c in range(3):
            base = slot(c, x) + PAD - RADIUS
            acc = taps[RADIUS] * pass_ref[pl.ds(base + RADIUS, y_rows)]
            for t in range(RADIUS):
                pair = pass_ref[pl.ds(base + t, y_rows)] + pass_ref[pl.ds(base + 2 * RADIUS - t, y_rows)]
                acc = acc + taps[t] * pair
            speed = step_scale * acc
            vel_buf[c, x] = speed
            if c == 0:
                backward = value - own_pad[inner(r - 1)]
                forward = own_pad[inner(r + 1)] - value
            elif c == 1:
                backward = value - own_pad[inner(r, -1)]
                forward = own_pad[inner(r, 1)] - value
            else:
                backward = value - shifted(value, -1, 1)
                forward = shifted(value, 1, 1) - value
            part = jnp.maximum(speed, 0.0) * backward + jnp.minimum(speed, 0.0) * forward
            change = part if change is None else change + part
        adv_buf[x] = value - change
        row = pl.ds(x, 1)
        pltpu.make_async_copy(vel_buf.at[:, row], vel_ref.at[:, row], sems.at[0]).start()
        pltpu.make_async_copy(adv_buf.at[row], adv_ref.at[row], sems.at[1]).start()
        return carry

    lax.fori_loop(0, x_rows, out_row, 0)
    pltpu.make_async_copy(vel_buf, vel_ref, sems.at[0]).wait()
    pltpu.make_async_copy(adv_buf, adv_ref, sems.at[1]).wait()


def band(length, taps):
    radius = len(taps) // 2
    matrix = np.zeros((length, length), np.float32)
    for i in range(length):
        for t in range(-radius, radius + 1):
            if 0 <= i + t < length:
                matrix[i, i + t] = taps[t + radius]
    return matrix


def post_stage(drive_ext, own_ext):
    extended, y_rows, z_rows = drive_ext.shape
    x_rows = extended - 2 * RADIUS
    taps = gauss_taps(RADIUS)
    wz = jnp.asarray(band(z_rows, taps).T)
    vmem = pl.BlockSpec(memory_space=pltpu.VMEM)
    return pl.pallas_call(
        post_kernel,
        out_shape=(
            jax.ShapeDtypeStruct((3, x_rows, y_rows, z_rows), jnp.float32),
            jax.ShapeDtypeStruct((x_rows, y_rows, z_rows), jnp.float32),
        ),
        in_specs=[vmem] * 3,
        out_specs=(pl.BlockSpec(memory_space=pl.ANY), pl.BlockSpec(memory_space=pl.ANY)),
        scratch_shapes=[
            pltpu.VMEM((extended + 2, y_rows + 2 * PAD, z_rows), jnp.float32),
            pltpu.VMEM((3 * extended * y_rows, z_rows), jnp.float32),
            pltpu.VMEM((3 * x_rows * (y_rows + 2 * PAD), z_rows), jnp.float32),
            pltpu.VMEM((3, x_rows, y_rows, z_rows), jnp.float32),
            pltpu.VMEM((x_rows, y_rows, z_rows), jnp.float32),
            pltpu.SemaphoreType.DMA((2,)),
            pltpu.VMEM((3 * x_rows * y_rows, z_rows), jnp.float32),
        ],
    )(drive_ext, own_ext, wz)


def shards(images, pairings):
    weights = gauss_taps(RADIUS)
    groups = lax.axis_size("img")
    own = images[0]
    x_rows, y_rows, _ = own.shape
    drive_ext, own_ext = front_stage(own, pairings, groups)
    velocity, advected = post_stage(drive_ext, own_ext)
    return (advected[None], velocity[None])


def solution(mesh):
    return jax.shard_map(
        shards,
        mesh=mesh,
        in_specs=(P("img", "space", None, None), P()),
        out_specs=(P("img", "space", None, None), P("img", None, "space", None, None)),
        check_vma=False,
    )
```

```python
import math

import jax
import numpy as np
import jax.numpy as jnp
from jax import lax
from jax.experimental import pallas as pl
from jax.experimental.pallas import tpu as pltpu
from jax.sharding import PartitionSpec as P

RADIUS = 4
PAIRINGS = 3

gauss_sigma = 1.5
step_scale = 8.0
floor_product = 0.25
floor_variance = 0.5


def gauss_taps(radius):
    raw_taps = [
        math.exp(-(offset * offset) / (2.0 * gauss_sigma * gauss_sigma))
        for offset in range(-radius, radius + 1)
    ]
    total_weight = sum(raw_taps)
    return [raw_weight / total_weight for raw_weight in raw_taps]


def halo_rows(value, width):
    peers = lax.axis_size("space")
    up = [(i, i + 1) for i in range(peers - 1)]
    down = [(i + 1, i) for i in range(peers - 1)]
    before = lax.ppermute(value[-width:], "space", up)
    after = lax.ppermute(value[:width], "space", down)
    return jnp.concatenate([before, value, after], axis=0)


def padded_along(volume, dimension, margin):
    widths = [(0, 0)] * volume.ndim
    widths[dimension] = (margin, margin)
    return jnp.pad(volume, widths)


def window(padded, dimension, offset, length):
    return lax.slice_in_dim(padded, offset, offset + length, axis=dimension)


def central(volume, dimension):
    length = volume.shape[dimension]
    padded = padded_along(volume, dimension, 1)
    return (window(padded, dimension, 2, length) - window(padded, dimension, 0, length)) * 0.5


def smooth_along(volume, dimension, weights):
    length = volume.shape[dimension]
    padded = padded_along(volume, dimension, len(weights) // 2)
    result = weights[0] * window(padded, dimension, 0, length)
    for tap_index in range(1, len(weights)):
        result = result + weights[tap_index] * window(padded, dimension, tap_index, length)
    return result


def smooth_rows(extended, weights):
    length = extended.shape[1] - len(weights) + 1
    result = weights[0] * window(extended, 1, 0, length)
    for tap_index in range(1, len(weights)):
        result = result + weights[tap_index] * window(extended, 1, tap_index, length)
    return result


def box_rows(volume):
    sx = volume[:-2] + volume[1:-1] + volume[2:]
    last = sx.shape[1] - 1
    row = lax.broadcasted_iota(jnp.int32, sx.shape, 1)
    before = jnp.where(row >= 1, pltpu.roll(sx, 1, 1), 0.0)
    after = jnp.where(row < last, pltpu.roll(sx, last, 1), 0.0)
    return (before + sx + after) * (1.0 / 9.0)


def pair_terms(g, pair_ref, stack_ref, mean_ref, spread_ref):
    own = stack_ref[g]
    mean_own = mean_ref[g]
    spread_own = spread_ref[g]
    center_own = own[1:-1] - mean_own
    inverse_spread = 1.0 / jnp.maximum(spread_own, floor_variance)
    drive_sum = None
    for pairing_row in range(PAIRINGS):
        h = pair_ref[pairing_row, g]
        partner = stack_ref[h]
        mean_partner = mean_ref[h]
        spread_partner = spread_ref[h]
        cross_term = box_rows(own * partner) - mean_own * mean_partner
        factor = 2.0 * cross_term / jnp.maximum(spread_own * spread_partner, floor_product)
        ratio_term = cross_term * inverse_spread
        pair_term = factor * (partner[1:-1] - mean_partner - ratio_term * center_own)
        drive_sum = pair_term if drive_sum is None else drive_sum + pair_term
    return drive_sum


def row_groups(first, count, rows):
    groups = []
    for r in range(first, first + count):
        owner = r // rows
        if groups and groups[-1][0] == owner:
            groups[-1][2] += 1
        else:
            groups.append([owner, r - owner * rows, 1, r - first])
    return groups


def front_kernel(
    pair_ref, own_ref, drive_ref, ext_ref, stack_ref, mean_ref, spread_ref, out_ref, zero_ref,
    send_a, recv_a, send_h, recv_h, send_b, recv_b, send_c, recv_c, local_sem, send_o, recv_o,
):
    mesh = pl.DeviceIdType.MESH
    groups, width, y_rows, z_rows = stack_ref.shape
    rows = width - 2
    x_rows = own_ref.shape[0]
    spaces = lax.axis_size("space")
    me = lax.axis_index("img")
    s = lax.axis_index("space")
    has_lo = (s + spaces - 1) // spaces
    has_hi = (2 * spaces - 2 - s) // spaces

    barrier = pltpu.get_barrier_semaphore()
    for offset in (-1, 0, 1):
        exists = {-1: s > 0, 0: s >= 0, 1: s < spaces - 1}[offset]
        for g in range(groups):
            @pl.when(exists & ((offset != 0) | (me != g)))
            def _():
                pl.semaphore_signal(barrier, inc=1, device_id=(g, (s + offset + spaces) % spaces), device_id_type=mesh)
    pl.semaphore_wait(barrier, groups * (1 + has_lo + has_hi) - 1)

    zero_ref[...] = jnp.zeros(zero_ref.shape, jnp.float32)
    margin = RADIUS + 1

    def own_halo(wait):
        copies = [
            (s < spaces - 1, own_ref.at[pl.ds(x_rows - margin, margin)], ext_ref.at[pl.ds(0, margin)],
             0, (s + 1) % spaces),
            (s > 0, own_ref.at[pl.ds(0, margin)], ext_ref.at[pl.ds(x_rows + margin, margin)],
             1, (s + spaces - 1) % spaces),
        ]
        for exists, src, dst, index, target in copies:
            @pl.when(exists)
            def _():
                copy = pltpu.make_async_remote_copy(
                    src, dst, send_o.at[index], recv_o.at[index],
                    device_id=(me, target), device_id_type=mesh,
                )
                if wait:
                    copy.wait_send()
                else:
                    copy.start()
        local = [
            (s >= 0, own_ref, ext_ref.at[pl.ds(margin, x_rows)], 2),
            (s == 0, zero_ref, ext_ref.at[pl.ds(0, margin)], 3),
            (s == spaces - 1, zero_ref, ext_ref.at[pl.ds(x_rows + margin, margin)], 4),
        ]
        for exists, src, dst, index in local:
            @pl.when(exists)
            def _():
                copy = pltpu.make_async_copy(src, dst, local_sem.at[index])
                if wait:
                    copy.wait()
                else:
                    copy.start()

    own_halo(False)

    def piece(t):
        lo = max(t * rows - 1, 0)
        hi = min(t * rows + rows + 1, x_rows)
        return own_ref.at[pl.ds(lo, hi - lo)], lo - (t * rows - 1), hi - lo

    def piece_copy(t, src_image):
        src, dst_lo, count = piece(t)
        dst = stack_ref.at[src_image, pl.ds(dst_lo, count)]
        return src, dst

    def forward_copy(t_dyn, wait):
        for kind in range(3):
            cond = {0: t_dyn == 0, 1: t_dyn == groups - 1, 2: (t_dyn > 0) & (t_dyn < groups - 1)}[kind]

            @pl.when(cond & (t_dyn != me))
            def _():
                if kind == 0:
                    src, dst_lo, count = own_ref.at[pl.ds(0, rows + 1)], 1, rows + 1
                elif kind == 1:
                    src, dst_lo, count = own_ref.at[pl.ds(x_rows - rows - 1, rows + 1)], 0, rows + 1
                else:
                    src, dst_lo, count = own_ref.at[pl.ds(t_dyn * rows - 1, rows + 2)], 0, rows + 2
                copy = pltpu.make_async_remote_copy(
                    src, stack_ref.at[me, pl.ds(dst_lo, count)], send_a.at[t_dyn], recv_a.at[me],
                    device_id=(t_dyn, s), device_id_type=mesh,
                )
                if wait:
                    copy.wait_send()
                else:
                    copy.start()

    for t in range(groups):
        src, dst = piece_copy(t, me)

        @pl.when(me == t)
        def _():
            pltpu.make_async_copy(src, dst, local_sem.at[0]).start()

    for i in range(1, groups):
        forward_copy((me + i) % groups, False)

    @pl.when(s < spaces - 1)
    def _():
        pltpu.make_async_remote_copy(
            own_ref.at[pl.ds(x_rows - 1, 1)], stack_ref.at[me, pl.ds(0, 1)],
            send_h.at[0], recv_h.at[0, me], device_id=(0, (s + 1) % spaces), device_id_type=mesh,
        ).start()

    @pl.when(s > 0)
    def _():
        pltpu.make_async_remote_copy(
            own_ref.at[pl.ds(0, 1)], stack_ref.at[me, pl.ds(width - 1, 1)],
            send_h.at[1], recv_h.at[1, me], device_id=(groups - 1, (s + spaces - 1) % spaces), device_id_type=mesh,
        ).start()

    def stats(g):
        value = stack_ref[g]
        mean = box_rows(value)
        mean_ref[g] = mean
        spread_ref[g] = box_rows(value * value) - mean * mean

    @pl.when((me == 0) & (s == 0))
    def _():
        stack_ref[:, 0] = jnp.zeros((groups, y_rows, z_rows), jnp.float32)

    @pl.when((me == groups - 1) & (s == spaces - 1))
    def _():
        stack_ref[:, width - 1] = jnp.zeros((groups, y_rows, z_rows), jnp.float32)

    def arrive(i, carry):
        g = (me + groups - i) % groups

        @pl.when(i == 0)
        def _():
            for t in range(groups):
                src, dst = piece_copy(t, me)

                @pl.when(me == t)
                def _():
                    pltpu.make_async_copy(src, dst, local_sem.at[0]).wait()

        @pl.when(i != 0)
        def _():
            for t in range(groups):
                src, dst = piece_copy(t, 0)

                @pl.when(me == t)
                def _():
                    pltpu.make_async_remote_copy(
                        src, stack_ref.at[g, pl.ds(piece(t)[1], piece(t)[2])],
                        send_a.at[0], recv_a.at[g], device_id=(g, s), device_id_type=mesh,
                    ).wait_recv()

        @pl.when((me == 0) & (s > 0))
        def _():
            pltpu.make_async_remote_copy(
                own_ref.at[pl.ds(0, 1)], stack_ref.at[g, pl.ds(0, 1)],
                send_h.at[0], recv_h.at[0, g], device_id=(0, s), device_id_type=mesh,
            ).wait_recv()

        @pl.when((me == groups - 1) & (s < spaces - 1))
        def _():
            pltpu.make_async_remote_copy(
                own_ref.at[pl.ds(0, 1)], stack_ref.at[g, pl.ds(width - 1, 1)],
                send_h.at[1], recv_h.at[1, g], device_id=(0, s), device_id_type=mesh,
            ).wait_recv()

        stats(g)
        return carry

    lax.fori_loop(0, groups, arrive, 0)

    below = row_groups(x_rows - RADIUS, RADIUS, rows)
    above = row_groups(0, RADIUS, rows)

    def main_copy(g):
        src = out_ref.at[g]
        dst = drive_ref.at[pl.ds(RADIUS + me * rows, rows)]
        return src, dst

    def halo_copies(g):
        copies = []
        for index, (owner, src_lo, count, dst_lo) in enumerate(below):
            copies.append((owner, s < spaces - 1, 1, index, out_ref.at[g, pl.ds(src_lo, count)],
                           drive_ref.at[pl.ds(dst_lo, count)]))
        for index, (owner, src_lo, count, dst_lo) in enumerate(above):
            copies.append((owner, s > 0, -1, len(below) + index, out_ref.at[g, pl.ds(src_lo, count)],
                           drive_ref.at[pl.ds(x_rows + RADIUS + dst_lo, count)]))
        return copies

    def pairs(i, carry):
        g = (me + i) % groups
        out_ref[g] = pair_terms(g, pair_ref, stack_ref, mean_ref, spread_ref)
        src, dst = main_copy(g)

        @pl.when(me == g)
        def _():
            pltpu.make_async_copy(src, dst, local_sem.at[1]).start()

        @pl.when(me != g)
        def _():
            pltpu.make_async_remote_copy(
                src, dst, send_b.at[g], recv_b.at[me], device_id=(g, s), device_id_type=mesh
            ).start()

        for owner, exists, offset, index, hsrc, hdst in halo_copies(g):
            @pl.when((me == owner) & exists)
            def _():
                pltpu.make_async_remote_copy(
                    hsrc, hdst, send_c.at[index, g], recv_c.at[index],
                    device_id=(g, (s + offset + spaces) % spaces), device_id_type=mesh,
                ).start()
        return carry

    lax.fori_loop(0, groups, pairs, 0)

    @pl.when(s == 0)
    def _():
        pltpu.make_async_copy(zero_ref.at[pl.ds(0, RADIUS)], drive_ref.at[pl.ds(0, RADIUS)], local_sem.at[5]).start()

    @pl.when(s == spaces - 1)
    def _():
        pltpu.make_async_copy(
            zero_ref.at[pl.ds(0, RADIUS)], drive_ref.at[pl.ds(x_rows + RADIUS, RADIUS)], local_sem.at[6]
        ).start()

    for i in range(1, groups):
        forward_copy((me + i) % groups, True)

    @pl.when(s < spaces - 1)
    def _():
        pltpu.make_async_remote_copy(
            own_ref.at[pl.ds(x_rows - 1, 1)], stack_ref.at[me, pl.ds(0, 1)],
            send_h.at[0], recv_h.at[0, me], device_id=(0, (s + 1) % spaces), device_id_type=mesh,
        ).wait_send()

    @pl.when(s > 0)
    def _():
        pltpu.make_async_remote_copy(
            own_ref.at[pl.ds(0, 1)], stack_ref.at[me, pl.ds(width - 1, 1)],
            send_h.at[1], recv_h.at[1, me], device_id=(groups - 1, (s + spaces - 1) % spaces), device_id_type=mesh,
        ).wait_send()

    for g in range(groups):
        src, dst = main_copy(g)

        @pl.when(me == g)
        def _():
            pltpu.make_async_copy(src, dst, local_sem.at[1]).wait()

        @pl.when(me != g)
        def _():
            pltpu.make_async_remote_copy(
                src, dst, send_b.at[g], recv_b.at[me], device_id=(g, s), device_id_type=mesh
            ).wait_send()

        for owner, exists, offset, index, hsrc, hdst in halo_copies(g):
            @pl.when((me == owner) & exists)
            def _():
                pltpu.make_async_remote_copy(
                    hsrc, hdst, send_c.at[index, g], recv_c.at[index],
                    device_id=(g, (s + offset + spaces) % spaces), device_id_type=mesh,
                ).wait_send()

    for t in range(groups):
        @pl.when(me != t)
        def _():
            pltpu.make_async_remote_copy(
                out_ref.at[0], drive_ref.at[pl.ds(RADIUS + t * rows, rows)],
                send_b.at[0], recv_b.at[t], device_id=(t, s), device_id_type=mesh,
            ).wait_recv()

    for owner, exists, offset, index, hsrc, hdst in halo_copies(0):
        @pl.when(((offset == 1) & (s > 0)) | ((offset == -1) & (s < spaces - 1)))
        def _():
            pltpu.make_async_remote_copy(
                hsrc, hdst, send_c.at[index, 0], recv_c.at[index],
                device_id=(owner, s), device_id_type=mesh,
            ).wait_recv()

    own_halo(True)
    for exists, dst, index in (
        (s > 0, ext_ref.at[pl.ds(0, margin)], 0),
        (s < spaces - 1, ext_ref.at[pl.ds(x_rows + margin, margin)], 1),
    ):
        @pl.when(exists)
        def _():
            pltpu.make_async_remote_copy(
                own_ref.at[pl.ds(0, margin)], dst, send_o.at[index], recv_o.at[index],
                device_id=(me, s), device_id_type=mesh,
            ).wait_recv()

    @pl.when(s == 0)
    def _():
        pltpu.make_async_copy(zero_ref.at[pl.ds(0, RADIUS)], drive_ref.at[pl.ds(0, RADIUS)], local_sem.at[5]).wait()

    @pl.when(s == spaces - 1)
    def _():
        pltpu.make_async_copy(
            zero_ref.at[pl.ds(0, RADIUS)], drive_ref.at[pl.ds(x_rows + RADIUS, RADIUS)], local_sem.at[6]
        ).wait()


def front_stage(own, pairings, groups):
    x_rows, y_rows, z_rows = own.shape
    rows = x_rows // groups
    shape = (groups, rows, y_rows, z_rows)
    halos = len(row_groups(x_rows - RADIUS, RADIUS, rows)) + len(row_groups(0, RADIUS, rows))
    dma = pltpu.SemaphoreType.DMA
    return pl.pallas_call(
        front_kernel,
        out_shape=(
            jax.ShapeDtypeStruct((x_rows + 2 * RADIUS, y_rows, z_rows), jnp.float32),
            jax.ShapeDtypeStruct((x_rows + 2 * RADIUS + 2, y_rows, z_rows), jnp.float32),
        ),
        in_specs=[
            pl.BlockSpec(memory_space=pltpu.SMEM),
            pl.BlockSpec(memory_space=pltpu.VMEM),
        ],
        out_specs=(pl.BlockSpec(memory_space=pl.ANY), pl.BlockSpec(memory_space=pl.ANY)),
        scratch_shapes=[
            pltpu.VMEM((groups, rows + 2, y_rows, z_rows), jnp.float32),
            pltpu.VMEM(shape, jnp.float32),
            pltpu.VMEM(shape, jnp.float32),
            pltpu.VMEM(shape, jnp.float32),
            pltpu.VMEM((RADIUS + 1, y_rows, z_rows), jnp.float32),
            dma((groups,)),
            dma((groups,)),
            dma((2,)),
            dma((2, groups)),
            dma((groups,)),
            dma((groups,)),
            dma((halos, groups)),
            dma((halos,)),
            dma((7,)),
            dma((2,)),
            dma((2,)),
        ],
        compiler_params=pltpu.CompilerParams(collective_id=0, has_side_effects=True),
    )(pairings, own)


def shifted(value, offset, axis):
    length = value.shape[axis]
    rolled = pltpu.roll(value, (-offset) % length, axis)
    index = lax.broadcasted_iota(jnp.int32, value.shape, axis) + offset
    return jnp.where((index >= 0) & (index < length), rolled, 0.0)


PAD = 8


def post_kernel(
    drive_ref, own_ref, wz_ref, vel_ref, adv_ref, own_pad, force_ref, pass_ref, vel_buf, adv_buf, sems,
    compact_ref,
):
    extended, y_rows, z_rows = drive_ref.shape
    x_rows = vel_ref.shape[1]
    padded = y_rows + 2 * PAD
    taps = gauss_taps(RADIUS)
    zeros = jnp.zeros((PAD, z_rows), jnp.float32)

    def inner(r, offset=0):
        return (r, pl.ds(PAD + offset, y_rows))

    def fill(r, carry):
        own_pad[r, pl.ds(0, PAD)] = zeros
        own_pad[r, pl.ds(PAD + y_rows, PAD)] = zeros
        own_pad[inner(r)] = own_ref[r]
        return carry

    lax.fori_loop(0, own_ref.shape[0], fill, 0)

    def plane(c, r, count):
        return pl.ds(pl.multiple_of((c * count + r) * y_rows, 8), y_rows)

    def force_row(r, carry):
        value = own_pad[inner(r + 1)]
        drive = drive_ref[r]
        force_ref[plane(0, r, extended)] = drive * ((own_pad[inner(r + 2)] - own_pad[inner(r)]) * 0.5)
        force_ref[plane(1, r, extended)] = drive * (
            (own_pad[inner(r + 1, 1)] - own_pad[inner(r + 1, -1)]) * 0.5
        )
        force_ref[plane(2, r, extended)] = drive * (
            (shifted(value, 1, 1) - shifted(value, -1, 1)) * 0.5
        )
        return carry

    lax.fori_loop(0, extended, force_row, 0)

    def slot(c, x):
        return pl.multiple_of((c * x_rows + x) * padded, 8)

    def x_pass(x, carry):
        for c in range(3):
            acc = taps[RADIUS] * force_ref[plane(c, x + RADIUS, extended)]
            for t in range(RADIUS):
                pair = force_ref[plane(c, x + t, extended)] + force_ref[plane(c, x + 2 * RADIUS - t, extended)]
                acc = acc + taps[t] * pair
            base = slot(c, x)
            pass_ref[pl.ds(base, PAD)] = zeros
            pass_ref[pl.ds(base + PAD + y_rows, PAD)] = zeros
            compact_ref[plane(c, x, x_rows)] = acc
        return carry

    lax.fori_loop(0, x_rows, x_pass, 0)
    wz = wz_ref[...]
    per_chunk = 8
    chunk = per_chunk * y_rows
    chunks = compact_ref.shape[0] // chunk

    def z_pass(i, carry):
        rows = pl.ds(pl.multiple_of(i * chunk, 8), chunk)
        result = jnp.dot(
            compact_ref[rows], wz, precision=lax.Precision.HIGH,
            preferred_element_type=jnp.float32,
        )
        for k in range(per_chunk):
            base = pl.multiple_of((i * per_chunk + k) * padded + PAD, 8)
            pass_ref[pl.ds(base, y_rows)] = result[k * y_rows:(k + 1) * y_rows]
        return carry

    lax.fori_loop(0, chunks, z_pass, 0)

    def out_row(x, carry):
        r = x + RADIUS + 1
        value = own_pad[inner(r)]
        change = None
        for c in range(3):
            base = slot(c, x) + PAD - RADIUS
            acc = taps[RADIUS] * pass_ref[pl.ds(base + RADIUS, y_rows)]
            for t in range(RADIUS):
                pair = pass_ref[pl.ds(base + t, y_rows)] + pass_ref[pl.ds(base + 2 * RADIUS - t, y_rows)]
                acc = acc + taps[t] * pair
            speed = step_scale * acc
            vel_buf[c, x] = speed
            if c == 0:
                backward = value - own_pad[inner(r - 1)]
                forward = own_pad[inner(r + 1)] - value
            elif c == 1:
                backward = value - own_pad[inner(r, -1)]
                forward = own_pad[inner(r, 1)] - value
            else:
                backward = value - shifted(value, -1, 1)
                forward = shifted(value, 1, 1) - value
            part = jnp.maximum(speed, 0.0) * backward + jnp.minimum(speed, 0.0) * forward
            change = part if change is None else change + part
        adv_buf[x] = value - change
        row = pl.ds(x, 1)
        pltpu.make_async_copy(vel_buf.at[:, row], vel_ref.at[:, row], sems.at[0]).start()
        pltpu.make_async_copy(adv_buf.at[row], adv_ref.at[row], sems.at[1]).start()
        return carry

    lax.fori_loop(0, x_rows, out_row, 0)
    pltpu.make_async_copy(vel_buf, vel_ref, sems.at[0]).wait()
    pltpu.make_async_copy(adv_buf, adv_ref, sems.at[1]).wait()


def band(length, taps):
    radius = len(taps) // 2
    matrix = np.zeros((length, length), np.float32)
    for i in range(length):
        for t in range(-radius, radius + 1):
            if 0 <= i + t < length:
                matrix[i, i + t] = taps[t + radius]
    return matrix


def post_stage(drive_ext, own_ext):
    extended, y_rows, z_rows = drive_ext.shape
    x_rows = extended - 2 * RADIUS
    taps = gauss_taps(RADIUS)
    wz = jnp.asarray(band(z_rows, taps).T)
    vmem = pl.BlockSpec(memory_space=pltpu.VMEM)
    return pl.pallas_call(
        post_kernel,
        out_shape=(
            jax.ShapeDtypeStruct((3, x_rows, y_rows, z_rows), jnp.float32),
            jax.ShapeDtypeStruct((x_rows, y_rows, z_rows), jnp.float32),
        ),
        in_specs=[vmem] * 3,
        out_specs=(pl.BlockSpec(memory_space=pl.ANY), pl.BlockSpec(memory_space=pl.ANY)),
        scratch_shapes=[
            pltpu.VMEM((extended + 2, y_rows + 2 * PAD, z_rows), jnp.float32),
            pltpu.VMEM((3 * extended * y_rows, z_rows), jnp.float32),
            pltpu.VMEM((3 * x_rows * (y_rows + 2 * PAD), z_rows), jnp.float32),
            pltpu.VMEM((3, x_rows, y_rows, z_rows), jnp.float32),
            pltpu.VMEM((x_rows, y_rows, z_rows), jnp.float32),
            pltpu.SemaphoreType.DMA((2,)),
            pltpu.VMEM((3 * x_rows * y_rows, z_rows), jnp.float32),
        ],
    )(drive_ext, own_ext, wz)


def shards(images, pairings):
    weights = gauss_taps(RADIUS)
    groups = lax.axis_size("img")
    own = images[0]
    x_rows, y_rows, _ = own.shape
    drive_ext, own_ext = front_stage(own, pairings, groups)
    velocity, advected = post_stage(drive_ext, own_ext)
    return (advected[None], velocity[None])


def solution(mesh):
    return jax.shard_map(
        shards,
        mesh=mesh,
        in_specs=(P("img", "space", None, None), P()),
        out_specs=(P("img", "space", None, None), P("img", None, "space", None, None)),
        check_vma=False,
    )
```

```python
import math

import jax
import numpy as np
import jax.numpy as jnp
from jax import lax
from jax.experimental import pallas as pl
from jax.experimental.pallas import tpu as pltpu
from jax.sharding import PartitionSpec as P

RADIUS = 4
PAIRINGS = 3

gauss_sigma = 1.5
step_scale = 8.0
floor_product = 0.25
floor_variance = 0.5


def gauss_taps(radius):
    raw_taps = [
        math.exp(-(offset * offset) / (2.0 * gauss_sigma * gauss_sigma))
        for offset in range(-radius, radius + 1)
    ]
    total_weight = sum(raw_taps)
    return [raw_weight / total_weight for raw_weight in raw_taps]


def halo_rows(value, width):
    peers = lax.axis_size("space")
    up = [(i, i + 1) for i in range(peers - 1)]
    down = [(i + 1, i) for i in range(peers - 1)]
    before = lax.ppermute(value[-width:], "space", up)
    after = lax.ppermute(value[:width], "space", down)
    return jnp.concatenate([before, value, after], axis=0)


def padded_along(volume, dimension, margin):
    widths = [(0, 0)] * volume.ndim
    widths[dimension] = (margin, margin)
    return jnp.pad(volume, widths)


def window(padded, dimension, offset, length):
    return lax.slice_in_dim(padded, offset, offset + length, axis=dimension)


def central(volume, dimension):
    length = volume.shape[dimension]
    padded = padded_along(volume, dimension, 1)
    return (window(padded, dimension, 2, length) - window(padded, dimension, 0, length)) * 0.5


def smooth_along(volume, dimension, weights):
    length = volume.shape[dimension]
    padded = padded_along(volume, dimension, len(weights) // 2)
    result = weights[0] * window(padded, dimension, 0, length)
    for tap_index in range(1, len(weights)):
        result = result + weights[tap_index] * window(padded, dimension, tap_index, length)
    return result


def smooth_rows(extended, weights):
    length = extended.shape[1] - len(weights) + 1
    result = weights[0] * window(extended, 1, 0, length)
    for tap_index in range(1, len(weights)):
        result = result + weights[tap_index] * window(extended, 1, tap_index, length)
    return result


def box_rows(volume):
    sx = volume[:-2] + volume[1:-1] + volume[2:]
    last = sx.shape[1] - 1
    row = lax.broadcasted_iota(jnp.int32, sx.shape, 1)
    before = jnp.where(row >= 1, pltpu.roll(sx, 1, 1), 0.0)
    after = jnp.where(row < last, pltpu.roll(sx, last, 1), 0.0)
    return (before + sx + after) * (1.0 / 9.0)


def pair_terms(g, pair_ref, stack_ref, mean_ref, spread_ref):
    own = stack_ref[g]
    mean_own = mean_ref[g]
    spread_own = spread_ref[g]
    center_own = own[1:-1] - mean_own
    inverse_spread = 1.0 / jnp.maximum(spread_own, floor_variance)
    drive_sum = None
    for pairing_row in range(PAIRINGS):
        h = pair_ref[pairing_row, g]
        partner = stack_ref[h]
        mean_partner = mean_ref[h]
        spread_partner = spread_ref[h]
        cross_term = box_rows(own * partner) - mean_own * mean_partner
        factor = 2.0 * cross_term / jnp.maximum(spread_own * spread_partner, floor_product)
        ratio_term = cross_term * inverse_spread
        pair_term = factor * (partner[1:-1] - mean_partner - ratio_term * center_own)
        drive_sum = pair_term if drive_sum is None else drive_sum + pair_term
    return drive_sum


def row_groups(first, count, rows):
    groups = []
    for r in range(first, first + count):
        owner = r // rows
        if groups and groups[-1][0] == owner:
            groups[-1][2] += 1
        else:
            groups.append([owner, r - owner * rows, 1, r - first])
    return groups


def front_kernel(
    pair_ref, own_ref, drive_ref, ext_ref, stack_ref, mean_ref, spread_ref, out_ref, zero_ref,
    send_a, recv_a, send_h, recv_h, send_b, recv_b, send_c, recv_c, local_sem, send_o, recv_o,
):
    mesh = pl.DeviceIdType.MESH
    groups, width, y_rows, z_rows = stack_ref.shape
    rows = width - 2
    x_rows = own_ref.shape[0]
    spaces = lax.axis_size("space")
    me = lax.axis_index("img")
    s = lax.axis_index("space")
    has_lo = (s + spaces - 1) // spaces
    has_hi = (2 * spaces - 2 - s) // spaces

    barrier = pltpu.get_barrier_semaphore()
    for offset in (-1, 0, 1):
        exists = {-1: s > 0, 0: s >= 0, 1: s < spaces - 1}[offset]
        for g in range(groups):
            @pl.when(exists & ((offset != 0) | (me != g)))
            def _():
                pl.semaphore_signal(barrier, inc=1, device_id=(g, (s + offset + spaces) % spaces), device_id_type=mesh)
    pl.semaphore_wait(barrier, groups * (1 + has_lo + has_hi) - 1)

    zero_ref[...] = jnp.zeros(zero_ref.shape, jnp.float32)
    margin = RADIUS + 1

    def own_halo(wait):
        copies = [
            (s < spaces - 1, own_ref.at[pl.ds(x_rows - margin, margin)], ext_ref.at[pl.ds(0, margin)],
             0, (s + 1) % spaces),
            (s > 0, own_ref.at[pl.ds(0, margin)], ext_ref.at[pl.ds(x_rows + margin, margin)],
             1, (s + spaces - 1) % spaces),
        ]
        for exists, src, dst, index, target in copies:
            @pl.when(exists)
            def _():
                copy = pltpu.make_async_remote_copy(
                    src, dst, send_o.at[index], recv_o.at[index],
                    device_id=(me, target), device_id_type=mesh,
                )
                if wait:
                    copy.wait_send()
                else:
                    copy.start()
        local = [
            (s >= 0, own_ref, ext_ref.at[pl.ds(margin, x_rows)], 2),
            (s == 0, zero_ref, ext_ref.at[pl.ds(0, margin)], 3),
            (s == spaces - 1, zero_ref, ext_ref.at[pl.ds(x_rows + margin, margin)], 4),
        ]
        for exists, src, dst, index in local:
            @pl.when(exists)
            def _():
                copy = pltpu.make_async_copy(src, dst, local_sem.at[index])
                if wait:
                    copy.wait()
                else:
                    copy.start()

    own_halo(False)

    def piece(t):
        lo = max(t * rows - 1, 0)
        hi = min(t * rows + rows + 1, x_rows)
        return own_ref.at[pl.ds(lo, hi - lo)], lo - (t * rows - 1), hi - lo

    def piece_copy(t, src_image):
        src, dst_lo, count = piece(t)
        dst = stack_ref.at[src_image, pl.ds(dst_lo, count)]
        return src, dst

    def forward_copy(t_dyn, wait):
        for kind in range(3):
            cond = {0: t_dyn == 0, 1: t_dyn == groups - 1, 2: (t_dyn > 0) & (t_dyn < groups - 1)}[kind]

            @pl.when(cond & (t_dyn != me))
            def _():
                if kind == 0:
                    src, dst_lo, count = own_ref.at[pl.ds(0, rows + 1)], 1, rows + 1
                elif kind == 1:
                    src, dst_lo, count = own_ref.at[pl.ds(x_rows - rows - 1, rows + 1)], 0, rows + 1
                else:
                    src, dst_lo, count = own_ref.at[pl.ds(t_dyn * rows - 1, rows + 2)], 0, rows + 2
                copy = pltpu.make_async_remote_copy(
                    src, stack_ref.at[me, pl.ds(dst_lo, count)], send_a.at[t_dyn], recv_a.at[me],
                    device_id=(t_dyn, s), device_id_type=mesh,
                )
                if wait:
                    copy.wait_send()
                else:
                    copy.start()

    for t in range(groups):
        src, dst = piece_copy(t, me)

        @pl.when(me == t)
        def _():
            pltpu.make_async_copy(src, dst, local_sem.at[0]).start()

    for i in range(1, groups):
        forward_copy((me + i) % groups, False)

    @pl.when(s < spaces - 1)
    def _():
        pltpu.make_async_remote_copy(
            own_ref.at[pl.ds(x_rows - 1, 1)], stack_ref.at[me, pl.ds(0, 1)],
            send_h.at[0], recv_h.at[0, me], device_id=(0, (s + 1) % spaces), device_id_type=mesh,
        ).start()

    @pl.when(s > 0)
    def _():
        pltpu.make_async_remote_copy(
            own_ref.at[pl.ds(0, 1)], stack_ref.at[me, pl.ds(width - 1, 1)],
            send_h.at[1], recv_h.at[1, me], device_id=(groups - 1, (s + spaces - 1) % spaces), device_id_type=mesh,
        ).start()

    def stats(g):
        value = stack_ref[g]
        mean = box_rows(value)
        mean_ref[g] = mean
        spread_ref[g] = box_rows(value * value) - mean * mean

    @pl.when((me == 0) & (s == 0))
    def _():
        stack_ref[:, 0] = jnp.zeros((groups, y_rows, z_rows), jnp.float32)

    @pl.when((me == groups - 1) & (s == spaces - 1))
    def _():
        stack_ref[:, width - 1] = jnp.zeros((groups, y_rows, z_rows), jnp.float32)

    def arrive(i, carry):
        g = (me + groups - i) % groups

        @pl.when(i == 0)
        def _():
            for t in range(groups):
                src, dst = piece_copy(t, me)

                @pl.when(me == t)
                def _():
                    pltpu.make_async_copy(src, dst, local_sem.at[0]).wait()

        @pl.when(i != 0)
        def _():
            for t in range(groups):
                src, dst = piece_copy(t, 0)

                @pl.when(me == t)
                def _():
                    pltpu.make_async_remote_copy(
                        src, stack_ref.at[g, pl.ds(piece(t)[1], piece(t)[2])],
                        send_a.at[0], recv_a.at[g], device_id=(g, s), device_id_type=mesh,
                    ).wait_recv()

        @pl.when((me == 0) & (s > 0))
        def _():
            pltpu.make_async_remote_copy(
                own_ref.at[pl.ds(0, 1)], stack_ref.at[g, pl.ds(0, 1)],
                send_h.at[0], recv_h.at[0, g], device_id=(0, s), device_id_type=mesh,
            ).wait_recv()

        @pl.when((me == groups - 1) & (s < spaces - 1))
        def _():
            pltpu.make_async_remote_copy(
                own_ref.at[pl.ds(0, 1)], stack_ref.at[g, pl.ds(width - 1, 1)],
                send_h.at[1], recv_h.at[1, g], device_id=(0, s), device_id_type=mesh,
            ).wait_recv()

        stats(g)
        return carry

    lax.fori_loop(0, groups, arrive, 0)

    below = row_groups(x_rows - RADIUS, RADIUS, rows)
    above = row_groups(0, RADIUS, rows)

    def main_copy(g):
        src = out_ref.at[g]
        dst = drive_ref.at[pl.ds(RADIUS + me * rows, rows)]
        return src, dst

    def halo_copies(g):
        copies = []
        for index, (owner, src_lo, count, dst_lo) in enumerate(below):
            copies.append((owner, s < spaces - 1, 1, index, out_ref.at[g, pl.ds(src_lo, count)],
                           drive_ref.at[pl.ds(dst_lo, count)]))
        for index, (owner, src_lo, count, dst_lo) in enumerate(above):
            copies.append((owner, s > 0, -1, len(below) + index, out_ref.at[g, pl.ds(src_lo, count)],
                           drive_ref.at[pl.ds(x_rows + RADIUS + dst_lo, count)]))
        return copies

    def pairs(i, carry):
        g = (me + i) % groups
        out_ref[g] = pair_terms(g, pair_ref, stack_ref, mean_ref, spread_ref)
        src, dst = main_copy(g)

        @pl.when(me == g)
        def _():
            pltpu.make_async_copy(src, dst, local_sem.at[1]).start()

        @pl.when(me != g)
        def _():
            pltpu.make_async_remote_copy(
                src, dst, send_b.at[g], recv_b.at[me], device_id=(g, s), device_id_type=mesh
            ).start()

        for owner, exists, offset, index, hsrc, hdst in halo_copies(g):
            @pl.when((me == owner) & exists)
            def _():
                pltpu.make_async_remote_copy(
                    hsrc, hdst, send_c.at[index, g], recv_c.at[index],
                    device_id=(g, (s + offset + spaces) % spaces), device_id_type=mesh,
                ).start()
        return carry

    lax.fori_loop(0, groups, pairs, 0)

    @pl.when(s == 0)
    def _():
        pltpu.make_async_copy(zero_ref.at[pl.ds(0, RADIUS)], drive_ref.at[pl.ds(0, RADIUS)], local_sem.at[5]).start()

    @pl.when(s == spaces - 1)
    def _():
        pltpu.make_async_copy(
            zero_ref.at[pl.ds(0, RADIUS)], drive_ref.at[pl.ds(x_rows + RADIUS, RADIUS)], local_sem.at[6]
        ).start()

    for i in range(1, groups):
        forward_copy((me + i) % groups, True)

    @pl.when(s < spaces - 1)
    def _():
        pltpu.make_async_remote_copy(
            own_ref.at[pl.ds(x_rows - 1, 1)], stack_ref.at[me, pl.ds(0, 1)],
            send_h.at[0], recv_h.at[0, me], device_id=(0, (s + 1) % spaces), device_id_type=mesh,
        ).wait_send()

    @pl.when(s > 0)
    def _():
        pltpu.make_async_remote_copy(
            own_ref.at[pl.ds(0, 1)], stack_ref.at[me, pl.ds(width - 1, 1)],
            send_h.at[1], recv_h.at[1, me], device_id=(groups - 1, (s + spaces - 1) % spaces), device_id_type=mesh,
        ).wait_send()

    for g in range(groups):
        src, dst = main_copy(g)

        @pl.when(me == g)
        def _():
            pltpu.make_async_copy(src, dst, local_sem.at[1]).wait()

        @pl.when(me != g)
        def _():
            pltpu.make_async_remote_copy(
                src, dst, send_b.at[g], recv_b.at[me], device_id=(g, s), device_id_type=mesh
            ).wait_send()

        for owner, exists, offset, index, hsrc, hdst in halo_copies(g):
            @pl.when((me == owner) & exists)
            def _():
                pltpu.make_async_remote_copy(
                    hsrc, hdst, send_c.at[index, g], recv_c.at[index],
                    device_id=(g, (s + offset + spaces) % spaces), device_id_type=mesh,
                ).wait_send()

    for t in range(groups):
        @pl.when(me != t)
        def _():
            pltpu.make_async_remote_copy(
                out_ref.at[0], drive_ref.at[pl.ds(RADIUS + t * rows, rows)],
                send_b.at[0], recv_b.at[t], device_id=(t, s), device_id_type=mesh,
            ).wait_recv()

    for owner, exists, offset, index, hsrc, hdst in halo_copies(0):
        @pl.when(((offset == 1) & (s > 0)) | ((offset == -1) & (s < spaces - 1)))
        def _():
            pltpu.make_async_remote_copy(
                hsrc, hdst, send_c.at[index, 0], recv_c.at[index],
                device_id=(owner, s), device_id_type=mesh,
            ).wait_recv()

    own_halo(True)
    for exists, dst, index in (
        (s > 0, ext_ref.at[pl.ds(0, margin)], 0),
        (s < spaces - 1, ext_ref.at[pl.ds(x_rows + margin, margin)], 1),
    ):
        @pl.when(exists)
        def _():
            pltpu.make_async_remote_copy(
                own_ref.at[pl.ds(0, margin)], dst, send_o.at[index], recv_o.at[index],
                device_id=(me, s), device_id_type=mesh,
            ).wait_recv()

    @pl.when(s == 0)
    def _():
        pltpu.make_async_copy(zero_ref.at[pl.ds(0, RADIUS)], drive_ref.at[pl.ds(0, RADIUS)], local_sem.at[5]).wait()

    @pl.when(s == spaces - 1)
    def _():
        pltpu.make_async_copy(
            zero_ref.at[pl.ds(0, RADIUS)], drive_ref.at[pl.ds(x_rows + RADIUS, RADIUS)], local_sem.at[6]
        ).wait()


def front_stage(own, pairings, groups):
    x_rows, y_rows, z_rows = own.shape
    rows = x_rows // groups
    shape = (groups, rows, y_rows, z_rows)
    halos = len(row_groups(x_rows - RADIUS, RADIUS, rows)) + len(row_groups(0, RADIUS, rows))
    dma = pltpu.SemaphoreType.DMA
    return pl.pallas_call(
        front_kernel,
        out_shape=(
            jax.ShapeDtypeStruct((x_rows + 2 * RADIUS, y_rows, z_rows), jnp.float32),
            jax.ShapeDtypeStruct((x_rows + 2 * RADIUS + 2, y_rows, z_rows), jnp.float32),
        ),
        in_specs=[
            pl.BlockSpec(memory_space=pltpu.SMEM),
            pl.BlockSpec(memory_space=pltpu.VMEM),
        ],
        out_specs=(pl.BlockSpec(memory_space=pl.ANY), pl.BlockSpec(memory_space=pl.ANY)),
        scratch_shapes=[
            pltpu.VMEM((groups, rows + 2, y_rows, z_rows), jnp.float32),
            pltpu.VMEM(shape, jnp.float32),
            pltpu.VMEM(shape, jnp.float32),
            pltpu.VMEM(shape, jnp.float32),
            pltpu.VMEM((RADIUS + 1, y_rows, z_rows), jnp.float32),
            dma((groups,)),
            dma((groups,)),
            dma((2,)),
            dma((2, groups)),
            dma((groups,)),
            dma((groups,)),
            dma((halos, groups)),
            dma((halos,)),
            dma((7,)),
            dma((2,)),
            dma((2,)),
        ],
        compiler_params=pltpu.CompilerParams(collective_id=0, has_side_effects=True),
    )(pairings, own)


def shifted(value, offset, axis):
    length = value.shape[axis]
    rolled = pltpu.roll(value, (-offset) % length, axis)
    index = lax.broadcasted_iota(jnp.int32, value.shape, axis) + offset
    return jnp.where((index >= 0) & (index < length), rolled, 0.0)


PAD = 8


def post_kernel(
    drive_ref, own_ref, wz_ref, vel_ref, adv_ref, own_pad, force_ref, pass_ref, vel_buf, adv_buf, sems,
    compact_ref,
):
    extended, y_rows, z_rows = drive_ref.shape
    x_rows = vel_ref.shape[1]
    padded = y_rows + 2 * PAD
    taps = gauss_taps(RADIUS)
    zeros = jnp.zeros((PAD, z_rows), jnp.float32)

    def inner(r, offset=0):
        return (r, pl.ds(PAD + offset, y_rows))

    def fill(r, carry):
        own_pad[r, pl.ds(0, PAD)] = zeros
        own_pad[r, pl.ds(PAD + y_rows, PAD)] = zeros
        own_pad[inner(r)] = own_ref[r]
        return carry

    lax.fori_loop(0, own_ref.shape[0], fill, 0)

    def plane(c, r, count):
        return pl.ds(pl.multiple_of((c * count + r) * y_rows, 8), y_rows)

    def force_row(r, carry):
        value = own_pad[inner(r + 1)]
        drive = drive_ref[r]
        force_ref[plane(0, r, extended)] = drive * ((own_pad[inner(r + 2)] - own_pad[inner(r)]) * 0.5)
        force_ref[plane(1, r, extended)] = drive * (
            (own_pad[inner(r + 1, 1)] - own_pad[inner(r + 1, -1)]) * 0.5
        )
        force_ref[plane(2, r, extended)] = drive * (
            (shifted(value, 1, 1) - shifted(value, -1, 1)) * 0.5
        )
        return carry

    lax.fori_loop(0, extended, force_row, 0)

    def slot(c, x):
        return pl.multiple_of((c * x_rows + x) * padded, 8)

    def x_pass(x, carry):
        for c in range(3):
            acc = taps[RADIUS] * force_ref[plane(c, x + RADIUS, extended)]
            for t in range(RADIUS):
                pair = force_ref[plane(c, x + t, extended)] + force_ref[plane(c, x + 2 * RADIUS - t, extended)]
                acc = acc + taps[t] * pair
            base = slot(c, x)
            pass_ref[pl.ds(base, PAD)] = zeros
            pass_ref[pl.ds(base + PAD + y_rows, PAD)] = zeros
            compact_ref[plane(c, x, x_rows)] = acc
        return carry

    lax.fori_loop(0, x_rows, x_pass, 0)
    wz = wz_ref[...]
    per_chunk = 24
    chunk = per_chunk * y_rows
    chunks = compact_ref.shape[0] // chunk

    def z_pass(i, carry):
        rows = pl.ds(pl.multiple_of(i * chunk, 8), chunk)
        result = jnp.dot(
            compact_ref[rows], wz, precision=lax.Precision.HIGH,
            preferred_element_type=jnp.float32,
        )
        for k in range(per_chunk):
            base = pl.multiple_of((i * per_chunk + k) * padded + PAD, 8)
            pass_ref[pl.ds(base, y_rows)] = result[k * y_rows:(k + 1) * y_rows]
        return carry

    lax.fori_loop(0, chunks, z_pass, 0)

    def out_row(x, carry):
        r = x + RADIUS + 1
        value = own_pad[inner(r)]
        change = None
        for c in range(3):
            base = slot(c, x) + PAD - RADIUS
            acc = taps[RADIUS] * pass_ref[pl.ds(base + RADIUS, y_rows)]
            for t in range(RADIUS):
                pair = pass_ref[pl.ds(base + t, y_rows)] + pass_ref[pl.ds(base + 2 * RADIUS - t, y_rows)]
                acc = acc + taps[t] * pair
            speed = step_scale * acc
            vel_buf[c, x] = speed
            if c == 0:
                backward = value - own_pad[inner(r - 1)]
                forward = own_pad[inner(r + 1)] - value
            elif c == 1:
                backward = value - own_pad[inner(r, -1)]
                forward = own_pad[inner(r, 1)] - value
            else:
                backward = value - shifted(value, -1, 1)
                forward = shifted(value, 1, 1) - value
            part = jnp.maximum(speed, 0.0) * backward + jnp.minimum(speed, 0.0) * forward
            change = part if change is None else change + part
        adv_buf[x] = value - change
        row = pl.ds(x, 1)
        pltpu.make_async_copy(vel_buf.at[:, row], vel_ref.at[:, row], sems.at[0]).start()
        pltpu.make_async_copy(adv_buf.at[row], adv_ref.at[row], sems.at[1]).start()
        return carry

    lax.fori_loop(0, x_rows, out_row, 0)
    pltpu.make_async_copy(vel_buf, vel_ref, sems.at[0]).wait()
    pltpu.make_async_copy(adv_buf, adv_ref, sems.at[1]).wait()


def band(length, taps):
    radius = len(taps) // 2
    matrix = np.zeros((length, length), np.float32)
    for i in range(length):
        for t in range(-radius, radius + 1):
            if 0 <= i + t < length:
                matrix[i, i + t] = taps[t + radius]
    return matrix


def post_stage(drive_ext, own_ext):
    extended, y_rows, z_rows = drive_ext.shape
    x_rows = extended - 2 * RADIUS
    taps = gauss_taps(RADIUS)
    wz = jnp.asarray(band(z_rows, taps).T)
    vmem = pl.BlockSpec(memory_space=pltpu.VMEM)
    return pl.pallas_call(
        post_kernel,
        out_shape=(
            jax.ShapeDtypeStruct((3, x_rows, y_rows, z_rows), jnp.float32),
            jax.ShapeDtypeStruct((x_rows, y_rows, z_rows), jnp.float32),
        ),
        in_specs=[vmem] * 3,
        out_specs=(pl.BlockSpec(memory_space=pl.ANY), pl.BlockSpec(memory_space=pl.ANY)),
        scratch_shapes=[
            pltpu.VMEM((extended + 2, y_rows + 2 * PAD, z_rows), jnp.float32),
            pltpu.VMEM((3 * extended * y_rows, z_rows), jnp.float32),
            pltpu.VMEM((3 * x_rows * (y_rows + 2 * PAD), z_rows), jnp.float32),
            pltpu.VMEM((3, x_rows, y_rows, z_rows), jnp.float32),
            pltpu.VMEM((x_rows, y_rows, z_rows), jnp.float32),
            pltpu.SemaphoreType.DMA((2,)),
            pltpu.VMEM((3 * x_rows * y_rows, z_rows), jnp.float32),
        ],
    )(drive_ext, own_ext, wz)


def shards(images, pairings):
    weights = gauss_taps(RADIUS)
    groups = lax.axis_size("img")
    own = images[0]
    x_rows, y_rows, _ = own.shape
    drive_ext, own_ext = front_stage(own, pairings, groups)
    velocity, advected = post_stage(drive_ext, own_ext)
    return (advected[None], velocity[None])


def solution(mesh):
    return jax.shard_map(
        shards,
        mesh=mesh,
        in_specs=(P("img", "space", None, None), P()),
        out_specs=(P("img", "space", None, None), P("img", None, "space", None, None)),
        check_vma=False,
    )
```

```python
import math

import jax
import numpy as np
import jax.numpy as jnp
from jax import lax
from jax.experimental import pallas as pl
from jax.experimental.pallas import tpu as pltpu
from jax.sharding import PartitionSpec as P

RADIUS = 4
PAIRINGS = 3

gauss_sigma = 1.5
step_scale = 8.0
floor_product = 0.25
floor_variance = 0.5


def gauss_taps(radius):
    raw_taps = [
        math.exp(-(offset * offset) / (2.0 * gauss_sigma * gauss_sigma))
        for offset in range(-radius, radius + 1)
    ]
    total_weight = sum(raw_taps)
    return [raw_weight / total_weight for raw_weight in raw_taps]


def halo_rows(value, width):
    peers = lax.axis_size("space")
    up = [(i, i + 1) for i in range(peers - 1)]
    down = [(i + 1, i) for i in range(peers - 1)]
    before = lax.ppermute(value[-width:], "space", up)
    after = lax.ppermute(value[:width], "space", down)
    return jnp.concatenate([before, value, after], axis=0)


def padded_along(volume, dimension, margin):
    widths = [(0, 0)] * volume.ndim
    widths[dimension] = (margin, margin)
    return jnp.pad(volume, widths)


def window(padded, dimension, offset, length):
    return lax.slice_in_dim(padded, offset, offset + length, axis=dimension)


def central(volume, dimension):
    length = volume.shape[dimension]
    padded = padded_along(volume, dimension, 1)
    return (window(padded, dimension, 2, length) - window(padded, dimension, 0, length)) * 0.5


def smooth_along(volume, dimension, weights):
    length = volume.shape[dimension]
    padded = padded_along(volume, dimension, len(weights) // 2)
    result = weights[0] * window(padded, dimension, 0, length)
    for tap_index in range(1, len(weights)):
        result = result + weights[tap_index] * window(padded, dimension, tap_index, length)
    return result


def smooth_rows(extended, weights):
    length = extended.shape[1] - len(weights) + 1
    result = weights[0] * window(extended, 1, 0, length)
    for tap_index in range(1, len(weights)):
        result = result + weights[tap_index] * window(extended, 1, tap_index, length)
    return result


def box_rows(volume):
    sx = volume[:-2] + volume[1:-1] + volume[2:]
    last = sx.shape[1] - 1
    row = lax.broadcasted_iota(jnp.int32, sx.shape, 1)
    before = jnp.where(row >= 1, pltpu.roll(sx, 1, 1), 0.0)
    after = jnp.where(row < last, pltpu.roll(sx, last, 1), 0.0)
    return (before + sx + after) * (1.0 / 9.0)


def pair_terms(g, pair_ref, stack_ref, mean_ref, spread_ref):
    own = stack_ref[g]
    mean_own = mean_ref[g]
    spread_own = spread_ref[g]
    center_own = own[1:-1] - mean_own
    inverse_spread = 1.0 / jnp.maximum(spread_own, floor_variance)
    drive_sum = None
    for pairing_row in range(PAIRINGS):
        h = pair_ref[pairing_row, g]
        partner = stack_ref[h]
        mean_partner = mean_ref[h]
        spread_partner = spread_ref[h]
        cross_term = box_rows(own * partner) - mean_own * mean_partner
        factor = 2.0 * cross_term / jnp.maximum(spread_own * spread_partner, floor_product)
        ratio_term = cross_term * inverse_spread
        pair_term = factor * (partner[1:-1] - mean_partner - ratio_term * center_own)
        drive_sum = pair_term if drive_sum is None else drive_sum + pair_term
    return drive_sum


def row_groups(first, count, rows):
    groups = []
    for r in range(first, first + count):
        owner = r // rows
        if groups and groups[-1][0] == owner:
            groups[-1][2] += 1
        else:
            groups.append([owner, r - owner * rows, 1, r - first])
    return groups


def front_kernel(
    pair_ref, own_ref, drive_ref, ext_ref, stack_ref, mean_ref, spread_ref, out_ref, zero_ref,
    send_a, recv_a, send_h, recv_h, send_b, recv_b, send_c, recv_c, local_sem, send_o, recv_o,
):
    mesh = pl.DeviceIdType.MESH
    groups, width, y_rows, z_rows = stack_ref.shape
    rows = width - 2
    x_rows = own_ref.shape[0]
    spaces = lax.axis_size("space")
    me = lax.axis_index("img")
    s = lax.axis_index("space")
    has_lo = (s + spaces - 1) // spaces
    has_hi = (2 * spaces - 2 - s) // spaces

    barrier = pltpu.get_barrier_semaphore()
    for offset in (-1, 0, 1):
        exists = {-1: s > 0, 0: s >= 0, 1: s < spaces - 1}[offset]
        for g in range(groups):
            @pl.when(exists & ((offset != 0) | (me != g)))
            def _():
                pl.semaphore_signal(barrier, inc=1, device_id=(g, (s + offset + spaces) % spaces), device_id_type=mesh)
    pl.semaphore_wait(barrier, groups * (1 + has_lo + has_hi) - 1)

    zero_ref[...] = jnp.zeros(zero_ref.shape, jnp.float32)
    margin = RADIUS + 1

    def own_halo(wait):
        copies = [
            (s < spaces - 1, own_ref.at[pl.ds(x_rows - margin, margin)], ext_ref.at[pl.ds(0, margin)],
             0, (s + 1) % spaces),
            (s > 0, own_ref.at[pl.ds(0, margin)], ext_ref.at[pl.ds(x_rows + margin, margin)],
             1, (s + spaces - 1) % spaces),
        ]
        for exists, src, dst, index, target in copies:
            @pl.when(exists)
            def _():
                copy = pltpu.make_async_remote_copy(
                    src, dst, send_o.at[index], recv_o.at[index],
                    device_id=(me, target), device_id_type=mesh,
                )
                if wait:
                    copy.wait_send()
                else:
                    copy.start()
        local = [
            (s >= 0, own_ref, ext_ref.at[pl.ds(margin, x_rows)], 2),
            (s == 0, zero_ref, ext_ref.at[pl.ds(0, margin)], 3),
            (s == spaces - 1, zero_ref, ext_ref.at[pl.ds(x_rows + margin, margin)], 4),
        ]
        for exists, src, dst, index in local:
            @pl.when(exists)
            def _():
                copy = pltpu.make_async_copy(src, dst, local_sem.at[index])
                if wait:
                    copy.wait()
                else:
                    copy.start()

    own_halo(False)

    def piece(t):
        lo = max(t * rows - 1, 0)
        hi = min(t * rows + rows + 1, x_rows)
        return own_ref.at[pl.ds(lo, hi - lo)], lo - (t * rows - 1), hi - lo

    def piece_copy(t, src_image):
        src, dst_lo, count = piece(t)
        dst = stack_ref.at[src_image, pl.ds(dst_lo, count)]
        return src, dst

    def forward_copy(t_dyn, wait):
        for kind in range(3):
            cond = {0: t_dyn == 0, 1: t_dyn == groups - 1, 2: (t_dyn > 0) & (t_dyn < groups - 1)}[kind]

            @pl.when(cond & (t_dyn != me))
            def _():
                if kind == 0:
                    src, dst_lo, count = own_ref.at[pl.ds(0, rows + 1)], 1, rows + 1
                elif kind == 1:
                    src, dst_lo, count = own_ref.at[pl.ds(x_rows - rows - 1, rows + 1)], 0, rows + 1
                else:
                    src, dst_lo, count = own_ref.at[pl.ds(t_dyn * rows - 1, rows + 2)], 0, rows + 2
                copy = pltpu.make_async_remote_copy(
                    src, stack_ref.at[me, pl.ds(dst_lo, count)], send_a.at[t_dyn], recv_a.at[me],
                    device_id=(t_dyn, s), device_id_type=mesh,
                )
                if wait:
                    copy.wait_send()
                else:
                    copy.start()

    for t in range(groups):
        src, dst = piece_copy(t, me)

        @pl.when(me == t)
        def _():
            pltpu.make_async_copy(src, dst, local_sem.at[0]).start()

    for i in range(1, groups):
        forward_copy((me + i) % groups, False)

    @pl.when(s < spaces - 1)
    def _():
        pltpu.make_async_remote_copy(
            own_ref.at[pl.ds(x_rows - 1, 1)], stack_ref.at[me, pl.ds(0, 1)],
            send_h.at[0], recv_h.at[0, me], device_id=(0, (s + 1) % spaces), device_id_type=mesh,
        ).start()

    @pl.when(s > 0)
    def _():
        pltpu.make_async_remote_copy(
            own_ref.at[pl.ds(0, 1)], stack_ref.at[me, pl.ds(width - 1, 1)],
            send_h.at[1], recv_h.at[1, me], device_id=(groups - 1, (s + spaces - 1) % spaces), device_id_type=mesh,
        ).start()

    def stats(g):
        value = stack_ref[g]
        mean = box_rows(value)
        mean_ref[g] = mean
        spread_ref[g] = box_rows(value * value) - mean * mean

    @pl.when((me == 0) & (s == 0))
    def _():
        stack_ref[:, 0] = jnp.zeros((groups, y_rows, z_rows), jnp.float32)

    @pl.when((me == groups - 1) & (s == spaces - 1))
    def _():
        stack_ref[:, width - 1] = jnp.zeros((groups, y_rows, z_rows), jnp.float32)

    def arrive(i, carry):
        g = (me + groups - i) % groups

        @pl.when(i == 0)
        def _():
            for t in range(groups):
                src, dst = piece_copy(t, me)

                @pl.when(me == t)
                def _():
                    pltpu.make_async_copy(src, dst, local_sem.at[0]).wait()

        @pl.when(i != 0)
        def _():
            for t in range(groups):
                src, dst = piece_copy(t, 0)

                @pl.when(me == t)
                def _():
                    pltpu.make_async_remote_copy(
                        src, stack_ref.at[g, pl.ds(piece(t)[1], piece(t)[2])],
                        send_a.at[0], recv_a.at[g], device_id=(g, s), device_id_type=mesh,
                    ).wait_recv()

        @pl.when((me == 0) & (s > 0))
        def _():
            pltpu.make_async_remote_copy(
                own_ref.at[pl.ds(0, 1)], stack_ref.at[g, pl.ds(0, 1)],
                send_h.at[0], recv_h.at[0, g], device_id=(0, s), device_id_type=mesh,
            ).wait_recv()

        @pl.when((me == groups - 1) & (s < spaces - 1))
        def _():
            pltpu.make_async_remote_copy(
                own_ref.at[pl.ds(0, 1)], stack_ref.at[g, pl.ds(width - 1, 1)],
                send_h.at[1], recv_h.at[1, g], device_id=(0, s), device_id_type=mesh,
            ).wait_recv()

        stats(g)
        return carry

    lax.fori_loop(0, groups, arrive, 0)

    below = row_groups(x_rows - RADIUS, RADIUS, rows)
    above = row_groups(0, RADIUS, rows)

    def main_copy(g):
        src = out_ref.at[g]
        dst = drive_ref.at[pl.ds(RADIUS + me * rows, rows)]
        return src, dst

    def halo_copies(g):
        copies = []
        for index, (owner, src_lo, count, dst_lo) in enumerate(below):
            copies.append((owner, s < spaces - 1, 1, index, out_ref.at[g, pl.ds(src_lo, count)],
                           drive_ref.at[pl.ds(dst_lo, count)]))
        for index, (owner, src_lo, count, dst_lo) in enumerate(above):
            copies.append((owner, s > 0, -1, len(below) + index, out_ref.at[g, pl.ds(src_lo, count)],
                           drive_ref.at[pl.ds(x_rows + RADIUS + dst_lo, count)]))
        return copies

    def pairs(i, carry):
        g = (me + i) % groups
        out_ref[g] = pair_terms(g, pair_ref, stack_ref, mean_ref, spread_ref)
        src, dst = main_copy(g)

        @pl.when(me == g)
        def _():
            pltpu.make_async_copy(src, dst, local_sem.at[1]).start()

        @pl.when(me != g)
        def _():
            pltpu.make_async_remote_copy(
                src, dst, send_b.at[g], recv_b.at[me], device_id=(g, s), device_id_type=mesh
            ).start()

        for owner, exists, offset, index, hsrc, hdst in halo_copies(g):
            @pl.when((me == owner) & exists)
            def _():
                pltpu.make_async_remote_copy(
                    hsrc, hdst, send_c.at[index, g], recv_c.at[index],
                    device_id=(g, (s + offset + spaces) % spaces), device_id_type=mesh,
                ).start()
        return carry

    lax.fori_loop(0, groups, pairs, 0)

    @pl.when(s == 0)
    def _():
        pltpu.make_async_copy(zero_ref.at[pl.ds(0, RADIUS)], drive_ref.at[pl.ds(0, RADIUS)], local_sem.at[5]).start()

    @pl.when(s == spaces - 1)
    def _():
        pltpu.make_async_copy(
            zero_ref.at[pl.ds(0, RADIUS)], drive_ref.at[pl.ds(x_rows + RADIUS, RADIUS)], local_sem.at[6]
        ).start()

    for i in range(1, groups):
        forward_copy((me + i) % groups, True)

    @pl.when(s < spaces - 1)
    def _():
        pltpu.make_async_remote_copy(
            own_ref.at[pl.ds(x_rows - 1, 1)], stack_ref.at[me, pl.ds(0, 1)],
            send_h.at[0], recv_h.at[0, me], device_id=(0, (s + 1) % spaces), device_id_type=mesh,
        ).wait_send()

    @pl.when(s > 0)
    def _():
        pltpu.make_async_remote_copy(
            own_ref.at[pl.ds(0, 1)], stack_ref.at[me, pl.ds(width - 1, 1)],
            send_h.at[1], recv_h.at[1, me], device_id=(groups - 1, (s + spaces - 1) % spaces), device_id_type=mesh,
        ).wait_send()

    for g in range(groups):
        src, dst = main_copy(g)

        @pl.when(me == g)
        def _():
            pltpu.make_async_copy(src, dst, local_sem.at[1]).wait()

        @pl.when(me != g)
        def _():
            pltpu.make_async_remote_copy(
                src, dst, send_b.at[g], recv_b.at[me], device_id=(g, s), device_id_type=mesh
            ).wait_send()

        for owner, exists, offset, index, hsrc, hdst in halo_copies(g):
            @pl.when((me == owner) & exists)
            def _():
                pltpu.make_async_remote_copy(
                    hsrc, hdst, send_c.at[index, g], recv_c.at[index],
                    device_id=(g, (s + offset + spaces) % spaces), device_id_type=mesh,
                ).wait_send()

    for t in range(groups):
        @pl.when(me != t)
        def _():
            pltpu.make_async_remote_copy(
                out_ref.at[0], drive_ref.at[pl.ds(RADIUS + t * rows, rows)],
                send_b.at[0], recv_b.at[t], device_id=(t, s), device_id_type=mesh,
            ).wait_recv()

    for owner, exists, offset, index, hsrc, hdst in halo_copies(0):
        @pl.when(((offset == 1) & (s > 0)) | ((offset == -1) & (s < spaces - 1)))
        def _():
            pltpu.make_async_remote_copy(
                hsrc, hdst, send_c.at[index, 0], recv_c.at[index],
                device_id=(owner, s), device_id_type=mesh,
            ).wait_recv()

    own_halo(True)
    for exists, dst, index in (
        (s > 0, ext_ref.at[pl.ds(0, margin)], 0),
        (s < spaces - 1, ext_ref.at[pl.ds(x_rows + margin, margin)], 1),
    ):
        @pl.when(exists)
        def _():
            pltpu.make_async_remote_copy(
                own_ref.at[pl.ds(0, margin)], dst, send_o.at[index], recv_o.at[index],
                device_id=(me, s), device_id_type=mesh,
            ).wait_recv()

    @pl.when(s == 0)
    def _():
        pltpu.make_async_copy(zero_ref.at[pl.ds(0, RADIUS)], drive_ref.at[pl.ds(0, RADIUS)], local_sem.at[5]).wait()

    @pl.when(s == spaces - 1)
    def _():
        pltpu.make_async_copy(
            zero_ref.at[pl.ds(0, RADIUS)], drive_ref.at[pl.ds(x_rows + RADIUS, RADIUS)], local_sem.at[6]
        ).wait()


def front_stage(own, pairings, groups):
    x_rows, y_rows, z_rows = own.shape
    rows = x_rows // groups
    shape = (groups, rows, y_rows, z_rows)
    halos = len(row_groups(x_rows - RADIUS, RADIUS, rows)) + len(row_groups(0, RADIUS, rows))
    dma = pltpu.SemaphoreType.DMA
    return pl.pallas_call(
        front_kernel,
        out_shape=(
            jax.ShapeDtypeStruct((x_rows + 2 * RADIUS, y_rows, z_rows), jnp.float32),
            jax.ShapeDtypeStruct((x_rows + 2 * RADIUS + 2, y_rows, z_rows), jnp.float32),
        ),
        in_specs=[
            pl.BlockSpec(memory_space=pltpu.SMEM),
            pl.BlockSpec(memory_space=pltpu.VMEM),
        ],
        out_specs=(pl.BlockSpec(memory_space=pl.ANY), pl.BlockSpec(memory_space=pl.ANY)),
        scratch_shapes=[
            pltpu.VMEM((groups, rows + 2, y_rows, z_rows), jnp.float32),
            pltpu.VMEM(shape, jnp.float32),
            pltpu.VMEM(shape, jnp.float32),
            pltpu.VMEM(shape, jnp.float32),
            pltpu.VMEM((RADIUS + 1, y_rows, z_rows), jnp.float32),
            dma((groups,)),
            dma((groups,)),
            dma((2,)),
            dma((2, groups)),
            dma((groups,)),
            dma((groups,)),
            dma((halos, groups)),
            dma((halos,)),
            dma((7,)),
            dma((2,)),
            dma((2,)),
        ],
        compiler_params=pltpu.CompilerParams(collective_id=0, has_side_effects=True),
    )(pairings, own)


def shifted(value, offset, axis):
    length = value.shape[axis]
    rolled = pltpu.roll(value, (-offset) % length, axis)
    index = lax.broadcasted_iota(jnp.int32, value.shape, axis) + offset
    return jnp.where((index >= 0) & (index < length), rolled, 0.0)


PAD = 8


def post_kernel(
    drive_ref, own_ref, wz_ref, vel_ref, adv_ref, own_pad, force_ref, pass_ref, vel_buf, adv_buf, sems,
    compact_ref,
):
    extended, y_rows, z_rows = drive_ref.shape
    x_rows = vel_ref.shape[1]
    padded = y_rows + 2 * PAD
    taps = gauss_taps(RADIUS)
    zeros = jnp.zeros((PAD, z_rows), jnp.float32)

    def inner(r, offset=0):
        return (r, pl.ds(PAD + offset, y_rows))

    def fill(r, carry):
        own_pad[r, pl.ds(0, PAD)] = zeros
        own_pad[r, pl.ds(PAD + y_rows, PAD)] = zeros
        own_pad[inner(r)] = own_ref[r]
        return carry

    lax.fori_loop(0, own_ref.shape[0], fill, 0)

    def plane(c, r, count):
        return pl.ds(pl.multiple_of((c * count + r) * y_rows, 8), y_rows)

    def force_row(r, carry):
        value = own_pad[inner(r + 1)]
        drive = drive_ref[r]
        force_ref[plane(0, r, extended)] = drive * ((own_pad[inner(r + 2)] - own_pad[inner(r)]) * 0.5)
        force_ref[plane(1, r, extended)] = drive * (
            (own_pad[inner(r + 1, 1)] - own_pad[inner(r + 1, -1)]) * 0.5
        )
        force_ref[plane(2, r, extended)] = drive * (
            (shifted(value, 1, 1) - shifted(value, -1, 1)) * 0.5
        )
        return carry

    lax.fori_loop(0, extended, force_row, 0)

    def slot(c, x):
        return pl.multiple_of((c * x_rows + x) * padded, 8)

    def x_pass(x, carry):
        for c in range(3):
            acc = taps[RADIUS] * force_ref[plane(c, x + RADIUS, extended)]
            for t in range(RADIUS):
                pair = force_ref[plane(c, x + t, extended)] + force_ref[plane(c, x + 2 * RADIUS - t, extended)]
                acc = acc + taps[t] * pair
            base = slot(c, x)
            pass_ref[pl.ds(base, PAD)] = zeros
            pass_ref[pl.ds(base + PAD + y_rows, PAD)] = zeros
            compact_ref[plane(c, x, x_rows)] = acc
        return carry

    lax.fori_loop(0, x_rows, x_pass, 0)
    wz = wz_ref[...]
    per_chunk = 72
    chunk = per_chunk * y_rows
    chunks = compact_ref.shape[0] // chunk

    def z_pass(i, carry):
        rows = pl.ds(pl.multiple_of(i * chunk, 8), chunk)
        result = jnp.dot(
            compact_ref[rows], wz, precision=lax.Precision.HIGH,
            preferred_element_type=jnp.float32,
        )
        for k in range(per_chunk):
            base = pl.multiple_of((i * per_chunk + k) * padded + PAD, 8)
            pass_ref[pl.ds(base, y_rows)] = result[k * y_rows:(k + 1) * y_rows]
        return carry

    lax.fori_loop(0, chunks, z_pass, 0)

    def out_row(x, carry):
        r = x + RADIUS + 1
        value = own_pad[inner(r)]
        change = None
        for c in range(3):
            base = slot(c, x) + PAD - RADIUS
            acc = taps[RADIUS] * pass_ref[pl.ds(base + RADIUS, y_rows)]
            for t in range(RADIUS):
                pair = pass_ref[pl.ds(base + t, y_rows)] + pass_ref[pl.ds(base + 2 * RADIUS - t, y_rows)]
                acc = acc + taps[t] * pair
            speed = step_scale * acc
            vel_buf[c, x] = speed
            if c == 0:
                backward = value - own_pad[inner(r - 1)]
                forward = own_pad[inner(r + 1)] - value
            elif c == 1:
                backward = value - own_pad[inner(r, -1)]
                forward = own_pad[inner(r, 1)] - value
            else:
                backward = value - shifted(value, -1, 1)
                forward = shifted(value, 1, 1) - value
            part = jnp.maximum(speed, 0.0) * backward + jnp.minimum(speed, 0.0) * forward
            change = part if change is None else change + part
        adv_buf[x] = value - change
        row = pl.ds(x, 1)
        pltpu.make_async_copy(vel_buf.at[:, row], vel_ref.at[:, row], sems.at[0]).start()
        pltpu.make_async_copy(adv_buf.at[row], adv_ref.at[row], sems.at[1]).start()
        return carry

    lax.fori_loop(0, x_rows, out_row, 0)
    pltpu.make_async_copy(vel_buf, vel_ref, sems.at[0]).wait()
    pltpu.make_async_copy(adv_buf, adv_ref, sems.at[1]).wait()


def band(length, taps):
    radius = len(taps) // 2
    matrix = np.zeros((length, length), np.float32)
    for i in range(length):
        for t in range(-radius, radius + 1):
            if 0 <= i + t < length:
                matrix[i, i + t] = taps[t + radius]
    return matrix


def post_stage(drive_ext, own_ext):
    extended, y_rows, z_rows = drive_ext.shape
    x_rows = extended - 2 * RADIUS
    taps = gauss_taps(RADIUS)
    wz = jnp.asarray(band(z_rows, taps).T)
    vmem = pl.BlockSpec(memory_space=pltpu.VMEM)
    return pl.pallas_call(
        post_kernel,
        out_shape=(
            jax.ShapeDtypeStruct((3, x_rows, y_rows, z_rows), jnp.float32),
            jax.ShapeDtypeStruct((x_rows, y_rows, z_rows), jnp.float32),
        ),
        in_specs=[vmem] * 3,
        out_specs=(pl.BlockSpec(memory_space=pl.ANY), pl.BlockSpec(memory_space=pl.ANY)),
        scratch_shapes=[
            pltpu.VMEM((extended + 2, y_rows + 2 * PAD, z_rows), jnp.float32),
            pltpu.VMEM((3 * extended * y_rows, z_rows), jnp.float32),
            pltpu.VMEM((3 * x_rows * (y_rows + 2 * PAD), z_rows), jnp.float32),
            pltpu.VMEM((3, x_rows, y_rows, z_rows), jnp.float32),
            pltpu.VMEM((x_rows, y_rows, z_rows), jnp.float32),
            pltpu.SemaphoreType.DMA((2,)),
            pltpu.VMEM((3 * x_rows * y_rows, z_rows), jnp.float32),
        ],
    )(drive_ext, own_ext, wz)


def shards(images, pairings):
    weights = gauss_taps(RADIUS)
    groups = lax.axis_size("img")
    own = images[0]
    x_rows, y_rows, _ = own.shape
    drive_ext, own_ext = front_stage(own, pairings, groups)
    velocity, advected = post_stage(drive_ext, own_ext)
    return (advected[None], velocity[None])


def solution(mesh):
    return jax.shard_map(
        shards,
        mesh=mesh,
        in_specs=(P("img", "space", None, None), P()),
        out_specs=(P("img", "space", None, None), P("img", None, "space", None, None)),
        check_vma=False,
    )
```

```python
import math

import jax
import numpy as np
import jax.numpy as jnp
from jax import lax
from jax.experimental import pallas as pl
from jax.experimental.pallas import tpu as pltpu
from jax.sharding import PartitionSpec as P

RADIUS = 4
PAIRINGS = 3

gauss_sigma = 1.5
step_scale = 8.0
floor_product = 0.25
floor_variance = 0.5


def gauss_taps(radius):
    raw_taps = [
        math.exp(-(offset * offset) / (2.0 * gauss_sigma * gauss_sigma))
        for offset in range(-radius, radius + 1)
    ]
    total_weight = sum(raw_taps)
    return [raw_weight / total_weight for raw_weight in raw_taps]


def halo_rows(value, width):
    peers = lax.axis_size("space")
    up = [(i, i + 1) for i in range(peers - 1)]
    down = [(i + 1, i) for i in range(peers - 1)]
    before = lax.ppermute(value[-width:], "space", up)
    after = lax.ppermute(value[:width], "space", down)
    return jnp.concatenate([before, value, after], axis=0)


def padded_along(volume, dimension, margin):
    widths = [(0, 0)] * volume.ndim
    widths[dimension] = (margin, margin)
    return jnp.pad(volume, widths)


def window(padded, dimension, offset, length):
    return lax.slice_in_dim(padded, offset, offset + length, axis=dimension)


def central(volume, dimension):
    length = volume.shape[dimension]
    padded = padded_along(volume, dimension, 1)
    return (window(padded, dimension, 2, length) - window(padded, dimension, 0, length)) * 0.5


def smooth_along(volume, dimension, weights):
    length = volume.shape[dimension]
    padded = padded_along(volume, dimension, len(weights) // 2)
    result = weights[0] * window(padded, dimension, 0, length)
    for tap_index in range(1, len(weights)):
        result = result + weights[tap_index] * window(padded, dimension, tap_index, length)
    return result


def smooth_rows(extended, weights):
    length = extended.shape[1] - len(weights) + 1
    result = weights[0] * window(extended, 1, 0, length)
    for tap_index in range(1, len(weights)):
        result = result + weights[tap_index] * window(extended, 1, tap_index, length)
    return result


def box_rows(volume):
    sx = volume[:-2] + volume[1:-1] + volume[2:]
    last = sx.shape[1] - 1
    row = lax.broadcasted_iota(jnp.int32, sx.shape, 1)
    before = jnp.where(row >= 1, pltpu.roll(sx, 1, 1), 0.0)
    after = jnp.where(row < last, pltpu.roll(sx, last, 1), 0.0)
    return (before + sx + after) * (1.0 / 9.0)


def pair_terms(g, pair_ref, stack_ref, mean_ref, spread_ref):
    own = stack_ref[g]
    mean_own = mean_ref[g]
    spread_own = spread_ref[g]
    center_own = own[1:-1] - mean_own
    inverse_spread = 1.0 / jnp.maximum(spread_own, floor_variance)
    drive_sum = None
    for pairing_row in range(PAIRINGS):
        h = pair_ref[pairing_row, g]
        partner = stack_ref[h]
        mean_partner = mean_ref[h]
        spread_partner = spread_ref[h]
        cross_term = box_rows(own * partner) - mean_own * mean_partner
        factor = 2.0 * cross_term / jnp.maximum(spread_own * spread_partner, floor_product)
        ratio_term = cross_term * inverse_spread
        pair_term = factor * (partner[1:-1] - mean_partner - ratio_term * center_own)
        drive_sum = pair_term if drive_sum is None else drive_sum + pair_term
    return drive_sum


def row_groups(first, count, rows):
    groups = []
    for r in range(first, first + count):
        owner = r // rows
        if groups and groups[-1][0] == owner:
            groups[-1][2] += 1
        else:
            groups.append([owner, r - owner * rows, 1, r - first])
    return groups


def front_kernel(
    pair_ref, own_ref, drive_ref, ext_ref, stack_ref, mean_ref, spread_ref, out_ref, zero_ref,
    send_a, recv_a, send_h, recv_h, send_b, recv_b, send_c, recv_c, local_sem, send_o, recv_o,
):
    mesh = pl.DeviceIdType.MESH
    groups, width, y_rows, z_rows = stack_ref.shape
    rows = width - 2
    x_rows = own_ref.shape[0]
    spaces = lax.axis_size("space")
    me = lax.axis_index("img")
    s = lax.axis_index("space")
    has_lo = (s + spaces - 1) // spaces
    has_hi = (2 * spaces - 2 - s) // spaces

    barrier = pltpu.get_barrier_semaphore()
    for offset in (-1, 0, 1):
        exists = {-1: s > 0, 0: s >= 0, 1: s < spaces - 1}[offset]
        for g in range(groups):
            @pl.when(exists & ((offset != 0) | (me != g)))
            def _():
                pl.semaphore_signal(barrier, inc=1, device_id=(g, (s + offset + spaces) % spaces), device_id_type=mesh)
    pl.semaphore_wait(barrier, groups * (1 + has_lo + has_hi) - 1)

    zero_ref[...] = jnp.zeros(zero_ref.shape, jnp.float32)
    margin = RADIUS + 1

    def own_halo(wait):
        copies = [
            (s < spaces - 1, own_ref.at[pl.ds(x_rows - margin, margin)], ext_ref.at[pl.ds(0, margin)],
             0, (s + 1) % spaces),
            (s > 0, own_ref.at[pl.ds(0, margin)], ext_ref.at[pl.ds(x_rows + margin, margin)],
             1, (s + spaces - 1) % spaces),
        ]
        for exists, src, dst, index, target in copies:
            @pl.when(exists)
            def _():
                copy = pltpu.make_async_remote_copy(
                    src, dst, send_o.at[index], recv_o.at[index],
                    device_id=(me, target), device_id_type=mesh,
                )
                if wait:
                    copy.wait_send()
                else:
                    copy.start()
        local = [
            (s >= 0, own_ref, ext_ref.at[pl.ds(margin, x_rows)], 2),
            (s == 0, zero_ref, ext_ref.at[pl.ds(0, margin)], 3),
            (s == spaces - 1, zero_ref, ext_ref.at[pl.ds(x_rows + margin, margin)], 4),
        ]
        for exists, src, dst, index in local:
            @pl.when(exists)
            def _():
                copy = pltpu.make_async_copy(src, dst, local_sem.at[index])
                if wait:
                    copy.wait()
                else:
                    copy.start()

    own_halo(False)

    def piece(t):
        lo = max(t * rows - 1, 0)
        hi = min(t * rows + rows + 1, x_rows)
        return own_ref.at[pl.ds(lo, hi - lo)], lo - (t * rows - 1), hi - lo

    def piece_copy(t, src_image):
        src, dst_lo, count = piece(t)
        dst = stack_ref.at[src_image, pl.ds(dst_lo, count)]
        return src, dst

    def forward_copy(t_dyn, wait):
        for kind in range(3):
            cond = {0: t_dyn == 0, 1: t_dyn == groups - 1, 2: (t_dyn > 0) & (t_dyn < groups - 1)}[kind]

            @pl.when(cond & (t_dyn != me))
            def _():
                if kind == 0:
                    src, dst_lo, count = own_ref.at[pl.ds(0, rows + 1)], 1, rows + 1
                elif kind == 1:
                    src, dst_lo, count = own_ref.at[pl.ds(x_rows - rows - 1, rows + 1)], 0, rows + 1
                else:
                    src, dst_lo, count = own_ref.at[pl.ds(t_dyn * rows - 1, rows + 2)], 0, rows + 2
                copy = pltpu.make_async_remote_copy(
                    src, stack_ref.at[me, pl.ds(dst_lo, count)], send_a.at[t_dyn], recv_a.at[me],
                    device_id=(t_dyn, s), device_id_type=mesh,
                )
                if wait:
                    copy.wait_send()
                else:
                    copy.start()

    for t in range(groups):
        src, dst = piece_copy(t, me)

        @pl.when(me == t)
        def _():
            pltpu.make_async_copy(src, dst, local_sem.at[0]).start()

    for i in range(1, groups):
        forward_copy((me + i) % groups, False)

    @pl.when(s < spaces - 1)
    def _():
        pltpu.make_async_remote_copy(
            own_ref.at[pl.ds(x_rows - 1, 1)], stack_ref.at[me, pl.ds(0, 1)],
            send_h.at[0], recv_h.at[0, me], device_id=(0, (s + 1) % spaces), device_id_type=mesh,
        ).start()

    @pl.when(s > 0)
    def _():
        pltpu.make_async_remote_copy(
            own_ref.at[pl.ds(0, 1)], stack_ref.at[me, pl.ds(width - 1, 1)],
            send_h.at[1], recv_h.at[1, me], device_id=(groups - 1, (s + spaces - 1) % spaces), device_id_type=mesh,
        ).start()

    def stats(g):
        value = stack_ref[g]
        mean = box_rows(value)
        mean_ref[g] = mean
        spread_ref[g] = box_rows(value * value) - mean * mean

    @pl.when((me == 0) & (s == 0))
    def _():
        stack_ref[:, 0] = jnp.zeros((groups, y_rows, z_rows), jnp.float32)

    @pl.when((me == groups - 1) & (s == spaces - 1))
    def _():
        stack_ref[:, width - 1] = jnp.zeros((groups, y_rows, z_rows), jnp.float32)

    def arrive(i, carry):
        g = (me + groups - i) % groups

        @pl.when(i == 0)
        def _():
            for t in range(groups):
                src, dst = piece_copy(t, me)

                @pl.when(me == t)
                def _():
                    pltpu.make_async_copy(src, dst, local_sem.at[0]).wait()

        @pl.when(i != 0)
        def _():
            for t in range(groups):
                src, dst = piece_copy(t, 0)

                @pl.when(me == t)
                def _():
                    pltpu.make_async_remote_copy(
                        src, stack_ref.at[g, pl.ds(piece(t)[1], piece(t)[2])],
                        send_a.at[0], recv_a.at[g], device_id=(g, s), device_id_type=mesh,
                    ).wait_recv()

        @pl.when((me == 0) & (s > 0))
        def _():
            pltpu.make_async_remote_copy(
                own_ref.at[pl.ds(0, 1)], stack_ref.at[g, pl.ds(0, 1)],
                send_h.at[0], recv_h.at[0, g], device_id=(0, s), device_id_type=mesh,
            ).wait_recv()

        @pl.when((me == groups - 1) & (s < spaces - 1))
        def _():
            pltpu.make_async_remote_copy(
                own_ref.at[pl.ds(0, 1)], stack_ref.at[g, pl.ds(width - 1, 1)],
                send_h.at[1], recv_h.at[1, g], device_id=(0, s), device_id_type=mesh,
            ).wait_recv()

        stats(g)
        return carry

    lax.fori_loop(0, groups, arrive, 0)

    below = row_groups(x_rows - RADIUS, RADIUS, rows)
    above = row_groups(0, RADIUS, rows)

    def main_copy(g):
        src = out_ref.at[g]
        dst = drive_ref.at[pl.ds(RADIUS + me * rows, rows)]
        return src, dst

    def halo_copies(g):
        copies = []
        for index, (owner, src_lo, count, dst_lo) in enumerate(below):
            copies.append((owner, s < spaces - 1, 1, index, out_ref.at[g, pl.ds(src_lo, count)],
                           drive_ref.at[pl.ds(dst_lo, count)]))
        for index, (owner, src_lo, count, dst_lo) in enumerate(above):
            copies.append((owner, s > 0, -1, len(below) + index, out_ref.at[g, pl.ds(src_lo, count)],
                           drive_ref.at[pl.ds(x_rows + RADIUS + dst_lo, count)]))
        return copies

    def pairs(i, carry):
        g = (me + i) % groups
        out_ref[g] = pair_terms(g, pair_ref, stack_ref, mean_ref, spread_ref)
        src, dst = main_copy(g)

        @pl.when(me == g)
        def _():
            pltpu.make_async_copy(src, dst, local_sem.at[1]).start()

        @pl.when(me != g)
        def _():
            pltpu.make_async_remote_copy(
                src, dst, send_b.at[g], recv_b.at[me], device_id=(g, s), device_id_type=mesh
            ).start()

        for owner, exists, offset, index, hsrc, hdst in halo_copies(g):
            @pl.when((me == owner) & exists)
            def _():
                pltpu.make_async_remote_copy(
                    hsrc, hdst, send_c.at[index, g], recv_c.at[index],
                    device_id=(g, (s + offset + spaces) % spaces), device_id_type=mesh,
                ).start()
        return carry

    lax.fori_loop(0, groups, pairs, 0)

    @pl.when(s == 0)
    def _():
        pltpu.make_async_copy(zero_ref.at[pl.ds(0, RADIUS)], drive_ref.at[pl.ds(0, RADIUS)], local_sem.at[5]).start()

    @pl.when(s == spaces - 1)
    def _():
        pltpu.make_async_copy(
            zero_ref.at[pl.ds(0, RADIUS)], drive_ref.at[pl.ds(x_rows + RADIUS, RADIUS)], local_sem.at[6]
        ).start()

    for i in range(1, groups):
        forward_copy((me + i) % groups, True)

    @pl.when(s < spaces - 1)
    def _():
        pltpu.make_async_remote_copy(
            own_ref.at[pl.ds(x_rows - 1, 1)], stack_ref.at[me, pl.ds(0, 1)],
            send_h.at[0], recv_h.at[0, me], device_id=(0, (s + 1) % spaces), device_id_type=mesh,
        ).wait_send()

    @pl.when(s > 0)
    def _():
        pltpu.make_async_remote_copy(
            own_ref.at[pl.ds(0, 1)], stack_ref.at[me, pl.ds(width - 1, 1)],
            send_h.at[1], recv_h.at[1, me], device_id=(groups - 1, (s + spaces - 1) % spaces), device_id_type=mesh,
        ).wait_send()

    for g in range(groups):
        src, dst = main_copy(g)

        @pl.when(me == g)
        def _():
            pltpu.make_async_copy(src, dst, local_sem.at[1]).wait()

        @pl.when(me != g)
        def _():
            pltpu.make_async_remote_copy(
                src, dst, send_b.at[g], recv_b.at[me], device_id=(g, s), device_id_type=mesh
            ).wait_send()

        for owner, exists, offset, index, hsrc, hdst in halo_copies(g):
            @pl.when((me == owner) & exists)
            def _():
                pltpu.make_async_remote_copy(
                    hsrc, hdst, send_c.at[index, g], recv_c.at[index],
                    device_id=(g, (s + offset + spaces) % spaces), device_id_type=mesh,
                ).wait_send()

    for t in range(groups):
        @pl.when(me != t)
        def _():
            pltpu.make_async_remote_copy(
                out_ref.at[0], drive_ref.at[pl.ds(RADIUS + t * rows, rows)],
                send_b.at[0], recv_b.at[t], device_id=(t, s), device_id_type=mesh,
            ).wait_recv()

    for owner, exists, offset, index, hsrc, hdst in halo_copies(0):
        @pl.when(((offset == 1) & (s > 0)) | ((offset == -1) & (s < spaces - 1)))
        def _():
            pltpu.make_async_remote_copy(
                hsrc, hdst, send_c.at[index, 0], recv_c.at[index],
                device_id=(owner, s), device_id_type=mesh,
            ).wait_recv()

    own_halo(True)
    for exists, dst, index in (
        (s > 0, ext_ref.at[pl.ds(0, margin)], 0),
        (s < spaces - 1, ext_ref.at[pl.ds(x_rows + margin, margin)], 1),
    ):
        @pl.when(exists)
        def _():
            pltpu.make_async_remote_copy(
                own_ref.at[pl.ds(0, margin)], dst, send_o.at[index], recv_o.at[index],
                device_id=(me, s), device_id_type=mesh,
            ).wait_recv()

    @pl.when(s == 0)
    def _():
        pltpu.make_async_copy(zero_ref.at[pl.ds(0, RADIUS)], drive_ref.at[pl.ds(0, RADIUS)], local_sem.at[5]).wait()

    @pl.when(s == spaces - 1)
    def _():
        pltpu.make_async_copy(
            zero_ref.at[pl.ds(0, RADIUS)], drive_ref.at[pl.ds(x_rows + RADIUS, RADIUS)], local_sem.at[6]
        ).wait()


def front_stage(own, pairings, groups):
    x_rows, y_rows, z_rows = own.shape
    rows = x_rows // groups
    shape = (groups, rows, y_rows, z_rows)
    halos = len(row_groups(x_rows - RADIUS, RADIUS, rows)) + len(row_groups(0, RADIUS, rows))
    dma = pltpu.SemaphoreType.DMA
    return pl.pallas_call(
        front_kernel,
        out_shape=(
            jax.ShapeDtypeStruct((x_rows + 2 * RADIUS, y_rows, z_rows), jnp.float32),
            jax.ShapeDtypeStruct((x_rows + 2 * RADIUS + 2, y_rows, z_rows), jnp.float32),
        ),
        in_specs=[
            pl.BlockSpec(memory_space=pltpu.SMEM),
            pl.BlockSpec(memory_space=pltpu.VMEM),
        ],
        out_specs=(pl.BlockSpec(memory_space=pl.ANY), pl.BlockSpec(memory_space=pl.ANY)),
        scratch_shapes=[
            pltpu.VMEM((groups, rows + 2, y_rows, z_rows), jnp.float32),
            pltpu.VMEM(shape, jnp.float32),
            pltpu.VMEM(shape, jnp.float32),
            pltpu.VMEM(shape, jnp.float32),
            pltpu.VMEM((RADIUS + 1, y_rows, z_rows), jnp.float32),
            dma((groups,)),
            dma((groups,)),
            dma((2,)),
            dma((2, groups)),
            dma((groups,)),
            dma((groups,)),
            dma((halos, groups)),
            dma((halos,)),
            dma((7,)),
            dma((2,)),
            dma((2,)),
        ],
        compiler_params=pltpu.CompilerParams(collective_id=0, has_side_effects=True),
    )(pairings, own)


def shifted(value, offset, axis):
    length = value.shape[axis]
    rolled = pltpu.roll(value, (-offset) % length, axis)
    index = lax.broadcasted_iota(jnp.int32, value.shape, axis) + offset
    return jnp.where((index >= 0) & (index < length), rolled, 0.0)


PAD = 8


def post_kernel(
    drive_ref, own_ref, wz_ref, vel_ref, adv_ref, own_pad, force_ref, pass_ref, vel_buf, adv_buf, sems,
    compact_ref,
):
    extended, y_rows, z_rows = drive_ref.shape
    x_rows = vel_ref.shape[1]
    padded = y_rows + 2 * PAD
    taps = gauss_taps(RADIUS)
    zeros = jnp.zeros((PAD, z_rows), jnp.float32)

    def inner(r, offset=0):
        return (r, pl.ds(PAD + offset, y_rows))

    def fill(r, carry):
        own_pad[r, pl.ds(0, PAD)] = zeros
        own_pad[r, pl.ds(PAD + y_rows, PAD)] = zeros
        own_pad[inner(r)] = own_ref[r]
        return carry

    lax.fori_loop(0, own_ref.shape[0], fill, 0)

    def plane(c, r, count):
        return pl.ds(pl.multiple_of((c * count + r) * y_rows, 8), y_rows)

    def force_row(r, carry):
        value = own_pad[inner(r + 1)]
        drive = drive_ref[r]
        force_ref[plane(0, r, extended)] = drive * ((own_pad[inner(r + 2)] - own_pad[inner(r)]) * 0.5)
        force_ref[plane(1, r, extended)] = drive * (
            (own_pad[inner(r + 1, 1)] - own_pad[inner(r + 1, -1)]) * 0.5
        )
        force_ref[plane(2, r, extended)] = drive * (
            (shifted(value, 1, 1) - shifted(value, -1, 1)) * 0.5
        )
        return carry

    lax.fori_loop(0, extended, force_row, 0)

    def slot(c, x):
        return pl.multiple_of((c * x_rows + x) * padded, 8)

    def x_pass(x, carry):
        for c in range(3):
            acc = taps[RADIUS] * force_ref[plane(c, x + RADIUS, extended)]
            for t in range(RADIUS):
                pair = force_ref[plane(c, x + t, extended)] + force_ref[plane(c, x + 2 * RADIUS - t, extended)]
                acc = acc + taps[t] * pair
            base = slot(c, x)
            pass_ref[pl.ds(base, PAD)] = zeros
            pass_ref[pl.ds(base + PAD + y_rows, PAD)] = zeros
            compact_ref[plane(c, x, x_rows)] = acc
        return carry

    lax.fori_loop(0, x_rows, x_pass, 0, unroll=2)
    wz = wz_ref[...]
    per_chunk = 72
    chunk = per_chunk * y_rows
    chunks = compact_ref.shape[0] // chunk

    def z_pass(i, carry):
        rows = pl.ds(pl.multiple_of(i * chunk, 8), chunk)
        result = jnp.dot(
            compact_ref[rows], wz, precision=lax.Precision.HIGH,
            preferred_element_type=jnp.float32,
        )
        for k in range(per_chunk):
            base = pl.multiple_of((i * per_chunk + k) * padded + PAD, 8)
            pass_ref[pl.ds(base, y_rows)] = result[k * y_rows:(k + 1) * y_rows]
        return carry

    lax.fori_loop(0, chunks, z_pass, 0)

    def out_row(x, carry):
        r = x + RADIUS + 1
        value = own_pad[inner(r)]
        change = None
        for c in range(3):
            base = slot(c, x) + PAD - RADIUS
            acc = taps[RADIUS] * pass_ref[pl.ds(base + RADIUS, y_rows)]
            for t in range(RADIUS):
                pair = pass_ref[pl.ds(base + t, y_rows)] + pass_ref[pl.ds(base + 2 * RADIUS - t, y_rows)]
                acc = acc + taps[t] * pair
            speed = step_scale * acc
            vel_buf[c, x] = speed
            if c == 0:
                backward = value - own_pad[inner(r - 1)]
                forward = own_pad[inner(r + 1)] - value
            elif c == 1:
                backward = value - own_pad[inner(r, -1)]
                forward = own_pad[inner(r, 1)] - value
            else:
                backward = value - shifted(value, -1, 1)
                forward = shifted(value, 1, 1) - value
            part = jnp.maximum(speed, 0.0) * backward + jnp.minimum(speed, 0.0) * forward
            change = part if change is None else change + part
        adv_buf[x] = value - change
        row = pl.ds(x, 1)
        pltpu.make_async_copy(vel_buf.at[:, row], vel_ref.at[:, row], sems.at[0]).start()
        pltpu.make_async_copy(adv_buf.at[row], adv_ref.at[row], sems.at[1]).start()
        return carry

    lax.fori_loop(0, x_rows, out_row, 0, unroll=2)
    pltpu.make_async_copy(vel_buf, vel_ref, sems.at[0]).wait()
    pltpu.make_async_copy(adv_buf, adv_ref, sems.at[1]).wait()


def band(length, taps):
    radius = len(taps) // 2
    matrix = np.zeros((length, length), np.float32)
    for i in range(length):
        for t in range(-radius, radius + 1):
            if 0 <= i + t < length:
                matrix[i, i + t] = taps[t + radius]
    return matrix


def post_stage(drive_ext, own_ext):
    extended, y_rows, z_rows = drive_ext.shape
    x_rows = extended - 2 * RADIUS
    taps = gauss_taps(RADIUS)
    wz = jnp.asarray(band(z_rows, taps).T)
    vmem = pl.BlockSpec(memory_space=pltpu.VMEM)
    return pl.pallas_call(
        post_kernel,
        out_shape=(
            jax.ShapeDtypeStruct((3, x_rows, y_rows, z_rows), jnp.float32),
            jax.ShapeDtypeStruct((x_rows, y_rows, z_rows), jnp.float32),
        ),
        in_specs=[vmem] * 3,
        out_specs=(pl.BlockSpec(memory_space=pl.ANY), pl.BlockSpec(memory_space=pl.ANY)),
        scratch_shapes=[
            pltpu.VMEM((extended + 2, y_rows + 2 * PAD, z_rows), jnp.float32),
            pltpu.VMEM((3 * extended * y_rows, z_rows), jnp.float32),
            pltpu.VMEM((3 * x_rows * (y_rows + 2 * PAD), z_rows), jnp.float32),
            pltpu.VMEM((3, x_rows, y_rows, z_rows), jnp.float32),
            pltpu.VMEM((x_rows, y_rows, z_rows), jnp.float32),
            pltpu.SemaphoreType.DMA((2,)),
            pltpu.VMEM((3 * x_rows * y_rows, z_rows), jnp.float32),
        ],
    )(drive_ext, own_ext, wz)


def shards(images, pairings):
    weights = gauss_taps(RADIUS)
    groups = lax.axis_size("img")
    own = images[0]
    x_rows, y_rows, _ = own.shape
    drive_ext, own_ext = front_stage(own, pairings, groups)
    velocity, advected = post_stage(drive_ext, own_ext)
    return (advected[None], velocity[None])


def solution(mesh):
    return jax.shard_map(
        shards,
        mesh=mesh,
        in_specs=(P("img", "space", None, None), P()),
        out_specs=(P("img", "space", None, None), P("img", None, "space", None, None)),
        check_vma=False,
    )
```

```python
import math

import jax
import numpy as np
import jax.numpy as jnp
from jax import lax
from jax.experimental import pallas as pl
from jax.experimental.pallas import tpu as pltpu
from jax.sharding import PartitionSpec as P

RADIUS = 4
PAIRINGS = 3

gauss_sigma = 1.5
step_scale = 8.0
floor_product = 0.25
floor_variance = 0.5


def gauss_taps(radius):
    raw_taps = [
        math.exp(-(offset * offset) / (2.0 * gauss_sigma * gauss_sigma))
        for offset in range(-radius, radius + 1)
    ]
    total_weight = sum(raw_taps)
    return [raw_weight / total_weight for raw_weight in raw_taps]


def halo_rows(value, width):
    peers = lax.axis_size("space")
    up = [(i, i + 1) for i in range(peers - 1)]
    down = [(i + 1, i) for i in range(peers - 1)]
    before = lax.ppermute(value[-width:], "space", up)
    after = lax.ppermute(value[:width], "space", down)
    return jnp.concatenate([before, value, after], axis=0)


def padded_along(volume, dimension, margin):
    widths = [(0, 0)] * volume.ndim
    widths[dimension] = (margin, margin)
    return jnp.pad(volume, widths)


def window(padded, dimension, offset, length):
    return lax.slice_in_dim(padded, offset, offset + length, axis=dimension)


def central(volume, dimension):
    length = volume.shape[dimension]
    padded = padded_along(volume, dimension, 1)
    return (window(padded, dimension, 2, length) - window(padded, dimension, 0, length)) * 0.5


def smooth_along(volume, dimension, weights):
    length = volume.shape[dimension]
    padded = padded_along(volume, dimension, len(weights) // 2)
    result = weights[0] * window(padded, dimension, 0, length)
    for tap_index in range(1, len(weights)):
        result = result + weights[tap_index] * window(padded, dimension, tap_index, length)
    return result


def smooth_rows(extended, weights):
    length = extended.shape[1] - len(weights) + 1
    result = weights[0] * window(extended, 1, 0, length)
    for tap_index in range(1, len(weights)):
        result = result + weights[tap_index] * window(extended, 1, tap_index, length)
    return result


def box_rows(volume):
    sx = volume[:-2] + volume[1:-1] + volume[2:]
    last = sx.shape[1] - 1
    row = lax.broadcasted_iota(jnp.int32, sx.shape, 1)
    before = jnp.where(row >= 1, pltpu.roll(sx, 1, 1), 0.0)
    after = jnp.where(row < last, pltpu.roll(sx, last, 1), 0.0)
    return (before + sx + after) * (1.0 / 9.0)


def pair_terms(g, pair_ref, stack_ref, mean_ref, spread_ref):
    own = stack_ref[g]
    mean_own = mean_ref[g]
    spread_own = spread_ref[g]
    center_own = own[1:-1] - mean_own
    inverse_spread = 1.0 / jnp.maximum(spread_own, floor_variance)
    drive_sum = None
    for pairing_row in range(PAIRINGS):
        h = pair_ref[pairing_row, g]
        partner = stack_ref[h]
        mean_partner = mean_ref[h]
        spread_partner = spread_ref[h]
        cross_term = box_rows(own * partner) - mean_own * mean_partner
        factor = 2.0 * cross_term / jnp.maximum(spread_own * spread_partner, floor_product)
        ratio_term = cross_term * inverse_spread
        pair_term = factor * (partner[1:-1] - mean_partner - ratio_term * center_own)
        drive_sum = pair_term if drive_sum is None else drive_sum + pair_term
    return drive_sum


def row_groups(first, count, rows):
    groups = []
    for r in range(first, first + count):
        owner = r // rows
        if groups and groups[-1][0] == owner:
            groups[-1][2] += 1
        else:
            groups.append([owner, r - owner * rows, 1, r - first])
    return groups


def front_kernel(
    pair_ref, own_ref, drive_ref, ext_ref, stack_ref, mean_ref, spread_ref, out_ref, zero_ref,
    send_a, recv_a, send_h, recv_h, send_b, recv_b, send_c, recv_c, local_sem, send_o, recv_o,
):
    mesh = pl.DeviceIdType.MESH
    groups, width, y_rows, z_rows = stack_ref.shape
    rows = width - 2
    x_rows = own_ref.shape[0]
    spaces = lax.axis_size("space")
    me = lax.axis_index("img")
    s = lax.axis_index("space")
    has_lo = (s + spaces - 1) // spaces
    has_hi = (2 * spaces - 2 - s) // spaces

    barrier = pltpu.get_barrier_semaphore()
    for offset in (-1, 0, 1):
        exists = {-1: s > 0, 0: s >= 0, 1: s < spaces - 1}[offset]
        for g in range(groups):
            @pl.when(exists & ((offset != 0) | (me != g)))
            def _():
                pl.semaphore_signal(barrier, inc=1, device_id=(g, (s + offset + spaces) % spaces), device_id_type=mesh)
    pl.semaphore_wait(barrier, groups * (1 + has_lo + has_hi) - 1)

    zero_ref[...] = jnp.zeros(zero_ref.shape, jnp.float32)
    margin = RADIUS + 1

    def own_halo(wait):
        copies = [
            (s < spaces - 1, own_ref.at[pl.ds(x_rows - margin, margin)], ext_ref.at[pl.ds(0, margin)],
             0, (s + 1) % spaces),
            (s > 0, own_ref.at[pl.ds(0, margin)], ext_ref.at[pl.ds(x_rows + margin, margin)],
             1, (s + spaces - 1) % spaces),
        ]
        for exists, src, dst, index, target in copies:
            @pl.when(exists)
            def _():
                copy = pltpu.make_async_remote_copy(
                    src, dst, send_o.at[index], recv_o.at[index],
                    device_id=(me, target), device_id_type=mesh,
                )
                if wait:
                    copy.wait_send()
                else:
                    copy.start()
        local = [
            (s >= 0, own_ref, ext_ref.at[pl.ds(margin, x_rows)], 2),
            (s == 0, zero_ref, ext_ref.at[pl.ds(0, margin)], 3),
            (s == spaces - 1, zero_ref, ext_ref.at[pl.ds(x_rows + margin, margin)], 4),
        ]
        for exists, src, dst, index in local:
            @pl.when(exists)
            def _():
                copy = pltpu.make_async_copy(src, dst, local_sem.at[index])
                if wait:
                    copy.wait()
                else:
                    copy.start()

    own_halo(False)

    def piece(t):
        lo = max(t * rows - 1, 0)
        hi = min(t * rows + rows + 1, x_rows)
        return own_ref.at[pl.ds(lo, hi - lo)], lo - (t * rows - 1), hi - lo

    def piece_copy(t, src_image):
        src, dst_lo, count = piece(t)
        dst = stack_ref.at[src_image, pl.ds(dst_lo, count)]
        return src, dst

    def forward_copy(t_dyn, wait):
        for kind in range(3):
            cond = {0: t_dyn == 0, 1: t_dyn == groups - 1, 2: (t_dyn > 0) & (t_dyn < groups - 1)}[kind]

            @pl.when(cond & (t_dyn != me))
            def _():
                if kind == 0:
                    src, dst_lo, count = own_ref.at[pl.ds(0, rows + 1)], 1, rows + 1
                elif kind == 1:
                    src, dst_lo, count = own_ref.at[pl.ds(x_rows - rows - 1, rows + 1)], 0, rows + 1
                else:
                    src, dst_lo, count = own_ref.at[pl.ds(t_dyn * rows - 1, rows + 2)], 0, rows + 2
                copy = pltpu.make_async_remote_copy(
                    src, stack_ref.at[me, pl.ds(dst_lo, count)], send_a.at[t_dyn], recv_a.at[me],
                    device_id=(t_dyn, s), device_id_type=mesh,
                )
                if wait:
                    copy.wait_send()
                else:
                    copy.start()

    for t in range(groups):
        src, dst = piece_copy(t, me)

        @pl.when(me == t)
        def _():
            pltpu.make_async_copy(src, dst, local_sem.at[0]).start()

    for i in range(1, groups):
        forward_copy((me + i) % groups, False)

    @pl.when(s < spaces - 1)
    def _():
        pltpu.make_async_remote_copy(
            own_ref.at[pl.ds(x_rows - 1, 1)], stack_ref.at[me, pl.ds(0, 1)],
            send_h.at[0], recv_h.at[0, me], device_id=(0, (s + 1) % spaces), device_id_type=mesh,
        ).start()

    @pl.when(s > 0)
    def _():
        pltpu.make_async_remote_copy(
            own_ref.at[pl.ds(0, 1)], stack_ref.at[me, pl.ds(width - 1, 1)],
            send_h.at[1], recv_h.at[1, me], device_id=(groups - 1, (s + spaces - 1) % spaces), device_id_type=mesh,
        ).start()

    def stats(g):
        value = stack_ref[g]
        mean = box_rows(value)
        mean_ref[g] = mean
        spread_ref[g] = box_rows(value * value) - mean * mean

    @pl.when((me == 0) & (s == 0))
    def _():
        stack_ref[:, 0] = jnp.zeros((groups, y_rows, z_rows), jnp.float32)

    @pl.when((me == groups - 1) & (s == spaces - 1))
    def _():
        stack_ref[:, width - 1] = jnp.zeros((groups, y_rows, z_rows), jnp.float32)

    def arrive(i, carry):
        g = (me + groups - i) % groups

        @pl.when(i == 0)
        def _():
            for t in range(groups):
                src, dst = piece_copy(t, me)

                @pl.when(me == t)
                def _():
                    pltpu.make_async_copy(src, dst, local_sem.at[0]).wait()

        @pl.when(i != 0)
        def _():
            for t in range(groups):
                src, dst = piece_copy(t, 0)

                @pl.when(me == t)
                def _():
                    pltpu.make_async_remote_copy(
                        src, stack_ref.at[g, pl.ds(piece(t)[1], piece(t)[2])],
                        send_a.at[0], recv_a.at[g], device_id=(g, s), device_id_type=mesh,
                    ).wait_recv()

        @pl.when((me == 0) & (s > 0))
        def _():
            pltpu.make_async_remote_copy(
                own_ref.at[pl.ds(0, 1)], stack_ref.at[g, pl.ds(0, 1)],
                send_h.at[0], recv_h.at[0, g], device_id=(0, s), device_id_type=mesh,
            ).wait_recv()

        @pl.when((me == groups - 1) & (s < spaces - 1))
        def _():
            pltpu.make_async_remote_copy(
                own_ref.at[pl.ds(0, 1)], stack_ref.at[g, pl.ds(width - 1, 1)],
                send_h.at[1], recv_h.at[1, g], device_id=(0, s), device_id_type=mesh,
            ).wait_recv()

        stats(g)
        return carry

    lax.fori_loop(0, groups, arrive, 0)

    below = row_groups(x_rows - RADIUS, RADIUS, rows)
    above = row_groups(0, RADIUS, rows)

    def main_copy(g):
        src = out_ref.at[g]
        dst = drive_ref.at[pl.ds(RADIUS + me * rows, rows)]
        return src, dst

    def halo_copies(g):
        copies = []
        for index, (owner, src_lo, count, dst_lo) in enumerate(below):
            copies.append((owner, s < spaces - 1, 1, index, out_ref.at[g, pl.ds(src_lo, count)],
                           drive_ref.at[pl.ds(dst_lo, count)]))
        for index, (owner, src_lo, count, dst_lo) in enumerate(above):
            copies.append((owner, s > 0, -1, len(below) + index, out_ref.at[g, pl.ds(src_lo, count)],
                           drive_ref.at[pl.ds(x_rows + RADIUS + dst_lo, count)]))
        return copies

    def pairs(i, carry):
        g = (me + i) % groups
        out_ref[g] = pair_terms(g, pair_ref, stack_ref, mean_ref, spread_ref)
        src, dst = main_copy(g)

        @pl.when(me == g)
        def _():
            pltpu.make_async_copy(src, dst, local_sem.at[1]).start()

        @pl.when(me != g)
        def _():
            pltpu.make_async_remote_copy(
                src, dst, send_b.at[g], recv_b.at[me], device_id=(g, s), device_id_type=mesh
            ).start()

        for owner, exists, offset, index, hsrc, hdst in halo_copies(g):
            @pl.when((me == owner) & exists)
            def _():
                pltpu.make_async_remote_copy(
                    hsrc, hdst, send_c.at[index, g], recv_c.at[index],
                    device_id=(g, (s + offset + spaces) % spaces), device_id_type=mesh,
                ).start()
        return carry

    lax.fori_loop(0, groups, pairs, 0)

    @pl.when(s == 0)
    def _():
        pltpu.make_async_copy(zero_ref.at[pl.ds(0, RADIUS)], drive_ref.at[pl.ds(0, RADIUS)], local_sem.at[5]).start()

    @pl.when(s == spaces - 1)
    def _():
        pltpu.make_async_copy(
            zero_ref.at[pl.ds(0, RADIUS)], drive_ref.at[pl.ds(x_rows + RADIUS, RADIUS)], local_sem.at[6]
        ).start()

    for i in range(1, groups):
        forward_copy((me + i) % groups, True)

    @pl.when(s < spaces - 1)
    def _():
        pltpu.make_async_remote_copy(
            own_ref.at[pl.ds(x_rows - 1, 1)], stack_ref.at[me, pl.ds(0, 1)],
            send_h.at[0], recv_h.at[0, me], device_id=(0, (s + 1) % spaces), device_id_type=mesh,
        ).wait_send()

    @pl.when(s > 0)
    def _():
        pltpu.make_async_remote_copy(
            own_ref.at[pl.ds(0, 1)], stack_ref.at[me, pl.ds(width - 1, 1)],
            send_h.at[1], recv_h.at[1, me], device_id=(groups - 1, (s + spaces - 1) % spaces), device_id_type=mesh,
        ).wait_send()

    for g in range(groups):
        src, dst = main_copy(g)

        @pl.when(me == g)
        def _():
            pltpu.make_async_copy(src, dst, local_sem.at[1]).wait()

        @pl.when(me != g)
        def _():
            pltpu.make_async_remote_copy(
                src, dst, send_b.at[g], recv_b.at[me], device_id=(g, s), device_id_type=mesh
            ).wait_send()

        for owner, exists, offset, index, hsrc, hdst in halo_copies(g):
            @pl.when((me == owner) & exists)
            def _():
                pltpu.make_async_remote_copy(
                    hsrc, hdst, send_c.at[index, g], recv_c.at[index],
                    device_id=(g, (s + offset + spaces) % spaces), device_id_type=mesh,
                ).wait_send()

    for t in range(groups):
        @pl.when(me != t)
        def _():
            pltpu.make_async_remote_copy(
                out_ref.at[0], drive_ref.at[pl.ds(RADIUS + t * rows, rows)],
                send_b.at[0], recv_b.at[t], device_id=(t, s), device_id_type=mesh,
            ).wait_recv()

    for owner, exists, offset, index, hsrc, hdst in halo_copies(0):
        @pl.when(((offset == 1) & (s > 0)) | ((offset == -1) & (s < spaces - 1)))
        def _():
            pltpu.make_async_remote_copy(
                hsrc, hdst, send_c.at[index, 0], recv_c.at[index],
                device_id=(owner, s), device_id_type=mesh,
            ).wait_recv()

    own_halo(True)
    for exists, dst, index in (
        (s > 0, ext_ref.at[pl.ds(0, margin)], 0),
        (s < spaces - 1, ext_ref.at[pl.ds(x_rows + margin, margin)], 1),
    ):
        @pl.when(exists)
        def _():
            pltpu.make_async_remote_copy(
                own_ref.at[pl.ds(0, margin)], dst, send_o.at[index], recv_o.at[index],
                device_id=(me, s), device_id_type=mesh,
            ).wait_recv()

    @pl.when(s == 0)
    def _():
        pltpu.make_async_copy(zero_ref.at[pl.ds(0, RADIUS)], drive_ref.at[pl.ds(0, RADIUS)], local_sem.at[5]).wait()

    @pl.when(s == spaces - 1)
    def _():
        pltpu.make_async_copy(
            zero_ref.at[pl.ds(0, RADIUS)], drive_ref.at[pl.ds(x_rows + RADIUS, RADIUS)], local_sem.at[6]
        ).wait()


def front_stage(own, pairings, groups):
    x_rows, y_rows, z_rows = own.shape
    rows = x_rows // groups
    shape = (groups, rows, y_rows, z_rows)
    halos = len(row_groups(x_rows - RADIUS, RADIUS, rows)) + len(row_groups(0, RADIUS, rows))
    dma = pltpu.SemaphoreType.DMA
    return pl.pallas_call(
        front_kernel,
        out_shape=(
            jax.ShapeDtypeStruct((x_rows + 2 * RADIUS, y_rows, z_rows), jnp.float32),
            jax.ShapeDtypeStruct((x_rows + 2 * RADIUS + 2, y_rows, z_rows), jnp.float32),
        ),
        in_specs=[
            pl.BlockSpec(memory_space=pltpu.SMEM),
            pl.BlockSpec(memory_space=pltpu.VMEM),
        ],
        out_specs=(pl.BlockSpec(memory_space=pl.ANY), pl.BlockSpec(memory_space=pl.ANY)),
        scratch_shapes=[
            pltpu.VMEM((groups, rows + 2, y_rows, z_rows), jnp.float32),
            pltpu.VMEM(shape, jnp.float32),
            pltpu.VMEM(shape, jnp.float32),
            pltpu.VMEM(shape, jnp.float32),
            pltpu.VMEM((RADIUS + 1, y_rows, z_rows), jnp.float32),
            dma((groups,)),
            dma((groups,)),
            dma((2,)),
            dma((2, groups)),
            dma((groups,)),
            dma((groups,)),
            dma((halos, groups)),
            dma((halos,)),
            dma((7,)),
            dma((2,)),
            dma((2,)),
        ],
        compiler_params=pltpu.CompilerParams(collective_id=0, has_side_effects=True),
    )(pairings, own)


def shifted(value, offset, axis):
    length = value.shape[axis]
    rolled = pltpu.roll(value, (-offset) % length, axis)
    index = lax.broadcasted_iota(jnp.int32, value.shape, axis) + offset
    return jnp.where((index >= 0) & (index < length), rolled, 0.0)


PAD = 8


def post_kernel(
    drive_ref, own_ref, wz_ref, vel_ref, adv_ref, own_pad, force_ref, pass_ref, vel_buf, adv_buf, sems,
    compact_ref,
):
    extended, y_rows, z_rows = drive_ref.shape
    x_rows = vel_ref.shape[1]
    padded = y_rows + 2 * PAD
    taps = gauss_taps(RADIUS)
    zeros = jnp.zeros((PAD, z_rows), jnp.float32)

    def inner(r, offset=0):
        return (r, pl.ds(PAD + offset, y_rows))

    def fill(r, carry):
        own_pad[r, pl.ds(0, PAD)] = zeros
        own_pad[r, pl.ds(PAD + y_rows, PAD)] = zeros
        own_pad[inner(r)] = own_ref[r]
        return carry

    lax.fori_loop(0, own_ref.shape[0], fill, 0)

    def plane(c, r, count):
        return pl.ds(pl.multiple_of((c * count + r) * y_rows, 8), y_rows)

    def force_row(r, carry):
        value = own_pad[inner(r + 1)]
        drive = drive_ref[r]
        force_ref[plane(0, r, extended)] = drive * ((own_pad[inner(r + 2)] - own_pad[inner(r)]) * 0.5)
        force_ref[plane(1, r, extended)] = drive * (
            (own_pad[inner(r + 1, 1)] - own_pad[inner(r + 1, -1)]) * 0.5
        )
        force_ref[plane(2, r, extended)] = drive * (
            (shifted(value, 1, 1) - shifted(value, -1, 1)) * 0.5
        )
        return carry

    lax.fori_loop(0, extended, force_row, 0, unroll=2)

    def slot(c, x):
        return pl.multiple_of((c * x_rows + x) * padded, 8)

    def x_pass(x, carry):
        for c in range(3):
            acc = taps[RADIUS] * force_ref[plane(c, x + RADIUS, extended)]
            for t in range(RADIUS):
                pair = force_ref[plane(c, x + t, extended)] + force_ref[plane(c, x + 2 * RADIUS - t, extended)]
                acc = acc + taps[t] * pair
            base = slot(c, x)
            pass_ref[pl.ds(base, PAD)] = zeros
            pass_ref[pl.ds(base + PAD + y_rows, PAD)] = zeros
            compact_ref[plane(c, x, x_rows)] = acc
        return carry

    lax.fori_loop(0, x_rows, x_pass, 0, unroll=2)
    wz = wz_ref[...]
    per_chunk = 72
    chunk = per_chunk * y_rows
    chunks = compact_ref.shape[0] // chunk

    def z_pass(i, carry):
        rows = pl.ds(pl.multiple_of(i * chunk, 8), chunk)
        result = jnp.dot(
            compact_ref[rows], wz, precision=lax.Precision.HIGH,
            preferred_element_type=jnp.float32,
        )
        for k in range(per_chunk):
            base = pl.multiple_of((i * per_chunk + k) * padded + PAD, 8)
            pass_ref[pl.ds(base, y_rows)] = result[k * y_rows:(k + 1) * y_rows]
        return carry

    lax.fori_loop(0, chunks, z_pass, 0)

    def out_row(x, carry):
        r = x + RADIUS + 1
        value = own_pad[inner(r)]
        change = None
        for c in range(3):
            base = slot(c, x) + PAD - RADIUS
            acc = taps[RADIUS] * pass_ref[pl.ds(base + RADIUS, y_rows)]
            for t in range(RADIUS):
                pair = pass_ref[pl.ds(base + t, y_rows)] + pass_ref[pl.ds(base + 2 * RADIUS - t, y_rows)]
                acc = acc + taps[t] * pair
            speed = step_scale * acc
            vel_buf[c, x] = speed
            if c == 0:
                backward = value - own_pad[inner(r - 1)]
                forward = own_pad[inner(r + 1)] - value
            elif c == 1:
                backward = value - own_pad[inner(r, -1)]
                forward = own_pad[inner(r, 1)] - value
            else:
                backward = value - shifted(value, -1, 1)
                forward = shifted(value, 1, 1) - value
            part = jnp.maximum(speed, 0.0) * backward + jnp.minimum(speed, 0.0) * forward
            change = part if change is None else change + part
        adv_buf[x] = value - change
        row = pl.ds(x, 1)
        pltpu.make_async_copy(vel_buf.at[:, row], vel_ref.at[:, row], sems.at[0]).start()
        pltpu.make_async_copy(adv_buf.at[row], adv_ref.at[row], sems.at[1]).start()
        return carry

    lax.fori_loop(0, x_rows, out_row, 0, unroll=2)
    pltpu.make_async_copy(vel_buf, vel_ref, sems.at[0]).wait()
    pltpu.make_async_copy(adv_buf, adv_ref, sems.at[1]).wait()


def band(length, taps):
    radius = len(taps) // 2
    matrix = np.zeros((length, length), np.float32)
    for i in range(length):
        for t in range(-radius, radius + 1):
            if 0 <= i + t < length:
                matrix[i, i + t] = taps[t + radius]
    return matrix


def post_stage(drive_ext, own_ext):
    extended, y_rows, z_rows = drive_ext.shape
    x_rows = extended - 2 * RADIUS
    taps = gauss_taps(RADIUS)
    wz = jnp.asarray(band(z_rows, taps).T)
    vmem = pl.BlockSpec(memory_space=pltpu.VMEM)
    return pl.pallas_call(
        post_kernel,
        out_shape=(
            jax.ShapeDtypeStruct((3, x_rows, y_rows, z_rows), jnp.float32),
            jax.ShapeDtypeStruct((x_rows, y_rows, z_rows), jnp.float32),
        ),
        in_specs=[vmem] * 3,
        out_specs=(pl.BlockSpec(memory_space=pl.ANY), pl.BlockSpec(memory_space=pl.ANY)),
        scratch_shapes=[
            pltpu.VMEM((extended + 2, y_rows + 2 * PAD, z_rows), jnp.float32),
            pltpu.VMEM((3 * extended * y_rows, z_rows), jnp.float32),
            pltpu.VMEM((3 * x_rows * (y_rows + 2 * PAD), z_rows), jnp.float32),
            pltpu.VMEM((3, x_rows, y_rows, z_rows), jnp.float32),
            pltpu.VMEM((x_rows, y_rows, z_rows), jnp.float32),
            pltpu.SemaphoreType.DMA((2,)),
            pltpu.VMEM((3 * x_rows * y_rows, z_rows), jnp.float32),
        ],
    )(drive_ext, own_ext, wz)


def shards(images, pairings):
    weights = gauss_taps(RADIUS)
    groups = lax.axis_size("img")
    own = images[0]
    x_rows, y_rows, _ = own.shape
    drive_ext, own_ext = front_stage(own, pairings, groups)
    velocity, advected = post_stage(drive_ext, own_ext)
    return (advected[None], velocity[None])


def solution(mesh):
    return jax.shard_map(
        shards,
        mesh=mesh,
        in_specs=(P("img", "space", None, None), P()),
        out_specs=(P("img", "space", None, None), P("img", None, "space", None, None)),
        check_vma=False,
    )
```
